128 devices in a mesh: gx: 8 (over y, core), gy: 16 (over x, z).
Axes of the slice: x: 4, y: 4, z: 4, core: 2. Of those that a mesh axis runs over, the one named last changes fastest.
Arguments:
- estimate: bfloat16 [64, 128, 32, 128], P('gx', 'gy'), may hold values from -16 to 16
- dual: bfloat16 [64, 128, 32, 128], P('gx', 'gy'), may hold values from -4 to 4
- corners: int32 [3, 8192], P(None, ('gx', 'gy')), may hold values from 0 to 120, as said below
- members: int32 [2048, 16], replicated, may hold values from -1 to 8191, as said below
- thresholds: float32 [2048], replicated, may hold values from 3000 to 60000
Outputs:
- lowrank: float32 [64, 128, 32, 128], P('gx', 'gy')
- dual_next: float32 [64, 128, 32, 128], P('gx', 'gy')
The draws below stay inside these ranges and needn't reach their ends.
Inputs may be any that keep to these rules, and one draw needn't show every extreme that they name: `corners`: patch p covers 8 cells from its corner along each dimension and lies inside the volume. Column p belongs to the device at position p // 64 in the mesh's order (gx slowest); such a patch starts at least 4 cells before that device's block and at most 4 cells before the block's end, along each of the first two dimensions. Every patch number appears in exactly one place of members. The root of group g is the device at position g // 16 in the mesh's order (gx slowest); at most 2 of one device's patches lie in groups of one root, and exactly 2 do for some device and root in every draw; some group lists 16 patches in every draw.
All inputs are finite; a program needn't handle non-finite values.
Results may differ from the reference program's by a relative error of at most 0.0093.
Values may be sent and summed in bfloat16 or wider, within the bound.
No kernel may reach another device: no remote copies, remote signals or barrier semaphores. Data moves between devices by JAX's collectives and lax.ppermute only.
A program may use at most 128 MiB of HBM per device.

```python
import math
import jax
import jax.numpy as jnp
from jax import lax

CX = 8
CY = 8
NZ = 32
COMP = 128
PATCH = 8
MEMBERS = 16
PATCH_DEV = 64
NX = 64
NY = 128
SLOTS = 256
CAP = 2
GRP_DEV = 16
GROUPS = 2048
NPATCH = 8192


def draw_estimate(key, part):
    scale_key = jax.random.fold_in(key, 11)
    mixing_key = jax.random.fold_in(key, 12)
    noise_key = jax.random.fold_in(key, 13)
    amplitude_key = jax.random.fold_in(key, 14)
    scales = jnp.exp(jax.random.uniform(scale_key, (COMP,), jnp.float32, jnp.log(0.3), jnp.log(3.0)))
    mixing = jnp.diag(scales) + 0.15 * jax.random.normal(mixing_key, (COMP, COMP), jnp.float32)
    cell_total = NX * NY * NZ
    noise = jax.random.normal(noise_key, (cell_total, COMP), jnp.float32)
    amplitude = jnp.exp(jax.random.uniform(amplitude_key, (cell_total, 1), jnp.float32, jnp.log(0.5), jnp.log(2.0)))
    values = amplitude * jnp.dot(noise, mixing)
    values = jnp.clip(values, -16.0, 16.0)
    return values.reshape(NX, NY, NZ, COMP).astype(jnp.bfloat16)


def draw_corners(key, part):
    blocks_y = NY // CY
    margin = PATCH // 2
    owner = jnp.arange(NPATCH, dtype=jnp.int32) // PATCH_DEV
    block_x = owner // blocks_y
    block_y = owner % blocks_y
    low_x = jnp.maximum(block_x * CX - margin, 0)
    high_x = jnp.minimum((block_x + 1) * CX - margin, NX - PATCH)
    low_y = jnp.maximum(block_y * CY - margin, 0)
    high_y = jnp.minimum((block_y + 1) * CY - margin, NY - PATCH)
    first_x = jax.random.randint(jax.random.fold_in(key, 21), (NPATCH,), low_x, high_x + 1)
    first_y = jax.random.randint(jax.random.fold_in(key, 22), (NPATCH,), low_y, high_y + 1)
    first_z = jax.random.randint(jax.random.fold_in(key, 23), (NPATCH,), 0, NZ - PATCH + 1)
    return jnp.stack([first_x, first_y, first_z]).astype(jnp.int32)


def draw_members(key, part):
    device_list = NPATCH // PATCH_DEV
    rank_key = jax.random.fold_in(key, 31)
    noise_key = jax.random.fold_in(key, 32)
    shuffle_key = jax.random.fold_in(key, 33)
    matrix_rank = jax.random.permutation(rank_key, device_list).astype(jnp.int32)
    preferred_choice = max(device_list // 8, 1)
    extra_credit = jnp.where(matrix_rank < preferred_choice, 1 << 20, (device_list - matrix_rank) * 1024 // device_list)
    random_perturbation = jax.random.randint(noise_key, (device_list, device_list), 0, 1024)
    rating_value = (extra_credit[None, :] + random_perturbation) * device_list + jnp.arange(device_list, dtype=jnp.int32)[None, :]
    preference = lax.top_k(rating_value, device_list)[1].astype(jnp.int32)
    position = jnp.arange(PATCH_DEV, dtype=jnp.int32)
    target = preference[:, position // CAP]
    lane_index = position % CAP
    patch_number = jnp.arange(device_list, dtype=jnp.int32)[:, None] * PATCH_DEV + position[None, :]
    inbox = jnp.arange(device_list, dtype=jnp.int32)[:, None] * CAP + lane_index[None, :]
    incoming = jnp.full((device_list, SLOTS), -1, jnp.int32).at[target, inbox].set(patch_number)
    shuffles = jax.vmap(lambda row_key: jax.random.permutation(row_key, SLOTS))(jax.random.split(shuffle_key, device_list))
    table = jnp.full((device_list, SLOTS), -1, jnp.int32).at[jnp.arange(device_list, dtype=jnp.int32)[:, None], shuffles].set(incoming)
    return table.reshape(device_list * GRP_DEV, MEMBERS).astype(jnp.int32)


def shard_levels(rng, shape, shards, smallest, top_value):
    factor_of, own = 1.0, jax.random.fold_in(rng, 6)
    for dim, parts in shards:
        draws = jnp.exp(jax.random.uniform(jax.random.fold_in(own, dim), (parts,), jnp.float32, smallest / len(shards), top_value / len(shards)))
        factor_of = factor_of * jnp.repeat(draws, shape[dim] // parts).reshape([-1 if axis == dim else 1 for axis in range(len(shape))])
    return factor_of


def bell_draw(stream_key, dims, deviation, bound, cuts=(), kind=jnp.bfloat16):
    array = deviation * jax.random.normal(stream_key, dims, jnp.float32)
    if cuts:
        array = array * shard_levels(stream_key, dims, cuts, -0.22, 0.18)
    return jnp.clip(array, -bound, bound).astype(kind)


def setup_inputs(seed: int = 0) -> dict:
    key_list = jax.random.split(jax.random.key(seed), 6)
    estimate = draw_estimate(jax.random.fold_in(key_list[5], 71), 0)
    dual = bell_draw(key_list[1], (NX, NY, NZ, COMP), 0.5, 4.0, ((0, 8), (1, 16)))
    corners = draw_corners(jax.random.fold_in(key_list[5], 71), 0)
    members = draw_members(jax.random.fold_in(key_list[5], 71), 0)
    thresholds = jnp.clip(jnp.exp(jax.random.uniform(key_list[4], (GROUPS,), jnp.float32, math.log(3000.0), math.log(60000.0))), 3000.0, 60000.0)
    return {"estimate": estimate, "dual": dual, "corners": corners, "members": members, "thresholds": thresholds}


data_weight = 2.0

def shrink(group_grams, tau):
    dimension = group_grams.shape[-1]
    identity = jnp.eye(dimension, dtype=group_grams.dtype)
    system = group_grams + tau[:, None, None] * identity
    cholesky_factor = jnp.linalg.cholesky(system)
    inverse_factor = lax.linalg.triangular_solve(cholesky_factor, jnp.broadcast_to(identity, system.shape), left_side=True, lower=True)
    inverse = jnp.einsum('gkc,gkd->gcd', inverse_factor, inverse_factor, precision=lax.Precision.HIGHEST)
    return (identity - tau[:, None, None] * inverse).astype(jnp.bfloat16)

def reference(estimate, dual, corners, members, thresholds):
    mixture = (estimate.astype(jnp.float32) + dual.astype(jnp.float32)).astype(jnp.bfloat16)
    cell_rows = mixture.reshape(NX * NY * NZ, COMP)
    within = jnp.arange(PATCH ** 3, dtype=jnp.int32)
    shift_amount = (within // (PATCH * PATCH) * NY + within // PATCH % PATCH) * NZ + within % PATCH
    first_cell = (corners[0] * NY + corners[1]) * NZ + corners[2]
    row_index = first_cell[:, None] + shift_amount[None, :]
    present = members >= 0
    chosen = jnp.where(present, members, 0)

    def group_gram(group_item):
        listed, weight = group_item
        values = cell_rows[row_index[listed].reshape(-1)].astype(jnp.float32)
        values = values * jnp.repeat(weight, PATCH ** 3)[:, None]
        return jnp.dot(values.T, values, precision=lax.Precision.HIGHEST)
    group_grams = lax.map(group_gram, (chosen, present.astype(jnp.float32)))
    factors = shrink(group_grams, thresholds)
    numbers = jnp.broadcast_to(jnp.arange(GROUPS, dtype=jnp.int32)[:, None], members.shape)
    group_of = jnp.zeros((NPATCH,), jnp.int32).at[jnp.where(present, members, NPATCH)].set(numbers, mode='drop')
    block_size = 256 if NPATCH % 256 == 0 else PATCH_DEV

    def add_block(aggregate, block_item):
        picked, group_index = block_item
        values = cell_rows[picked].astype(jnp.float32)
        weights = factors[group_index].astype(jnp.float32)
        result = jnp.einsum('kvc,kcd->kvd', values, weights, precision=lax.Precision.HIGHEST)
        return (aggregate.at[picked.reshape(-1)].add(result.reshape(-1, COMP)), None)
    aggregate, _ = lax.scan(add_block, jnp.zeros((NX * NY * NZ, COMP), jnp.float32), (row_index.reshape(-1, block_size, PATCH ** 3), group_of.reshape(-1, block_size)))
    counts = jnp.zeros((NX * NY * NZ,), jnp.float32).at[row_index.reshape(-1)].add(1.0)
    lowrank = (aggregate + data_weight * cell_rows.astype(jnp.float32)) / (counts + data_weight)[:, None]
    lowrank = lowrank.reshape(NX, NY, NZ, COMP)
    dual_next = dual.astype(jnp.float32) + estimate.astype(jnp.float32) - lowrank
    return (lowrank, dual_next)
```

```python
import functools

import jax
import jax.numpy as jnp
from jax import lax
from jax.experimental import pallas as pl
from jax.experimental.pallas import tpu as pltpu
from jax.sharding import PartitionSpec as P

PATCH = 8
DATA_WEIGHT = 2.0
F32 = jnp.float32
BF16 = jnp.bfloat16
BOTH = ("gx", "gy")
NB = 16

VMEM = pl.BlockSpec(memory_space=pltpu.VMEM)
SMEM = pl.BlockSpec(memory_space=pltpu.SMEM)
PARAMS = pltpu.CompilerParams(vmem_limit_bytes=48 * 1024 * 1024)


def call(body, out_shape, *args, specs=None, scratch=(), flops=0, nbytes=0):
    outs = jax.tree.map(lambda _: VMEM, out_shape)
    return pl.pallas_call(
        body,
        out_shape=out_shape,
        in_specs=specs or [VMEM] * len(args),
        out_specs=outs,
        scratch_shapes=list(scratch),
        compiler_params=PARAMS,
        cost_estimate=pl.CostEstimate(flops=flops, bytes_accessed=nbytes, transcendentals=0),
    )(*args)


def neighbors(value, axis, first, last):
    size = lax.axis_size(axis)
    up = [(i, i + 1) for i in range(size - 1)]
    down = [(j, i) for i, j in up]
    before = lax.ppermute(last, axis, up)
    after = lax.ppermute(first, axis, down)
    return before, after


def group_table_body(members_ref, out_ref):
    rows = members_ref.shape[0]
    per = 8
    high = lax.broadcasted_iota(jnp.int32, (64, 128), 0)
    low = lax.broadcasted_iota(jnp.int32, (128, 128), 0)
    lane = lax.broadcasted_iota(jnp.int32, (1, 128), 1)

    def step(i, acc):
        block = members_ref[pl.ds(pl.multiple_of(i * per, per), per), :]
        coarse, fine, lows = [], [], []
        for j in range(per):
            entry = block[j : j + 1, :]
            on = high == (entry >> 7)
            group = (i * per + j) * 8 + (lane >> 4)
            zero = jnp.zeros((64, 128), F32)
            coarse.append(
                jnp.where(on, jnp.broadcast_to((group >> 4).astype(F32), (64, 128)), zero)
            )
            fine.append(
                jnp.where(on, jnp.broadcast_to((group & 15).astype(F32), (64, 128)), zero)
            )
            lows.append(jnp.where(low == (entry & 127), 1.0, 0.0))
        left = jnp.concatenate(
            [jnp.concatenate(coarse, 1), jnp.concatenate(fine, 1)], 0
        ).astype(BF16)
        right = jnp.concatenate(lows, 1).astype(BF16)
        return acc + lax.dot_general(
            left, right, (((1,), (1,)), ((), ())), preferred_element_type=F32
        )

    acc = lax.fori_loop(0, rows // per, step, jnp.zeros((128, 128), F32))
    out_ref[...] = (acc[:64] * 16.0 + acc[64:]).astype(jnp.int32)


def counts_body(corner_ref, base_ref, out_ref):
    lanes = corner_ref.shape[1]
    px = corner_ref[0:1, :] - base_ref[0]
    py = corner_ref[1:2, :] - base_ref[1]
    pz = corner_ref[2:3, :]
    z = lax.broadcasted_iota(jnp.int32, (32, lanes), 0)
    in_z = jnp.where((z >= pz) & (z < pz + PATCH), 1.0, 0.0)
    ones = jnp.ones((lanes, 128), BF16)

    def column(x, _):
        in_x = (px <= x) & (px > x - PATCH)
        parts = []
        for y in range(8):
            hit = jnp.where(in_x & (py <= y) & (py > y - PATCH), 1.0, 0.0)
            parts.append((hit * in_z).astype(BF16))
        cover = jnp.dot(jnp.concatenate(parts, 0), ones, preferred_element_type=F32)
        out_ref[pl.ds(pl.multiple_of(x * 256, 256), 256), :] = 1.0 / (cover + DATA_WEIGHT)
        return 0

    lax.fori_loop(0, 8, column, 0)


def load_patch(cells_ref, first):
    rows = []
    for a in range(PATCH):
        for b in range(PATCH):
            rows.append(cells_ref[pl.ds(first + (a * 16 + b) * 32, PATCH), :])
    return jnp.concatenate(rows, 0)


def gram_body(first_ref, own_ref, yb_ref, ya_ref, xb_ref, xa_ref, cells_ref, out_ref):
    cells_ref[pl.ds(0, 2048), :] = xb_ref[...].reshape(2048, 128).astype(F32)
    cells_ref[pl.ds(6144, 2048), :] = xa_ref[...].reshape(2048, 128).astype(F32)

    def fill(x, _):
        row = pl.multiple_of((x + 4) * 512, 512)
        cells_ref[pl.ds(row, 128), :] = yb_ref[x].reshape(128, 128).astype(F32)
        cells_ref[pl.ds(row + 128, 256), :] = own_ref[x].reshape(256, 128).astype(F32)
        cells_ref[pl.ds(row + 384, 128), :] = ya_ref[x].reshape(128, 128).astype(F32)
        return 0

    lax.fori_loop(0, 8, fill, 0)

    def patch(p, _):
        values = load_patch(cells_ref, first_ref[p]).astype(BF16)
        gram = lax.dot_general(values, values, (((0,), (0,)), ((), ())), preferred_element_type=F32)
        out_ref[pl.ds(p, 128, stride=64), :] = gram
        return 0

    lax.fori_loop(0, 64, patch, 0, unroll=2)


def group_sum_body(group_ref, rows_ref, out_ref, limbs_ref, hot_ref):
    def split(i, _):
        row = pl.multiple_of(i * 128, 128)
        value = rows_ref[pl.ds(row, 128), :]
        high = value.astype(BF16)
        limbs_ref[pl.ds(row, 128), 0:128] = high
        limbs_ref[pl.ds(row, 128), 128:256] = (value - high.astype(F32)).astype(BF16)
        return 0

    lax.fori_loop(0, 64, split, 0)
    sub = lax.broadcasted_iota(jnp.int32, (256, 128), 0)

    def chunk(i, _):
        base = i * 256
        for t in range(64):
            entry = group_ref[t : t + 1, :] - base
            hot_ref[:, t * 128 : (t + 1) * 128] = jnp.where(sub == entry, 1.0, 0.0).astype(BF16)
        total = jnp.dot(hot_ref[...], limbs_ref[...], preferred_element_type=F32)
        out_ref[pl.ds(pl.multiple_of(base, 256), 256), :] = total[:, :128] + total[:, 128:]
        return 0

    lax.fori_loop(0, 8, chunk, 0)


def shrink_body(tau_ref, rows_ref, out_ref, sys_ref, stage_ref):
    per = 16
    row_id = lax.broadcasted_iota(jnp.int32, (128, 128), 0)
    lane_id = lax.broadcasted_iota(jnp.int32, (128, 128), 1)
    diagonal = row_id == lane_id
    for g in range(per):
        matrix = rows_ref[pl.ds(g, 128, stride=per), :]
        sys_ref[g] = matrix + jnp.where(diagonal, tau_ref[g], 0.0)
    panel_sub = lax.broadcasted_iota(jnp.int32, (per, NB, 128), 1)
    panel_lane = lax.broadcasted_iota(jnp.int32, (per, NB, 128), 2)

    def block(b, _):
        start = pl.multiple_of(b * NB, NB)
        panel = sys_ref[:, pl.ds(start, NB), :]
        panel = pltpu.roll(panel.reshape(per * NB, 128), 128 - start, axis=1).reshape(per, NB, 128)
        for j in range(NB):
            column = panel[:, :, j : j + 1]
            pivot_row = panel[:, j : j + 1, :]
            pivot = 1.0 / panel[:, j : j + 1, j : j + 1]
            scaled = jnp.where(panel_lane[:, j : j + 1, :] == j, pivot, pivot_row * pivot)
            cleared = jnp.where(panel_lane == j, 0.0, panel)
            panel = jnp.where(panel_sub == j, scaled, cleared - column * scaled)
        panel = pltpu.roll(panel.reshape(per * NB, 128), start, axis=1).reshape(per, NB, 128)
        in_block = (lane_id >= start) & (lane_id < start + NB)
        for g in range(per):
            stage_ref[...] = jnp.zeros((128, 128), F32)
            stage_ref[pl.ds(start, NB), :] = panel[g]
            matrix = sys_ref[g]
            update = jnp.dot(
                matrix, stage_ref[...], precision=lax.Precision.HIGHEST, preferred_element_type=F32
            )
            sys_ref[g] = jnp.where(in_block, 0.0, matrix) - update
            sys_ref[g, pl.ds(start, NB), :] = panel[g]
        return 0

    lax.fori_loop(0, 128 // NB, block, 0)
    for g in range(per):
        factor = jnp.where(diagonal, 1.0, 0.0) - tau_ref[g] * sys_ref[g]
        out_ref[pl.ds(g, 128, stride=per), :] = factor


def expand_body(group_ref, rows_ref, out_ref, turned_ref):
    turned_ref[...] = group_ref[...].astype(F32).T.astype(jnp.int32)
    lane = lax.broadcasted_iota(jnp.int32, (128, 2048), 1)
    table = rows_ref[...]
    for t in range(64):
        hot = jnp.where(lane == turned_ref[:, t : t + 1], 1.0, 0.0).astype(BF16)
        out_ref[t * 128 : (t + 1) * 128, :] = jnp.dot(
            hot, table, preferred_element_type=F32
        ).astype(BF16)


def apply_body(first_ref, cells_ref, rows_ref, out_ref, wide_ref):
    wide_ref[...] = rows_ref[...].astype(F32)
    out_ref[...] = jnp.zeros_like(out_ref)

    def patch(p, _):
        first = first_ref[p]
        values = load_patch(cells_ref, first).astype(BF16)
        factor = wide_ref[pl.ds(p, 128, stride=64), :].astype(BF16)
        result = jnp.dot(values, factor, preferred_element_type=F32)
        for a in range(PATCH):
            for b in range(PATCH):
                at = pl.ds(first + (a * 16 + b) * 32, PATCH)
                i = (a * PATCH + b) * PATCH
                out_ref[at, :] += result[i : i + PATCH]
        return 0

    lax.fori_loop(0, 64, patch, 0)


def exchange(rows, chunk):
    shape = rows.shape
    rows = rows.reshape(128, chunk, 128)
    rows = lax.all_to_all(rows, BOTH, split_axis=0, concat_axis=0, tiled=True)
    return rows.reshape(shape)


def shards(estimate, dual, corners, members, thresholds):
    margin = PATCH // 2
    index_x = lax.axis_index("gx")
    index_y = lax.axis_index("gy")
    myself = index_x * 16 + index_y
    mixture = (estimate.astype(F32) + dual.astype(F32)).astype(BF16)

    yb, ya = neighbors(mixture, "gy", mixture[:, :margin], mixture[:, 8 - margin :])
    marked = corners + 1
    cb, ca = neighbors(marked, "gy", marked, marked)
    wide = jnp.concatenate([yb, mixture, ya], 1)
    xb, xa = neighbors(wide, "gx", wide[:margin], wide[8 - margin :])
    near = jnp.concatenate([cb, marked, ca], 1)
    nb, na = neighbors(near, "gx", near, near)
    near = jnp.concatenate([nb, near, na, jnp.zeros((3, 64), jnp.int32)], 1)
    near = jnp.where(near == 0, -1000, near - 1)

    table = call(
        group_table_body,
        jax.ShapeDtypeStruct((64, 128), jnp.int32),
        members.reshape(256, 128),
        flops=2 * 128 * 32768 * 128,
        nbytes=1 << 17,
    )
    base = jnp.stack([index_x * 8, index_y * 8])
    inverse_counts = call(
        counts_body,
        jax.ShapeDtypeStruct((2048, 128), F32),
        near,
        base,
        specs=[VMEM, SMEM],
        flops=2 * 2048 * 640 * 128,
        nbytes=1 << 20,
    )

    begin_x = corners[0] - (index_x * 8 - margin)
    begin_y = corners[1] - (index_y * 8 - margin)
    first = (begin_x * 16 + begin_y) * 32 + corners[2]
    cells, grams = call(
        gram_body,
        (jax.ShapeDtypeStruct((8192, 128), F32), jax.ShapeDtypeStruct((8192, 128), F32)),
        first,
        mixture,
        yb,
        ya,
        xb,
        xa,
        specs=[SMEM] + [VMEM] * 5,
        flops=2 * 64 * 512 * 128 * 128,
        nbytes=10 << 20,
    )
    rows = exchange(grams, 64)
    sums = call(
        group_sum_body,
        jax.ShapeDtypeStruct((2048, 128), F32),
        table,
        rows,
        scratch=[pltpu.VMEM((8192, 256), BF16), pltpu.VMEM((256, 8192), BF16)],
        flops=2 * 2048 * 8192 * 256,
        nbytes=5 << 20,
    )
    mine = exchange(sums, 16)
    tau = lax.dynamic_slice_in_dim(thresholds, myself * 16, 16)
    factors = call(
        shrink_body,
        jax.ShapeDtypeStruct((2048, 128), F32),
        tau,
        mine,
        specs=[SMEM, VMEM],
        scratch=[pltpu.VMEM((16, 128, 128), F32), pltpu.VMEM((128, 128), F32)],
        flops=2 * 16 * 8 * 6 * 128**3,
        nbytes=2 << 20,
    )
    factor_rows = exchange(factors.astype(BF16), 16)
    patch_rows = call(
        expand_body,
        jax.ShapeDtypeStruct((8192, 128), BF16),
        table,
        factor_rows,
        scratch=[pltpu.VMEM((128, 64), jnp.int32)],
        flops=2 * 2048 * 8192 * 128,
        nbytes=3 << 20,
    )
    patch_factors = exchange(patch_rows, 64)
    aggregate = call(
        apply_body,
        jax.ShapeDtypeStruct((8192, 128), F32),
        first,
        cells,
        patch_factors,
        specs=[SMEM, VMEM, VMEM],
        scratch=[pltpu.VMEM((8192, 128), F32)],
        flops=2 * 64 * 512 * 128 * 128,
        nbytes=10 << 20,
    )
    aggregate = aggregate.reshape(16, 16, 32, 128)

    from_low, from_high = neighbors(
        aggregate, "gx", aggregate[:margin].astype(BF16), aggregate[16 - margin :].astype(BF16)
    )
    inner = aggregate[margin : 16 - margin]
    inner = jnp.concatenate(
        [inner[:margin] + from_low.astype(F32), inner[margin:] + from_high.astype(F32)], 0
    )
    from_low, from_high = neighbors(
        inner, "gy", inner[:, :margin].astype(BF16), inner[:, 16 - margin :].astype(BF16)
    )
    sums = inner[:, margin : 16 - margin]
    sums = jnp.concatenate(
        [sums[:, :margin] + from_low.astype(F32), sums[:, margin:] + from_high.astype(F32)], 1
    )
    lowrank = (sums + DATA_WEIGHT * mixture.astype(F32)) * inverse_counts.reshape(8, 8, 32, 128)
    dual_next = dual.astype(F32) + estimate.astype(F32) - lowrank
    return lowrank, dual_next


def solution(mesh):
    in_specs = (
        P("gx", "gy", None, None),
        P("gx", "gy", None, None),
        P(None, ("gx", "gy")),
        P(),
        P(),
    )
    out_specs = (P("gx", "gy", None, None), P("gx", "gy", None, None))
    return jax.shard_map(shards, mesh=mesh, in_specs=in_specs, out_specs=out_specs, check_vma=False)
```

```python
import functools

import jax
import jax.numpy as jnp
from jax import lax
from jax.experimental import pallas as pl
from jax.experimental.pallas import tpu as pltpu
from jax.sharding import PartitionSpec as P

PATCH = 8
DATA_WEIGHT = 2.0
F32 = jnp.float32
BF16 = jnp.bfloat16
BOTH = ("gx", "gy")
NB = 16

VMEM = pl.BlockSpec(memory_space=pltpu.VMEM)
SMEM = pl.BlockSpec(memory_space=pltpu.SMEM)
PARAMS = pltpu.CompilerParams(vmem_limit_bytes=48 * 1024 * 1024)


def call(body, out_shape, *args, specs=None, scratch=(), flops=0, nbytes=0):
    outs = jax.tree.map(lambda _: VMEM, out_shape)
    return pl.pallas_call(
        body,
        out_shape=out_shape,
        in_specs=specs or [VMEM] * len(args),
        out_specs=outs,
        scratch_shapes=list(scratch),
        compiler_params=PARAMS,
        cost_estimate=pl.CostEstimate(flops=flops, bytes_accessed=nbytes, transcendentals=0),
    )(*args)


def neighbors(value, axis, first, last):
    size = lax.axis_size(axis)
    up = [(i, i + 1) for i in range(size - 1)]
    down = [(j, i) for i, j in up]
    before = lax.ppermute(last, axis, up)
    after = lax.ppermute(first, axis, down)
    return before, after


def packed_masks():
    row = lax.broadcasted_iota(jnp.int32, (64, 128), 0)
    lane = lax.broadcasted_iota(jnp.int32, (64, 128), 1)
    return (lane < 64) & (row > lane), row == lane, lane == row + 64


def pack_symmetric(matrix, masks):
    moved, _, low_diagonal = masks
    top, bottom = matrix[:64], matrix[64:]
    packed = jnp.where(moved, pltpu.roll(bottom, 64, axis=1), top)
    return packed, jnp.where(low_diagonal, bottom, 0.0)


def unpack_symmetric(packed, diagonal, masks):
    moved, top_diagonal, low_diagonal = masks
    top = jnp.where(moved, 0.0, jnp.where(top_diagonal, 0.5 * packed, packed))
    bottom = pltpu.roll(jnp.where(moved, packed, 0.0), 64, axis=1)
    bottom = bottom + jnp.where(low_diagonal, 0.5 * diagonal, 0.0)
    half = jnp.concatenate([top, bottom], 0)
    return half + half.T


def group_table_body(side_ref, members_ref, out_ref):
    rows = members_ref.shape[0]
    per = 8
    high = lax.broadcasted_iota(jnp.int32, (32, 128), 0)
    low = lax.broadcasted_iota(jnp.int32, (128, 128), 0)
    lane = lax.broadcasted_iota(jnp.int32, (1, 128), 1)
    side = side_ref[0]

    def step(i, acc):
        block = members_ref[pl.ds(pl.multiple_of(i * per, per), per), :]
        coarse, fine, lows = [], [], []
        for j in range(per):
            entry = block[j : j + 1, :]
            at_high = jnp.where(((entry >> 5) & 1) == side, entry >> 8, -1)
            at_low = ((entry >> 6) & 3) * 32 + (entry & 31)
            on = high == at_high
            group = (i * per + j) * 8 + (lane >> 4)
            coarse.append(
                jnp.where(on, jnp.broadcast_to((group >> 4).astype(F32), (32, 128)), 0.0)
            )
            fine.append(
                jnp.where(on, jnp.broadcast_to((group & 15).astype(F32), (32, 128)), 0.0)
            )
            lows.append(jnp.where(low == at_low, 1.0, 0.0))
        left = jnp.concatenate(
            [jnp.concatenate(coarse, 1), jnp.concatenate(fine, 1)], 0
        ).astype(BF16)
        right = jnp.concatenate(lows, 1).astype(BF16)
        return acc + lax.dot_general(
            left, right, (((1,), (1,)), ((), ())), preferred_element_type=F32
        )

    acc = lax.fori_loop(0, rows // per, step, jnp.zeros((64, 128), F32))
    out_ref[...] = (acc[:32] * 16.0 + acc[32:]).astype(jnp.int32)


def counts_body(corner_ref, base_ref, out_ref):
    lanes = corner_ref.shape[1]
    px = corner_ref[0:1, :] - base_ref[0]
    py = corner_ref[1:2, :] - base_ref[1]
    pz = corner_ref[2:3, :]
    z = lax.broadcasted_iota(jnp.int32, (32, lanes), 0)
    in_z = jnp.where((z >= pz) & (z < pz + PATCH), 1.0, 0.0)
    ones = jnp.ones((lanes, 128), BF16)

    def column(x, _):
        in_x = (px <= x) & (px > x - PATCH)
        parts = []
        for y in range(8):
            hit = jnp.where(in_x & (py <= y) & (py > y - PATCH), 1.0, 0.0)
            parts.append((hit * in_z).astype(BF16))
        cover = jnp.dot(jnp.concatenate(parts, 0), ones, preferred_element_type=F32)
        out_ref[pl.ds(pl.multiple_of(x * 256, 256), 256), :] = 1.0 / (cover + DATA_WEIGHT)
        return 0

    lax.fori_loop(0, 8, column, 0)


def load_patch(cells_ref, first):
    rows = []
    for a in range(PATCH):
        for b in range(PATCH):
            rows.append(cells_ref[pl.ds(first + (a * 16 + b) * 32, PATCH), :])
    return jnp.concatenate(rows, 0)


def gram_body(first_ref, own_ref, yb_ref, ya_ref, xb_ref, xa_ref, cells_ref, out_ref, diag_ref):
    cells_ref[pl.ds(0, 2048), :] = xb_ref[...].reshape(2048, 128).astype(F32)
    cells_ref[pl.ds(6144, 2048), :] = xa_ref[...].reshape(2048, 128).astype(F32)

    def fill(x, _):
        row = pl.multiple_of((x + 4) * 512, 512)
        cells_ref[pl.ds(row, 128), :] = yb_ref[x].reshape(128, 128).astype(F32)
        cells_ref[pl.ds(row + 128, 256), :] = own_ref[x].reshape(256, 128).astype(F32)
        cells_ref[pl.ds(row + 384, 128), :] = ya_ref[x].reshape(128, 128).astype(F32)
        return 0

    lax.fori_loop(0, 8, fill, 0)
    diag_ref[...] = jnp.zeros_like(diag_ref)
    masks = packed_masks()

    def patch(p, _):
        values = load_patch(cells_ref, first_ref[p]).astype(BF16)
        gram = lax.dot_general(values, values, (((0,), (0,)), ((), ())), preferred_element_type=F32)
        packed, rest = pack_symmetric(gram, masks)
        side = p // 32
        out_ref[pl.ds(side * (64 * 33) + p - side * 32, 64, stride=33), :] = packed
        diag_ref[pl.ds(p, 1), :] = jnp.sum(rest, axis=0, keepdims=True)
        return 0

    lax.fori_loop(0, 64, patch, 0, unroll=2)
    turned = diag_ref[...].T[64:]
    out_ref[pl.ds(32, 64, stride=33), :] = turned
    out_ref[pl.ds(64 * 33 + 32, 64, stride=33), :] = pltpu.roll(turned, 96, axis=1)


def group_sum_body(group_ref, rows_ref, out_ref, limbs_ref, hot_ref, diag_ref):
    def split(i, _):
        value = rows_ref[pl.ds(i * 33, 32), :]
        high = value.astype(BF16)
        row = pl.multiple_of(i * 32, 32)
        limbs_ref[pl.ds(row, 32), 0:128] = high
        limbs_ref[pl.ds(row, 32), 128:256] = (value - high.astype(F32)).astype(BF16)
        return 0

    lax.fori_loop(0, 128, split, 0, unroll=4)
    used = lax.broadcasted_iota(jnp.int32, (32, 128), 1) < 32
    diagonal = jnp.zeros((32, 128), F32)
    for c in range(4):
        part = jnp.where(used, rows_ref[pl.ds(32 + 33 * c, 32, stride=132), :], 0.0)
        diagonal = diagonal + (pltpu.roll(part, 32 * c, axis=1) if c else part)
    diag_ref[...] = diagonal
    sub = lax.broadcasted_iota(jnp.int32, (256, 128), 0)
    eye = lax.broadcasted_iota(jnp.int32, (16, 128), 0) == lax.broadcasted_iota(
        jnp.int32, (16, 128), 1
    )

    def chunk(i, _):
        base = i * 256
        picked = jnp.zeros((256, 128), F32)
        for t in range(32):
            on = sub == group_ref[t : t + 1, :] - base
            hot_ref[:, t * 128 : (t + 1) * 128] = jnp.where(on, 1.0, 0.0).astype(BF16)
            picked = picked + jnp.where(on, diag_ref[t : t + 1, :], 0.0)
        total = jnp.dot(hot_ref[...], limbs_ref[...], preferred_element_type=F32)
        total = total[:, :128] + total[:, 128:]
        picked = jnp.sum(picked, axis=1, keepdims=True)
        for d in range(16):
            row = (i * 16 + d) * 17
            part = slice(d * 16, d * 16 + 16)
            out_ref[pl.ds(row, 16), :] = total[part]
            out_ref[pl.ds(row + 16, 1), :] = jnp.sum(
                jnp.where(eye, picked[part], 0.0), axis=0, keepdims=True
            )
        return 0

    lax.fori_loop(0, 8, chunk, 0)


def shrink_body(tau_ref, rows_ref, out_ref, sys_ref, stage_ref):
    per = 16
    row_id = lax.broadcasted_iota(jnp.int32, (128, 128), 0)
    lane_id = lax.broadcasted_iota(jnp.int32, (128, 128), 1)
    eye = jnp.where(row_id == lane_id, 1.0, 0.0)
    masks = packed_masks()
    half = 64 * 17
    diagonals = rows_ref[pl.ds(16, 64, stride=17), :] + rows_ref[pl.ds(half + 16, 64, stride=17), :]
    for g in range(per):
        packed = rows_ref[pl.ds(g, 64, stride=17), :] + rows_ref[pl.ds(half + g, 64, stride=17), :]
        sys_ref[g] = unpack_symmetric(packed, diagonals[:, g : g + 1], masks) + tau_ref[g] * eye
    panel_sub = lax.broadcasted_iota(jnp.int32, (per, NB, 128), 1)
    panel_lane = lax.broadcasted_iota(jnp.int32, (per, NB, 128), 2)

    def block(b, _):
        start = pl.multiple_of(b * NB, NB)
        panel = sys_ref[:, pl.ds(start, NB), :]
        panel = pltpu.roll(panel.reshape(per * NB, 128), 128 - start, axis=1).reshape(per, NB, 128)
        for j in range(NB):
            column = panel[:, :, j : j + 1]
            pivot_row = panel[:, j : j + 1, :]
            pivot = 1.0 / panel[:, j : j + 1, j : j + 1]
            scaled = jnp.where(panel_lane[:, j : j + 1, :] == j, pivot, pivot_row * pivot)
            cleared = jnp.where(panel_lane == j, 0.0, panel)
            panel = jnp.where(panel_sub == j, scaled, cleared - column * scaled)
        panel = pltpu.roll(panel.reshape(per * NB, 128), start, axis=1).reshape(per, NB, 128)
        in_lanes = (lane_id >= start) & (lane_id < start + NB)
        in_rows = (row_id >= start) & (row_id < start + NB)
        for g in range(per):
            matrix = sys_ref[g]
            wide = jnp.where(in_rows, jnp.concatenate([panel[g]] * (128 // NB), 0), 0.0)
            w0, w1, w2 = limbs(wide)
            a0, a1, a2 = limbs(matrix)
            main = jnp.dot(
                jnp.concatenate([a0, a1], 1),
                jnp.concatenate([jnp.concatenate([w0, w0], 0), jnp.concatenate([w1, w1], 0)], 1),
                preferred_element_type=F32,
            )
            small = jnp.dot(
                jnp.concatenate([a0, a2], 1),
                jnp.concatenate([w2, w0], 0),
                preferred_element_type=F32,
            )
            update = main[:, :128] + (main[:, 128:] + small)
            sys_ref[g] = jnp.where(in_rows, wide, jnp.where(in_lanes, 0.0, matrix) - update)
        return 0

    lax.fori_loop(0, 128 // NB, block, 0)
    place = lax.broadcasted_iota(jnp.int32, (64, 128), 1)
    extra = jnp.zeros((64, 128), F32)
    for g in range(per):
        packed, rest = pack_symmetric(eye - tau_ref[g] * sys_ref[g], masks)
        stage_ref[pl.ds(g, 64, stride=18), :] = packed
        extra = jnp.where(place == g, jnp.sum(rest, axis=1, keepdims=True), extra)
    stage_ref[pl.ds(16, 64, stride=18), :] = extra
    stage_ref[pl.ds(17, 64, stride=18), :] = jnp.zeros((64, 128), F32)
    result = stage_ref[...].astype(BF16)
    out_ref[0:1152, :] = result
    out_ref[1152:2304, :] = result


def limbs(value):
    first = value.astype(BF16)
    rest = value - first.astype(F32)
    second = rest.astype(BF16)
    return first, second, (rest - second.astype(F32)).astype(BF16)


def expand_body(group_ref, rows_ref, out_ref, turned_ref, wide_ref, table_ref, stage_ref):
    turned_ref[...] = group_ref[...].astype(F32).T.astype(jnp.int32)
    wide_ref[...] = rows_ref[...].astype(F32)
    eye = lax.broadcasted_iota(jnp.int32, (16, 128), 0) == lax.broadcasted_iota(
        jnp.int32, (16, 128), 1
    )

    def gather(d, _):
        row = pl.multiple_of(d * 16, 16)
        table_ref[pl.ds(row, 16), 0:128] = wide_ref[pl.ds(d * 18, 16), :].astype(BF16)
        extra = wide_ref[pl.ds(d * 18 + 16, 1), :]
        table_ref[pl.ds(row, 16), 128:256] = jnp.where(eye, extra, 0.0).astype(BF16)
        return 0

    lax.fori_loop(0, 128, gather, 0, unroll=4)
    lane = lax.broadcasted_iota(jnp.int32, (128, 2048), 1)
    eye = lax.broadcasted_iota(jnp.int32, (32, 128), 0) == lax.broadcasted_iota(
        jnp.int32, (32, 128), 1
    )
    for t in range(32):
        hot = jnp.where(lane == turned_ref[:, t : t + 1], 1.0, 0.0).astype(BF16)
        both = jnp.dot(hot, table_ref[...], preferred_element_type=F32)
        value = jnp.sum(both[:, 128:], axis=1, keepdims=True)
        for s in range(4):
            row = (t * 4 + s) * 34
            part = slice(s * 32, s * 32 + 32)
            stage_ref[row : row + 32, :] = both[part, :128]
            stage_ref[row + 32 : row + 33, :] = jnp.sum(
                jnp.where(eye, value[part], 0.0), axis=0, keepdims=True
            )
            stage_ref[row + 33 : row + 34, :] = jnp.zeros((1, 128), F32)
    out_ref[...] = stage_ref[...].astype(BF16)


def apply_body(first_ref, cells_ref, rows_ref, inner_ref, low_ref, high_ref, wide_ref, sum_ref):
    wide_ref[...] = rows_ref[...].astype(F32)
    sum_ref[...] = jnp.zeros_like(sum_ref)
    masks = packed_masks()
    lane = lax.broadcasted_iota(jnp.int32, (64, 128), 1)

    def product(p):
        side = p // 32
        slot = p - side * 32
        base = side * (64 * 34)
        packed = wide_ref[pl.ds(base + slot, 64, stride=34), :]
        diagonals = wide_ref[pl.ds(base + 32, 64, stride=34), :]
        diagonal = jnp.sum(jnp.where(lane == slot, diagonals, 0.0), axis=1, keepdims=True)
        factor = unpack_symmetric(packed, diagonal, masks).astype(BF16)
        values = load_patch(cells_ref, first_ref[p]).astype(BF16)
        return jnp.dot(values, factor, preferred_element_type=F32)

    def pair(i, _):
        for p, result in [(2 * i + k, product(2 * i + k)) for k in range(2)]:
            first = first_ref[p]
            for a in range(PATCH):
                for b in range(PATCH):
                    at = pl.ds(first + (a * 16 + b) * 32, PATCH)
                    row = (a * PATCH + b) * PATCH
                    sum_ref[at, :] += result[row : row + PATCH]
        return 0

    lax.fori_loop(0, 32, pair, 0)
    low_ref[...] = sum_ref[0:2048, :].astype(BF16)
    inner_ref[...] = sum_ref[2048:6144, :]
    high_ref[...] = sum_ref[6144:8192, :].astype(BF16)


def exchange(rows, sublanes):
    shape = rows.shape
    rows = rows.reshape(128, shape[0] // (128 * sublanes), sublanes, 128)
    rows = lax.all_to_all(rows, BOTH, split_axis=0, concat_axis=0, tiled=True)
    return rows.reshape(shape)


def shards(estimate, dual, corners, members, thresholds):
    margin = PATCH // 2
    index_x = lax.axis_index("gx")
    index_y = lax.axis_index("gy")
    myself = index_x * 16 + index_y
    mixture = (estimate.astype(F32) + dual.astype(F32)).astype(BF16)

    yb, ya = neighbors(mixture, "gy", mixture[:, :margin], mixture[:, 8 - margin :])
    marked = corners + 1
    cb, ca = neighbors(marked, "gy", marked, marked)
    wide = jnp.concatenate([yb, mixture, ya], 1)
    xb, xa = neighbors(wide, "gx", wide[:margin], wide[8 - margin :])
    near = jnp.concatenate([cb, marked, ca], 1)
    nb, na = neighbors(near, "gx", near, near)
    near = jnp.concatenate([nb, near, na, jnp.zeros((3, 64), jnp.int32)], 1)
    near = jnp.where(near == 0, -1000, near - 1)

    side = (myself // 64).reshape(1)
    table = call(
        group_table_body,
        jax.ShapeDtypeStruct((32, 128), jnp.int32),
        side,
        members.reshape(256, 128),
        specs=[SMEM, VMEM],
        flops=2 * 128 * 32768 * 64,
        nbytes=1 << 17,
    )
    base = jnp.stack([index_x * 8, index_y * 8])
    inverse_counts = call(
        counts_body,
        jax.ShapeDtypeStruct((2048, 128), F32),
        near,
        base,
        specs=[VMEM, SMEM],
        flops=2 * 2048 * 640 * 128,
        nbytes=1 << 20,
    )

    begin_x = corners[0] - (index_x * 8 - margin)
    begin_y = corners[1] - (index_y * 8 - margin)
    first = (begin_x * 16 + begin_y) * 32 + corners[2]
    cells, grams = call(
        gram_body,
        (jax.ShapeDtypeStruct((8192, 128), F32), jax.ShapeDtypeStruct((128 * 33, 128), F32)),
        first,
        mixture,
        yb,
        ya,
        xb,
        xa,
        specs=[SMEM] + [VMEM] * 5,
        scratch=[pltpu.VMEM((128, 128), F32)],
        flops=2 * 64 * 512 * 128 * 128,
        nbytes=10 << 20,
    )
    rows = exchange(grams, 1)
    sums = call(
        group_sum_body,
        jax.ShapeDtypeStruct((128 * 17, 128), F32),
        table,
        rows,
        scratch=[
            pltpu.VMEM((4096, 256), BF16),
            pltpu.VMEM((256, 4096), BF16),
            pltpu.VMEM((32, 128), F32),
        ],
        flops=2 * 2048 * 4096 * 256,
        nbytes=5 << 20,
    )
    mine = exchange(sums, 1)
    tau = lax.dynamic_slice_in_dim(thresholds, myself * 16, 16)
    factors = call(
        shrink_body,
        jax.ShapeDtypeStruct((128 * 18, 128), BF16),
        tau,
        mine,
        specs=[SMEM, VMEM],
        scratch=[pltpu.VMEM((16, 128, 128), F32), pltpu.VMEM((64 * 18, 128), F32)],
        flops=2 * 16 * 8 * 6 * 128**3,
        nbytes=2 << 20,
    )
    factor_rows = exchange(factors, 2)
    patch_rows = call(
        expand_body,
        jax.ShapeDtypeStruct((128 * 34, 128), BF16),
        table,
        factor_rows,
        scratch=[
            pltpu.VMEM((128, 32), jnp.int32),
            pltpu.VMEM((128 * 18, 128), F32),
            pltpu.VMEM((2048, 256), BF16),
            pltpu.VMEM((128 * 34, 128), F32),
        ],
        flops=2 * 2048 * 4096 * 256,
        nbytes=3 << 20,
    )
    patch_factors = exchange(patch_rows, 2)
    edge = jax.ShapeDtypeStruct((2048, 128), BF16)
    inner, low, high = call(
        apply_body,
        (jax.ShapeDtypeStruct((4096, 128), F32), edge, edge),
        first,
        cells,
        patch_factors,
        specs=[SMEM, VMEM, VMEM],
        scratch=[pltpu.VMEM((128 * 34, 128), F32), pltpu.VMEM((8192, 128), F32)],
        flops=2 * 64 * 512 * 128 * 128,
        nbytes=10 << 20,
    )
    inner = inner.reshape(8, 16, 32, 128)
    from_low, from_high = neighbors(
        inner, "gx", low.reshape(4, 16, 32, 128), high.reshape(4, 16, 32, 128)
    )
    inner = jnp.concatenate(
        [inner[:margin] + from_low.astype(F32), inner[margin:] + from_high.astype(F32)], 0
    )
    from_low, from_high = neighbors(
        inner, "gy", inner[:, :margin].astype(BF16), inner[:, 16 - margin :].astype(BF16)
    )
    sums = inner[:, margin : 16 - margin]
    sums = jnp.concatenate(
        [sums[:, :margin] + from_low.astype(F32), sums[:, margin:] + from_high.astype(F32)], 1
    )
    lowrank = (sums + DATA_WEIGHT * mixture.astype(F32)) * inverse_counts.reshape(8, 8, 32, 128)
    dual_next = dual.astype(F32) + estimate.astype(F32) - lowrank
    return lowrank, dual_next


def solution(mesh):
    in_specs = (
        P("gx", "gy", None, None),
        P("gx", "gy", None, None),
        P(None, ("gx", "gy")),
        P(),
        P(),
    )
    out_specs = (P("gx", "gy", None, None), P("gx", "gy", None, None))
    return jax.shard_map(shards, mesh=mesh, in_specs=in_specs, out_specs=out_specs, check_vma=False)
```

```python
import functools

import jax
import jax.numpy as jnp
from jax import lax
from jax.experimental import pallas as pl
from jax.experimental.pallas import tpu as pltpu
from jax.sharding import PartitionSpec as P

PATCH = 8
DATA_WEIGHT = 2.0
F32 = jnp.float32
BF16 = jnp.bfloat16
BOTH = ("gx", "gy")
NB = 16

VMEM = pl.BlockSpec(memory_space=pltpu.VMEM)
SMEM = pl.BlockSpec(memory_space=pltpu.SMEM)
PARAMS = pltpu.CompilerParams(vmem_limit_bytes=48 * 1024 * 1024)


def call(body, out_shape, *args, specs=None, scratch=(), flops=0, nbytes=0):
    outs = jax.tree.map(lambda _: VMEM, out_shape)
    return pl.pallas_call(
        body,
        out_shape=out_shape,
        in_specs=specs or [VMEM] * len(args),
        out_specs=outs,
        scratch_shapes=list(scratch),
        compiler_params=PARAMS,
        cost_estimate=pl.CostEstimate(flops=flops, bytes_accessed=nbytes, transcendentals=0),
    )(*args)


def neighbors(value, axis, first, last):
    size = lax.axis_size(axis)
    up = [(i, i + 1) for i in range(size - 1)]
    down = [(j, i) for i, j in up]
    before = lax.ppermute(last, axis, up)
    after = lax.ppermute(first, axis, down)
    return before, after


def packed_masks():
    row = lax.broadcasted_iota(jnp.int32, (64, 128), 0)
    lane = lax.broadcasted_iota(jnp.int32, (64, 128), 1)
    return (lane < 64) & (row > lane), row == lane, lane == row + 64


def pack_symmetric(matrix, masks):
    moved, _, low_diagonal = masks
    top, bottom = matrix[:64], matrix[64:]
    packed = jnp.where(moved, pltpu.roll(bottom, 64, axis=1), top)
    return packed, jnp.where(low_diagonal, bottom, 0.0)


def unpack_symmetric(packed, diagonal, masks, dtype):
    moved, top_diagonal, low_diagonal = masks
    top = jnp.where(moved, 0.0, jnp.where(top_diagonal, 0.5 * packed, packed))
    bottom = pltpu.roll(jnp.where(moved, packed, 0.0), 64, axis=1)
    bottom = bottom + jnp.where(low_diagonal, 0.5 * diagonal, 0.0)
    half = jnp.concatenate([top, bottom], 0).astype(dtype)
    return half + half.T


def group_table_body(side_ref, members_ref, out_ref):
    rows = members_ref.shape[0]
    per = 8
    high = lax.broadcasted_iota(jnp.int32, (32, 128), 0)
    low = lax.broadcasted_iota(jnp.int32, (128, 128), 0)
    lane = lax.broadcasted_iota(jnp.int32, (1, 128), 1)
    side = side_ref[0]

    def step(i, acc):
        block = members_ref[pl.ds(pl.multiple_of(i * per, per), per), :]
        coarse, fine, lows = [], [], []
        for j in range(per):
            entry = block[j : j + 1, :]
            at_high = jnp.where(((entry >> 5) & 1) == side, entry >> 8, -1)
            at_low = ((entry >> 6) & 3) * 32 + (entry & 31)
            on = high == at_high
            group = (i * per + j) * 8 + (lane >> 4)
            coarse.append(
                jnp.where(on, jnp.broadcast_to((group >> 4).astype(F32), (32, 128)), 0.0)
            )
            fine.append(
                jnp.where(on, jnp.broadcast_to((group & 15).astype(F32), (32, 128)), 0.0)
            )
            lows.append(jnp.where(low == at_low, 1.0, 0.0))
        left = jnp.concatenate(
            [jnp.concatenate(coarse, 1), jnp.concatenate(fine, 1)], 0
        ).astype(BF16)
        right = jnp.concatenate(lows, 1).astype(BF16)
        return acc + lax.dot_general(
            left, right, (((1,), (1,)), ((), ())), preferred_element_type=F32
        )

    acc = lax.fori_loop(0, rows // per, step, jnp.zeros((64, 128), F32))
    out_ref[...] = (acc[:32] * 16.0 + acc[32:]).astype(jnp.int32)


def counts_body(corner_ref, base_ref, out_ref):
    lanes = corner_ref.shape[1]
    px = corner_ref[0:1, :] - base_ref[0]
    py = corner_ref[1:2, :] - base_ref[1]
    pz = corner_ref[2:3, :]
    z = lax.broadcasted_iota(jnp.int32, (32, lanes), 0)
    in_z = jnp.where((z >= pz) & (z < pz + PATCH), 1.0, 0.0)
    ones = jnp.ones((lanes, 128), BF16)

    def column(x, _):
        in_x = (px <= x) & (px > x - PATCH)
        parts = []
        for y in range(8):
            hit = jnp.where(in_x & (py <= y) & (py > y - PATCH), 1.0, 0.0)
            parts.append((hit * in_z).astype(BF16))
        cover = jnp.dot(jnp.concatenate(parts, 0), ones, preferred_element_type=F32)
        out_ref[pl.ds(pl.multiple_of(x * 256, 256), 256), :] = 1.0 / (cover + DATA_WEIGHT)
        return 0

    lax.fori_loop(0, 8, column, 0)


def load_patch(cells_ref, first):
    rows = []
    for a in range(PATCH):
        for b in range(PATCH):
            rows.append(cells_ref[pl.ds(first + (a * 16 + b) * 32, PATCH), :])
    return jnp.concatenate(rows, 0)


def gram_body(first_ref, own_ref, yb_ref, ya_ref, xb_ref, xa_ref, cells_ref, out_ref, diag_ref):
    cells_ref[pl.ds(0, 2048), :] = xb_ref[...].reshape(2048, 128).astype(F32)
    cells_ref[pl.ds(6144, 2048), :] = xa_ref[...].reshape(2048, 128).astype(F32)

    def fill(x, _):
        row = pl.multiple_of((x + 4) * 512, 512)
        cells_ref[pl.ds(row, 128), :] = yb_ref[x].reshape(128, 128).astype(F32)
        cells_ref[pl.ds(row + 128, 256), :] = own_ref[x].reshape(256, 128).astype(F32)
        cells_ref[pl.ds(row + 384, 128), :] = ya_ref[x].reshape(128, 128).astype(F32)
        return 0

    lax.fori_loop(0, 8, fill, 0)
    diag_ref[...] = jnp.zeros_like(diag_ref)
    masks = packed_masks()

    def patch(p, _):
        values = load_patch(cells_ref, first_ref[p]).astype(BF16)
        gram = lax.dot_general(values, values, (((0,), (0,)), ((), ())), preferred_element_type=F32)
        packed, rest = pack_symmetric(gram, masks)
        side = p // 32
        out_ref[pl.ds(side * (64 * 33) + p - side * 32, 64, stride=33), :] = packed
        diag_ref[pl.ds(p, 1), :] = jnp.sum(rest, axis=0, keepdims=True)
        return 0

    lax.fori_loop(0, 64, patch, 0, unroll=8)
    turned = diag_ref[...].T[64:]
    out_ref[pl.ds(32, 64, stride=33), :] = turned
    out_ref[pl.ds(64 * 33 + 32, 64, stride=33), :] = pltpu.roll(turned, 96, axis=1)


def group_sum_body(group_ref, rows_ref, out_ref, limbs_ref):
    def split(i, _):
        value = rows_ref[pl.ds(i * 33, 32), :]
        high = value.astype(BF16)
        row = pl.multiple_of(i * 32, 32)
        limbs_ref[pl.ds(row, 32), 0:128] = high
        limbs_ref[pl.ds(row, 32), 128:256] = (value - high.astype(F32)).astype(BF16)
        return 0

    lax.fori_loop(0, 128, split, 0, unroll=8)
    one = jnp.ones((128, 128), BF16)
    zero = jnp.zeros((128, 128), BF16)
    sub = lax.broadcasted_iota(jnp.int32, (128, 128), 0)
    sub16 = sub.astype(F32).astype(BF16)

    used = lax.broadcasted_iota(jnp.int32, (32, 128), 1) < 32
    diagonal = jnp.zeros((32, 128), F32)
    for c in range(4):
        part = jnp.where(used, rows_ref[pl.ds(32 + 33 * c, 32, stride=132), :], 0.0)
        diagonal = diagonal + (pltpu.roll(part, 32 * c, axis=1) if c else part)
    group = group_ref[...]
    owner, place = group >> 4, (group & 15).astype(F32).astype(BF16)
    left, right = [], []
    for t in range(32):
        value = jnp.where(sub == owner[t : t + 1, :], diagonal[t : t + 1, :], 0.0)
        high = value.astype(BF16)
        left.append(jnp.concatenate([high, (value - high.astype(F32)).astype(BF16)], 0))
        spot = jnp.broadcast_to(place[t : t + 1, :], (128, 128))
        right.append(jnp.where(sub16 == spot, one, zero))
    extra = lax.dot_general(
        jnp.concatenate(left, 1),
        jnp.concatenate(right, 1),
        (((1,), (1,)), ((), ())),
        preferred_element_type=F32,
    )
    out_ref[pl.ds(16, 128, stride=17), :] = extra[:128] + extra[128:]

    def chunk(i, _):
        local = group_ref[...] - i * 256
        local = jnp.where((local >= 0) & (local < 256), local, 512).astype(F32).astype(BF16)
        hot = []
        for t in range(32):
            entry = jnp.broadcast_to(local[t : t + 1, :], (128, 128))
            hot.append(
                jnp.concatenate(
                    [
                        jnp.where(sub16 == entry, one, zero),
                        jnp.where(sub16 + jnp.asarray(128, BF16) == entry, one, zero),
                    ],
                    0,
                )
            )
        total = jnp.dot(jnp.concatenate(hot, 1), limbs_ref[...], preferred_element_type=F32)
        total = total[:, :128] + total[:, 128:]
        for d in range(16):
            out_ref[pl.ds((i * 16 + d) * 17, 16), :] = total[d * 16 : d * 16 + 16]
        return 0

    lax.fori_loop(0, 8, chunk, 0)


def shrink_body(tau_ref, rows_ref, out_ref, sys_ref, stage_ref):
    per = 16
    row_id = lax.broadcasted_iota(jnp.int32, (128, 128), 0)
    lane_id = lax.broadcasted_iota(jnp.int32, (128, 128), 1)
    eye = jnp.where(row_id == lane_id, 1.0, 0.0)
    masks = packed_masks()
    half = 64 * 17
    diagonals = rows_ref[pl.ds(16, 64, stride=17), :] + rows_ref[pl.ds(half + 16, 64, stride=17), :]
    diagonals = jnp.concatenate([jnp.zeros((64, 128), F32), diagonals], 0).T
    for g in range(per):
        packed = rows_ref[pl.ds(g, 64, stride=17), :] + rows_ref[pl.ds(half + g, 64, stride=17), :]
        sys_ref[g] = unpack_symmetric(packed, diagonals[g : g + 1], masks, F32) + tau_ref[g] * eye
    lane16 = lax.broadcasted_iota(jnp.int32, (NB, 128), 1)
    sub16 = lax.broadcasted_iota(jnp.int32, (NB, 128), 0)
    same = (row_id >> 4) == (lane_id >> 4)

    def block(b, _):
        start = pl.multiple_of(b * NB, NB)
        panels = [sys_ref[g, pl.ds(start, NB), :] for g in range(per)]
        pivots = []
        for h in range(2):
            joined = jnp.zeros((NB, 128), F32)
            for k in range(8):
                moved = pltpu.roll(panels[h * 8 + k], lax.rem(128 + k * NB - start, 128), axis=1)
                joined = jnp.where((lane16 >> 4) == k, moved, joined)
            pivots.append(joined)
        pivots = invert_blocks(jnp.concatenate(pivots, 0))
        in_block = (lane16 >= start) & (lane16 < start + NB)
        identity = jnp.where(lane16 - start == sub16, 1.0, 0.0)
        in_lanes = (lane_id >= start) & (lane_id < start + NB)
        in_rows = (row_id >= start) & (row_id < start + NB)
        scaled = []
        for h in range(2):
            left = jnp.where(same, jnp.concatenate([pivots[h * NB : (h + 1) * NB]] * 8, 0), 0.0)
            right = jnp.concatenate(
                [jnp.where(in_block, identity, panels[h * 8 + k]) for k in range(8)], 0
            )
            product = wide_product(left, right)
            scaled += [product[k * NB : (k + 1) * NB] for k in range(8)]
        for g in range(per):
            matrix = sys_ref[g]
            wide = jnp.where(in_rows, jnp.concatenate([scaled[g]] * (128 // NB), 0), 0.0)
            update = wide_product(matrix, wide)
            sys_ref[g] = jnp.where(in_rows, wide, jnp.where(in_lanes, 0.0, matrix) - update)
        return 0

    lax.fori_loop(0, 128 // NB, block, 0)
    extra = []
    for g in range(per):
        packed, rest = pack_symmetric(eye - tau_ref[g] * sys_ref[g], masks)
        stage_ref[pl.ds(g, 64, stride=18), :] = packed
        extra.append(jnp.sum(rest, axis=0, keepdims=True))
    extra = jnp.concatenate(extra + [jnp.zeros((128 - per, 128), F32)], 0)
    stage_ref[pl.ds(16, 64, stride=18), :] = extra.T[64:]
    stage_ref[pl.ds(17, 64, stride=18), :] = jnp.zeros((64, 128), F32)
    result = stage_ref[...].astype(BF16)
    out_ref[0:1152, :] = result
    out_ref[1152:2304, :] = result


def limbs(value):
    first = value.astype(BF16)
    rest = value - first.astype(F32)
    second = rest.astype(BF16)
    return first, second, (rest - second.astype(F32)).astype(BF16)


def wide_product(left, right):
    a0, a1, a2 = limbs(left)
    w0, w1, w2 = limbs(right)
    main = jnp.dot(
        jnp.concatenate([a0, a1], 1),
        jnp.concatenate([jnp.concatenate([w0, w0], 0), jnp.concatenate([w1, w1], 0)], 1),
        preferred_element_type=F32,
    )
    small = jnp.dot(
        jnp.concatenate([a0, a2], 1), jnp.concatenate([w2, w0], 0), preferred_element_type=F32
    )
    return main[:, :128] + (main[:, 128:] + small)


def invert_blocks(value):
    shape = value.shape
    lane = lax.broadcasted_iota(jnp.int32, shape, 1)
    sub = lax.broadcasted_iota(jnp.int32, shape, 0) & (NB - 1)
    within = lane & (NB - 1)
    segment = lane - within

    def spread(x, row):
        parts = [jnp.broadcast_to(x[h * NB + row : h * NB + row + 1], (NB, 128)) for h in range(2)]
        return jnp.concatenate(parts, 0)

    for j in range(0, NB, 2):
        c0 = jnp.take_along_axis(value, segment + j, axis=1, mode="promise_in_bounds")
        c1 = jnp.take_along_axis(value, segment + (j + 1), axis=1, mode="promise_in_bounds")
        at0, at1 = within == j, within == j + 1
        r0, r1 = spread(value, j), spread(value, j + 1)
        inverse = 1.0 / spread(c0, j)
        ratio = spread(c1, j) * inverse
        below = spread(c0, j + 1)
        s0 = jnp.where(at0, inverse, r0 * inverse)
        pivot = 1.0 / (spread(c1, j + 1) - below * ratio)
        rest = jnp.where(at0, 0.0, r1) - below * s0
        s1 = jnp.where(at1, pivot, rest * pivot)
        s0 = jnp.where(at1, 0.0, s0) - ratio * s1
        kept = jnp.where(at0 | at1, 0.0, value)
        c1 = c1 - c0 * ratio
        first = jnp.where(at0, inverse, jnp.where(at1, 0.0, r0 * inverse))
        value = jnp.where(
            sub == j, s0, jnp.where(sub == j + 1, s1, (kept - c0 * first) - c1 * s1)
        )
    return value


def expand_body(group_ref, rows_ref, out_ref, turned_ref, wide_ref, table_ref, stage_ref):
    turned_ref[...] = group_ref[...].astype(F32).T.astype(jnp.int32)
    wide_ref[...] = rows_ref[...].astype(F32)
    for j in range(4):

        def gather(d, _):
            value = wide_ref[pl.ds((d + 32 * j) * 18, 16), :].astype(BF16)
            table_ref[pl.ds(pl.multiple_of(d * 16, 16), 16), j * 128 : (j + 1) * 128] = value
            return 0

        lax.fori_loop(0, 32, gather, 0, unroll=8)
    extras = wide_ref[pl.ds(16, 128, stride=18), :].astype(BF16)
    lane = lax.broadcasted_iota(jnp.int32, (128, 128), 1)
    lane16 = lane.astype(F32).astype(BF16)
    zero = jnp.zeros((128, 128), BF16)
    one = jnp.ones((128, 128), BF16)
    eye = lax.broadcasted_iota(jnp.int32, (32, 128), 0) == lax.broadcasted_iota(
        jnp.int32, (32, 128), 1
    )
    stage_ref[pl.ds(33, 128, stride=34), :] = jnp.zeros((128, 128), F32)
    for u in range(8):
        groups, hot, owners = [], [], []
        for v in range(4):
            group = jnp.broadcast_to(turned_ref[:, u * 4 + v : u * 4 + v + 1], (128, 128))
            groups.append(group)
            low = jnp.where((group & 127).astype(F32).astype(BF16) == lane16, one, zero)
            high = ((group >> 7) & 3).astype(F32).astype(BF16)
            hot.append(
                jnp.concatenate(
                    [jnp.where(high == jnp.full((128, 128), c, BF16), low, zero) for c in range(4)],
                    1,
                )
            )
            owners.append(jnp.where((group >> 4).astype(F32).astype(BF16) == lane16, one, zero))
        wide = jnp.dot(jnp.concatenate(hot, 0), table_ref[...], preferred_element_type=F32)
        spots = jnp.dot(jnp.concatenate(owners, 0), extras, preferred_element_type=F32)
        for v in range(4):
            group = groups[v]
            rows = slice(v * 128, (v + 1) * 128)
            quarter = group >> 9
            piece = wide[rows, 384:512]
            for j in (2, 1, 0):
                piece = jnp.where(quarter == j, wide[rows, j * 128 : (j + 1) * 128], piece)
            spot = jnp.where(lane == (group & 15), spots[rows], 0.0)
            value = jnp.sum(spot, axis=1, keepdims=True)
            for k in range(4):
                row = ((u * 4 + v) * 4 + k) * 34
                part = slice(k * 32, k * 32 + 32)
                stage_ref[row : row + 32, :] = piece[part]
                stage_ref[row + 32 : row + 33, :] = jnp.sum(
                    jnp.where(eye, value[part], 0.0), axis=0, keepdims=True
                )
    out_ref[...] = stage_ref[...].astype(BF16)


def apply_body(
    first_ref,
    cells_ref,
    rows_ref,
    inner_ref,
    low_ref,
    high_ref,
    wide_ref,
    sum_ref,
    factor_ref,
    even_ref,
    odd_ref,
    diag_ref,
):
    wide_ref[...] = rows_ref[...].astype(F32)
    masks = packed_masks()
    used = lax.broadcasted_iota(jnp.int32, (64, 128), 1) < 32
    first_side = jnp.where(used, wide_ref[pl.ds(32, 64, stride=34), :], 0.0)
    last_side = jnp.where(used, wide_ref[pl.ds(64 * 34 + 32, 64, stride=34), :], 0.0)
    diagonals = first_side + pltpu.roll(last_side, 32, axis=1)
    diag_ref[...] = jnp.concatenate([jnp.zeros((64, 128), F32), diagonals], 0).T

    def unpack(p, _):
        side = p // 32
        packed = wide_ref[pl.ds(side * (64 * 34 - 32) + p, 64, stride=34), :]
        sum_ref[pl.ds(pl.multiple_of(p * 128, 128), 128), :] = jnp.zeros((128, 128), F32)
        factor_ref[p] = unpack_symmetric(packed, diag_ref[pl.ds(p, 1), :], masks, BF16)
        return 0

    lax.fori_loop(0, 64, unpack, 0, unroll=8)
    odd_ref[...] = jnp.zeros_like(odd_ref)
    count = 4

    def multiply(p, ref):
        for k in range(count):
            values = load_patch(cells_ref, first_ref[p + k]).astype(BF16)
            ref[k * 512 : (k + 1) * 512, :] = jnp.dot(
                values, factor_ref[p + k], preferred_element_type=F32
            )

    def accumulate(p, ref):
        for k in range(count):
            first = first_ref[p + k]
            for a in range(PATCH):
                for b in range(PATCH):
                    at = pl.ds(first + (a * 16 + b) * 32, PATCH)
                    row = k * 512 + (a * PATCH + b) * PATCH
                    sum_ref[at, :] += ref[row : row + PATCH, :]

    def several(i, _):
        p = i * (2 * count)
        multiply(p, even_ref)
        accumulate(jnp.maximum(p - count, 0), odd_ref)
        multiply(p + count, odd_ref)
        accumulate(p, even_ref)
        return 0

    lax.fori_loop(0, 64 // (2 * count), several, 0)
    accumulate(64 - count, odd_ref)
    low_ref[...] = sum_ref[0:2048, :].astype(BF16)
    inner_ref[...] = sum_ref[2048:6144, :]
    high_ref[...] = sum_ref[6144:8192, :].astype(BF16)


def exchange(rows, sublanes):
    shape = rows.shape
    rows = rows.reshape(128, shape[0] // (128 * sublanes), sublanes, 128)
    rows = lax.all_to_all(rows, BOTH, split_axis=0, concat_axis=0, tiled=True)
    return rows.reshape(shape)


def shards(estimate, dual, corners, members, thresholds):
    margin = PATCH // 2
    index_x = lax.axis_index("gx")
    index_y = lax.axis_index("gy")
    myself = index_x * 16 + index_y
    mixture = (estimate.astype(F32) + dual.astype(F32)).astype(BF16)

    yb, ya = neighbors(mixture, "gy", mixture[:, :margin], mixture[:, 8 - margin :])
    marked = corners + 1
    cb, ca = neighbors(marked, "gy", marked, marked)
    wide = jnp.concatenate([yb, mixture, ya], 1)
    xb, xa = neighbors(wide, "gx", wide[:margin], wide[8 - margin :])
    near = jnp.concatenate([cb, marked, ca], 1)
    nb, na = neighbors(near, "gx", near, near)
    near = jnp.concatenate([nb, near, na, jnp.zeros((3, 64), jnp.int32)], 1)
    near = jnp.where(near == 0, -1000, near - 1)

    side = (myself // 64).reshape(1)
    table = call(
        group_table_body,
        jax.ShapeDtypeStruct((32, 128), jnp.int32),
        side,
        members.reshape(256, 128),
        specs=[SMEM, VMEM],
        flops=2 * 128 * 32768 * 64,
        nbytes=1 << 17,
    )
    base = jnp.stack([index_x * 8, index_y * 8])
    inverse_counts = call(
        counts_body,
        jax.ShapeDtypeStruct((2048, 128), F32),
        near,
        base,
        specs=[VMEM, SMEM],
        flops=2 * 2048 * 640 * 128,
        nbytes=1 << 20,
    )

    begin_x = corners[0] - (index_x * 8 - margin)
    begin_y = corners[1] - (index_y * 8 - margin)
    first = (begin_x * 16 + begin_y) * 32 + corners[2]
    cells, grams = call(
        gram_body,
        (jax.ShapeDtypeStruct((8192, 128), F32), jax.ShapeDtypeStruct((128 * 33, 128), F32)),
        first,
        mixture,
        yb,
        ya,
        xb,
        xa,
        specs=[SMEM] + [VMEM] * 5,
        scratch=[pltpu.VMEM((128, 128), F32)],
        flops=2 * 64 * 512 * 128 * 128,
        nbytes=10 << 20,
    )
    rows = exchange(grams, 1)
    sums = call(
        group_sum_body,
        jax.ShapeDtypeStruct((128 * 17, 128), F32),
        table,
        rows,
        scratch=[pltpu.VMEM((4096, 256), BF16)],
        flops=2 * 2048 * 4096 * 256,
        nbytes=5 << 20,
    )
    mine = exchange(sums, 1)
    tau = lax.dynamic_slice_in_dim(thresholds, myself * 16, 16)
    factors = call(
        shrink_body,
        jax.ShapeDtypeStruct((128 * 18, 128), BF16),
        tau,
        mine,
        specs=[SMEM, VMEM],
        scratch=[pltpu.VMEM((16, 128, 128), F32), pltpu.VMEM((64 * 18, 128), F32)],
        flops=2 * 16 * 8 * 6 * 128**3,
        nbytes=2 << 20,
    )
    factor_rows = exchange(factors, 2)
    patch_rows = call(
        expand_body,
        jax.ShapeDtypeStruct((128 * 34, 128), BF16),
        table,
        factor_rows,
        scratch=[
            pltpu.VMEM((128, 32), jnp.int32),
            pltpu.VMEM((128 * 18, 128), F32),
            pltpu.VMEM((512, 512), BF16),
            pltpu.VMEM((128 * 34, 128), F32),
        ],
        flops=2 * 2048 * 4096 * 256,
        nbytes=3 << 20,
    )
    patch_factors = exchange(patch_rows, 2)
    edge = jax.ShapeDtypeStruct((2048, 128), BF16)
    inner, low, high = call(
        apply_body,
        (jax.ShapeDtypeStruct((4096, 128), F32), edge, edge),
        first,
        cells,
        patch_factors,
        specs=[SMEM, VMEM, VMEM],
        scratch=[
            pltpu.VMEM((128 * 34, 128), F32),
            pltpu.VMEM((8192, 128), F32),
            pltpu.VMEM((64, 128, 128), BF16),
            pltpu.VMEM((2048, 128), F32),
            pltpu.VMEM((2048, 128), F32),
            pltpu.VMEM((128, 128), F32),
        ],
        flops=2 * 64 * 512 * 128 * 128,
        nbytes=10 << 20,
    )
    inner = inner.reshape(8, 16, 32, 128)
    from_low, from_high = neighbors(
        inner, "gx", low.reshape(4, 16, 32, 128), high.reshape(4, 16, 32, 128)
    )
    inner = jnp.concatenate(
        [inner[:margin] + from_low.astype(F32), inner[margin:] + from_high.astype(F32)], 0
    )
    from_low, from_high = neighbors(
        inner, "gy", inner[:, :margin].astype(BF16), inner[:, 16 - margin :].astype(BF16)
    )
    sums = inner[:, margin : 16 - margin]
    sums = jnp.concatenate(
        [sums[:, :margin] + from_low.astype(F32), sums[:, margin:] + from_high.astype(F32)], 1
    )
    lowrank = (sums + DATA_WEIGHT * mixture.astype(F32)) * inverse_counts.reshape(8, 8, 32, 128)
    dual_next = dual.astype(F32) + estimate.astype(F32) - lowrank
    return lowrank, dual_next


def solution(mesh):
    in_specs = (
        P("gx", "gy", None, None),
        P("gx", "gy", None, None),
        P(None, ("gx", "gy")),
        P(),
        P(),
    )
    out_specs = (P("gx", "gy", None, None), P("gx", "gy", None, None))
    return jax.shard_map(shards, mesh=mesh, in_specs=in_specs, out_specs=out_specs, check_vma=False)
```

```python
import functools

import jax
import jax.numpy as jnp
from jax import lax
from jax.experimental import pallas as pl
from jax.experimental.pallas import tpu as pltpu
from jax.sharding import PartitionSpec as P

PATCH = 8
DATA_WEIGHT = 2.0
F32 = jnp.float32
BF16 = jnp.bfloat16
BOTH = ("gx", "gy")
NB = 16

VMEM = pl.BlockSpec(memory_space=pltpu.VMEM)
SMEM = pl.BlockSpec(memory_space=pltpu.SMEM)
PARAMS = pltpu.CompilerParams(vmem_limit_bytes=48 * 1024 * 1024)


def call(body, out_shape, *args, specs=None, scratch=(), flops=0, nbytes=0):
    outs = jax.tree.map(lambda _: VMEM, out_shape)
    return pl.pallas_call(
        body,
        out_shape=out_shape,
        in_specs=specs or [VMEM] * len(args),
        out_specs=outs,
        scratch_shapes=list(scratch),
        compiler_params=PARAMS,
        cost_estimate=pl.CostEstimate(flops=flops, bytes_accessed=nbytes, transcendentals=0),
    )(*args)


def neighbors(value, axis, first, last):
    size = lax.axis_size(axis)
    up = [(i, i + 1) for i in range(size - 1)]
    down = [(j, i) for i, j in up]
    before = lax.ppermute(last, axis, up)
    after = lax.ppermute(first, axis, down)
    return before, after


def packed_masks():
    row = lax.broadcasted_iota(jnp.int32, (64, 128), 0)
    lane = lax.broadcasted_iota(jnp.int32, (64, 128), 1)
    return (lane < 64) & (row > lane), row == lane, lane == row + 64


def pack_symmetric(matrix, masks):
    moved, _, low_diagonal = masks
    top, bottom = matrix[:64], matrix[64:]
    packed = jnp.where(moved, pltpu.roll(bottom, 64, axis=1), top)
    return packed, jnp.where(low_diagonal, bottom, 0.0)


def unpack_symmetric(packed, diagonal, masks, dtype):
    moved, top_diagonal, low_diagonal = masks
    top = jnp.where(moved, 0.0, jnp.where(top_diagonal, 0.5 * packed, packed))
    bottom = pltpu.roll(jnp.where(moved, packed, 0.0), 64, axis=1)
    bottom = bottom + jnp.where(low_diagonal, 0.5 * diagonal, 0.0)
    half = jnp.concatenate([top, bottom], 0).astype(dtype)
    return half + half.T


def group_table_body(side_ref, members_ref, out_ref):
    rows = members_ref.shape[0]
    per = 8
    high = lax.broadcasted_iota(jnp.int32, (32, 128), 0)
    low = lax.broadcasted_iota(jnp.int32, (128, 128), 0)
    lane = lax.broadcasted_iota(jnp.int32, (1, 128), 1)
    side = side_ref[0]

    def step(i, acc):
        block = members_ref[pl.ds(pl.multiple_of(i * per, per), per), :]
        coarse, fine, lows = [], [], []
        for j in range(per):
            entry = block[j : j + 1, :]
            at_high = jnp.where(((entry >> 5) & 1) == side, entry >> 8, -1)
            at_low = ((entry >> 6) & 3) * 32 + (entry & 31)
            on = high == at_high
            group = (i * per + j) * 8 + (lane >> 4)
            coarse.append(
                jnp.where(on, jnp.broadcast_to((group >> 4).astype(F32), (32, 128)), 0.0)
            )
            fine.append(
                jnp.where(on, jnp.broadcast_to((group & 15).astype(F32), (32, 128)), 0.0)
            )
            lows.append(jnp.where(low == at_low, 1.0, 0.0))
        left = jnp.concatenate(
            [jnp.concatenate(coarse, 1), jnp.concatenate(fine, 1)], 0
        ).astype(BF16)
        right = jnp.concatenate(lows, 1).astype(BF16)
        return acc + lax.dot_general(
            left, right, (((1,), (1,)), ((), ())), preferred_element_type=F32
        )

    acc = lax.fori_loop(0, rows // per, step, jnp.zeros((64, 128), F32))
    out_ref[...] = (acc[:32] * 16.0 + acc[32:]).astype(jnp.int32)


def counts_body(near_ref, base_ref, out_ref):
    code = jnp.concatenate([near_ref[m : m + 1, :] for m in range(5)], 1).astype(jnp.int32)
    lanes = code.shape[1]
    px = jnp.where(code < 0, -1000, code >> 12) - base_ref[0]
    py = ((code >> 5) & 127) - base_ref[1]
    pz = code & 31
    z = lax.broadcasted_iota(jnp.int32, (32, lanes), 0)
    in_z = jnp.where((z >= pz) & (z < pz + PATCH), 1.0, 0.0)
    ones = jnp.ones((lanes, 128), BF16)

    def column(x, _):
        in_x = (px <= x) & (px > x - PATCH)
        parts = []
        for y in range(8):
            hit = jnp.where(in_x & (py <= y) & (py > y - PATCH), 1.0, 0.0)
            parts.append((hit * in_z).astype(BF16))
        cover = jnp.dot(jnp.concatenate(parts, 0), ones, preferred_element_type=F32)
        out_ref[pl.ds(pl.multiple_of(x * 256, 256), 256), :] = 1.0 / (cover + DATA_WEIGHT)
        return 0

    lax.fori_loop(0, 8, column, 0)


def load_half(cells_ref, first):
    rows = []
    for a in range(PATCH // 2):
        for b in range(PATCH):
            rows.append(cells_ref[pl.ds(first + (a * 16 + b) * 32, PATCH), :])
    return jnp.concatenate(rows, 0).astype(BF16)


def half_gram(cells_ref, first):
    values = load_half(cells_ref, first)
    return lax.dot_general(values, values, (((0,), (0,)), ((), ())), preferred_element_type=F32)


def inner_gram_body(first_ref, own_ref, yb_ref, ya_ref, cells_ref, gram_ref):
    def fill(x, _):
        row = pl.multiple_of(x * 512, 512)
        cells_ref[pl.ds(row, 128), :] = yb_ref[x].reshape(128, 128).astype(F32)
        cells_ref[pl.ds(row + 128, 256), :] = own_ref[x].reshape(256, 128).astype(F32)
        cells_ref[pl.ds(row + 384, 128), :] = ya_ref[x].reshape(128, 128).astype(F32)
        return 0

    lax.fori_loop(0, 8, fill, 0)

    def patch(p, _):
        gram_ref[p] = half_gram(cells_ref, first_ref[p])
        return 0

    lax.fori_loop(0, 64, patch, 0, unroll=8)


def gram_body(
    first_ref, code_ref, inner_ref, xb_ref, xa_ref, half_ref, cells_ref, out_ref, diag_ref
):
    cells_ref[0:2048, :] = xb_ref[...].reshape(2048, 128).astype(F32)
    cells_ref[2048:6144, :] = inner_ref[...]
    cells_ref[6144:8192, :] = xa_ref[...].reshape(2048, 128).astype(F32)
    diag_ref[...] = jnp.zeros_like(diag_ref)
    masks = packed_masks()

    def patch(p, _):
        gram = half_ref[p] + half_gram(cells_ref, first_ref[p])
        packed, rest = pack_symmetric(gram, masks)
        out_ref[pl.ds((p // 32) * (64 * 33 - 32) + p, 64, stride=33), :] = packed
        diag_ref[pl.ds(p, 1), :] = jnp.sum(rest, axis=0, keepdims=True)
        return 0

    lax.fori_loop(0, 64, patch, 0, unroll=8)
    left = lax.broadcasted_iota(jnp.int32, (64, 128), 1) < 64
    turned = diag_ref[...].T[64:]
    out_ref[pl.ds(32, 64, stride=33), :] = jnp.where(left, turned, code_ref[...])
    out_ref[pl.ds(64 * 33 + 32, 64, stride=33), :] = jnp.where(
        left, pltpu.roll(turned, 96, axis=1), code_ref[...]
    )


def group_sum_body(near_id_ref, group_ref, rows_ref, out_ref, near_ref, limbs_ref):
    right_half = lax.broadcasted_iota(jnp.int32, (1, 128), 1) >= 64
    codes = []
    for n in range(10):
        code = jnp.full((1, 128), -1.0, F32)
        if n < 9:
            source = near_id_ref[n]
            row = rows_ref[pl.ds(jnp.maximum(source, 0) * 33 + 32, 1), :]
            code = jnp.where(source >= 0, row, code)
        codes.append(code)
    near_ref[...] = jnp.concatenate(
        [
            jnp.where(right_half, codes[2 * m], pltpu.roll(codes[2 * m + 1], 64, axis=1))
            for m in range(5)
        ]
        + [jnp.full((3, 128), -1.0, F32)],
        0,
    )

    def split(i, _):
        value = rows_ref[pl.ds(i * 33, 32), :]
        high = value.astype(BF16)
        row = pl.multiple_of(i * 32, 32)
        limbs_ref[pl.ds(row, 32), 0:128] = high
        limbs_ref[pl.ds(row, 32), 128:256] = (value - high.astype(F32)).astype(BF16)
        return 0

    lax.fori_loop(0, 128, split, 0, unroll=8)
    one = jnp.ones((128, 128), BF16)
    zero = jnp.zeros((128, 128), BF16)
    sub = lax.broadcasted_iota(jnp.int32, (128, 128), 0)
    sub16 = sub.astype(F32).astype(BF16)

    used = lax.broadcasted_iota(jnp.int32, (32, 128), 1) < 32
    diagonal = jnp.zeros((32, 128), F32)
    for c in range(4):
        part = jnp.where(used, rows_ref[pl.ds(32 + 33 * c, 32, stride=132), :], 0.0)
        diagonal = diagonal + (pltpu.roll(part, 32 * c, axis=1) if c else part)
    group = group_ref[...]
    owner, place = group >> 4, (group & 15).astype(F32).astype(BF16)
    left, right = [], []
    for t in range(32):
        value = jnp.where(sub == owner[t : t + 1, :], diagonal[t : t + 1, :], 0.0)
        high = value.astype(BF16)
        left.append(jnp.concatenate([high, (value - high.astype(F32)).astype(BF16)], 0))
        spot = jnp.broadcast_to(place[t : t + 1, :], (128, 128))
        right.append(jnp.where(sub16 == spot, one, zero))
    extra = lax.dot_general(
        jnp.concatenate(left, 1),
        jnp.concatenate(right, 1),
        (((1,), (1,)), ((), ())),
        preferred_element_type=F32,
    )
    out_ref[pl.ds(16, 128, stride=17), :] = extra[:128] + extra[128:]

    def chunk(i, _):
        local = group_ref[...] - i * 256
        local = jnp.where((local >= 0) & (local < 256), local, 512).astype(F32).astype(BF16)
        hot = []
        for t in range(32):
            entry = jnp.broadcast_to(local[t : t + 1, :], (128, 128))
            hot.append(
                jnp.concatenate(
                    [
                        jnp.where(sub16 == entry, one, zero),
                        jnp.where(sub16 + jnp.asarray(128, BF16) == entry, one, zero),
                    ],
                    0,
                )
            )
        total = jnp.dot(jnp.concatenate(hot, 1), limbs_ref[...], preferred_element_type=F32)
        total = total[:, :128] + total[:, 128:]
        for d in range(16):
            out_ref[pl.ds((i * 16 + d) * 17, 16), :] = total[d * 16 : d * 16 + 16]
        return 0

    lax.fori_loop(0, 8, chunk, 0)


def shrink_body(tau_ref, rows_ref, out_ref, sys_ref, stage_ref):
    per = 16
    row_id = lax.broadcasted_iota(jnp.int32, (128, 128), 0)
    lane_id = lax.broadcasted_iota(jnp.int32, (128, 128), 1)
    eye = jnp.where(row_id == lane_id, 1.0, 0.0)
    masks = packed_masks()
    half = 64 * 17
    diagonals = rows_ref[pl.ds(16, 64, stride=17), :] + rows_ref[pl.ds(half + 16, 64, stride=17), :]
    diagonals = jnp.concatenate([jnp.zeros((64, 128), F32), diagonals], 0).T
    for g in range(per):
        packed = rows_ref[pl.ds(g, 64, stride=17), :] + rows_ref[pl.ds(half + g, 64, stride=17), :]
        sys_ref[g] = unpack_symmetric(packed, diagonals[g : g + 1], masks, F32) + tau_ref[g] * eye
    lane16 = lax.broadcasted_iota(jnp.int32, (NB, 128), 1)
    sub16 = lax.broadcasted_iota(jnp.int32, (NB, 128), 0)
    same = (row_id >> 4) == (lane_id >> 4)
    segment = (lane_id >> 4).astype(F32).astype(BF16)
    first_lanes = segment < jnp.asarray(3, BF16)
    second_lanes = segment < jnp.asarray(5, BF16)

    def block(b, _):
        start = pl.multiple_of(b * NB, NB)
        panels = [sys_ref[g, pl.ds(start, NB), :] for g in range(per)]
        pivots = []
        for h in range(2):
            joined = jnp.zeros((NB, 128), F32)
            for k in range(8):
                moved = pltpu.roll(panels[h * 8 + k], lax.rem(128 + k * NB - start, 128), axis=1)
                joined = jnp.where((lane16 >> 4) == k, moved, joined)
            pivots.append(joined)
        pivots = invert_blocks(jnp.concatenate(pivots, 0))
        in_block = (lane16 >= start) & (lane16 < start + NB)
        identity = jnp.where(lane16 - start == sub16, 1.0, 0.0)
        in_lanes = (lane_id >= start) & (lane_id < start + NB)
        scaled = []
        for h in range(2):
            left = jnp.where(same, jnp.concatenate([pivots[h * NB : (h + 1) * NB]] * 8, 0), 0.0)
            right = jnp.concatenate(
                [jnp.where(in_block, identity, panels[h * 8 + k]) for k in range(8)], 0
            )
            product = wide_product(left, right)
            scaled += [product[k * NB : (k + 1) * NB] for k in range(8)]
        pick = start + (lane_id & (NB - 1))
        for g in range(per):
            matrix = sys_ref[g]
            columns = jnp.take_along_axis(matrix, pick, axis=1, mode="promise_in_bounds")
            c0, c1, c2 = limbs(columns)
            w0, w1, w2 = limbs(scaled[g])
            none = jnp.zeros_like(w0)
            update = jnp.dot(
                jnp.where(first_lanes, c0, jnp.where(second_lanes, c1, c2)),
                jnp.concatenate([w2, w1, w0, w1, w0, w0, none, none], 0),
                preferred_element_type=F32,
            )
            sys_ref[g] = jnp.where(in_lanes, 0.0, matrix) - update
        for g in range(per):
            sys_ref[g, pl.ds(start, NB), :] = scaled[g]
        return 0

    lax.fori_loop(0, 128 // NB, block, 0)
    extra = []
    for g in range(per):
        packed, rest = pack_symmetric(eye - tau_ref[g] * sys_ref[g], masks)
        stage_ref[pl.ds(g, 64, stride=18), :] = packed
        extra.append(jnp.sum(rest, axis=0, keepdims=True))
    extra = jnp.concatenate(extra + [jnp.zeros((128 - per, 128), F32)], 0)
    stage_ref[pl.ds(16, 64, stride=18), :] = extra.T[64:]
    stage_ref[pl.ds(17, 64, stride=18), :] = jnp.zeros((64, 128), F32)
    result = stage_ref[...].astype(BF16)
    out_ref[0:1152, :] = result
    out_ref[1152:2304, :] = result


def limbs(value):
    first = value.astype(BF16)
    rest = value - first.astype(F32)
    second = rest.astype(BF16)
    return first, second, (rest - second.astype(F32)).astype(BF16)


def wide_product(left, right):
    a0, a1, a2 = limbs(left)
    w0, w1, w2 = limbs(right)
    main = jnp.dot(
        jnp.concatenate([a0, a1], 1),
        jnp.concatenate([jnp.concatenate([w0, w0], 0), jnp.concatenate([w1, w1], 0)], 1),
        preferred_element_type=F32,
    )
    small = jnp.dot(
        jnp.concatenate([a0, a2], 1), jnp.concatenate([w2, w0], 0), preferred_element_type=F32
    )
    return main[:, :128] + (main[:, 128:] + small)


def invert_blocks(value):
    shape = value.shape
    lane = lax.broadcasted_iota(jnp.int32, shape, 1)
    sub = lax.broadcasted_iota(jnp.int32, shape, 0) & (NB - 1)
    within = lane & (NB - 1)
    segment = lane - within

    def spread(x, row):
        parts = [jnp.broadcast_to(x[h * NB + row : h * NB + row + 1], (NB, 128)) for h in range(2)]
        return jnp.concatenate(parts, 0)

    for j in range(0, NB, 2):
        c0 = jnp.take_along_axis(value, segment + j, axis=1, mode="promise_in_bounds")
        c1 = jnp.take_along_axis(value, segment + (j + 1), axis=1, mode="promise_in_bounds")
        at0, at1 = within == j, within == j + 1
        r0, r1 = spread(value, j), spread(value, j + 1)
        inverse = 1.0 / spread(c0, j)
        ratio = spread(c1, j) * inverse
        below = spread(c0, j + 1)
        s0 = jnp.where(at0, inverse, r0 * inverse)
        pivot = 1.0 / (spread(c1, j + 1) - below * ratio)
        rest = jnp.where(at0, 0.0, r1) - below * s0
        s1 = jnp.where(at1, pivot, rest * pivot)
        s0 = jnp.where(at1, 0.0, s0) - ratio * s1
        kept = jnp.where(at0 | at1, 0.0, value)
        c1 = c1 - c0 * ratio
        first = jnp.where(at0, inverse, jnp.where(at1, 0.0, r0 * inverse))
        value = jnp.where(
            sub == j, s0, jnp.where(sub == j + 1, s1, (kept - c0 * first) - c1 * s1)
        )
    return value


def expand_body(group_ref, rows_ref, out_ref, turned_ref, wide_ref, table_ref, stage_ref):
    turned_ref[...] = group_ref[...].astype(F32).T.astype(jnp.int32)
    wide_ref[...] = rows_ref[...].astype(F32)
    for j in range(4):

        def gather(d, _):
            value = wide_ref[pl.ds((d + 32 * j) * 18, 16), :].astype(BF16)
            table_ref[pl.ds(pl.multiple_of(d * 16, 16), 16), j * 128 : (j + 1) * 128] = value
            return 0

        lax.fori_loop(0, 32, gather, 0, unroll=8)
    extras = wide_ref[pl.ds(16, 128, stride=18), :].astype(BF16)
    lane = lax.broadcasted_iota(jnp.int32, (128, 128), 1)
    lane16 = lane.astype(F32).astype(BF16)
    zero = jnp.zeros((128, 128), BF16)
    one = jnp.ones((128, 128), BF16)
    eye = lax.broadcasted_iota(jnp.int32, (32, 128), 0) == lax.broadcasted_iota(
        jnp.int32, (32, 128), 1
    )
    stage_ref[pl.ds(33, 128, stride=34), :] = jnp.zeros((128, 128), F32)
    for u in range(8):
        groups, hot, owners = [], [], []
        for v in range(4):
            group = jnp.broadcast_to(turned_ref[:, u * 4 + v : u * 4 + v + 1], (128, 128))
            groups.append(group)
            low = jnp.where((group & 127).astype(F32).astype(BF16) == lane16, one, zero)
            high = ((group >> 7) & 3).astype(F32).astype(BF16)
            hot.append(
                jnp.concatenate(
                    [jnp.where(high == jnp.full((128, 128), c, BF16), low, zero) for c in range(4)],
                    1,
                )
            )
            owners.append(jnp.where((group >> 4).astype(F32).astype(BF16) == lane16, one, zero))
        wide = jnp.dot(jnp.concatenate(hot, 0), table_ref[...], preferred_element_type=F32)
        spots = jnp.dot(jnp.concatenate(owners, 0), extras, preferred_element_type=F32)
        for v in range(4):
            group = groups[v]
            rows = slice(v * 128, (v + 1) * 128)
            quarter = group >> 9
            piece = wide[rows, 384:512]
            for j in (2, 1, 0):
                piece = jnp.where(quarter == j, wide[rows, j * 128 : (j + 1) * 128], piece)
            spot = jnp.where(lane == (group & 15), spots[rows], 0.0)
            value = jnp.sum(spot, axis=1, keepdims=True)
            for k in range(4):
                row = ((u * 4 + v) * 4 + k) * 34
                part = slice(k * 32, k * 32 + 32)
                stage_ref[row : row + 32, :] = piece[part]
                stage_ref[row + 32 : row + 33, :] = jnp.sum(
                    jnp.where(eye, value[part], 0.0), axis=0, keepdims=True
                )
    out_ref[...] = stage_ref[...].astype(BF16)


def add_halves(first_ref, cells_ref, factor_ref, sum_ref, even_ref, odd_ref):
    odd_ref[...] = jnp.zeros_like(odd_ref)
    count = 4

    def multiply(p, ref):
        for k in range(count):
            values = load_half(cells_ref, first_ref[p + k])
            ref[k * 256 : (k + 1) * 256, :] = jnp.dot(
                values, factor_ref[p + k], preferred_element_type=F32
            )

    def accumulate(p, ref):
        for k in range(count):
            first = first_ref[p + k]
            for a in range(PATCH // 2):
                for b in range(PATCH):
                    at = pl.ds(first + (a * 16 + b) * 32, PATCH)
                    row = k * 256 + (a * PATCH + b) * PATCH
                    sum_ref[at, :] += ref[row : row + PATCH, :]

    def several(i, _):
        p = i * (2 * count)
        multiply(p, even_ref)
        accumulate(jnp.maximum(p - count, 0), odd_ref)
        multiply(p + count, odd_ref)
        accumulate(p, even_ref)
        return 0

    lax.fori_loop(0, 64 // (2 * count), several, 0)
    accumulate(64 - count, odd_ref)


def edge_apply_body(
    first_ref,
    cells_ref,
    rows_ref,
    inner_ref,
    low_ref,
    high_ref,
    factor_ref,
    wide_ref,
    sum_ref,
    even_ref,
    odd_ref,
    diag_ref,
):
    wide_ref[...] = rows_ref[...].astype(F32)
    masks = packed_masks()
    used = lax.broadcasted_iota(jnp.int32, (64, 128), 1) < 32
    first_side = jnp.where(used, wide_ref[pl.ds(32, 64, stride=34), :], 0.0)
    last_side = jnp.where(used, wide_ref[pl.ds(64 * 34 + 32, 64, stride=34), :], 0.0)
    diagonals = first_side + pltpu.roll(last_side, 32, axis=1)
    diag_ref[...] = jnp.concatenate([jnp.zeros((64, 128), F32), diagonals], 0).T

    def unpack(p, _):
        side = p // 32
        packed = wide_ref[pl.ds(side * (64 * 34 - 32) + p, 64, stride=34), :]
        sum_ref[pl.ds(pl.multiple_of(p * 128, 128), 128), :] = jnp.zeros((128, 128), F32)
        factor_ref[p] = unpack_symmetric(packed, diag_ref[pl.ds(p, 1), :], masks, BF16)
        return 0

    lax.fori_loop(0, 64, unpack, 0, unroll=8)
    add_halves(first_ref, cells_ref, factor_ref, sum_ref, even_ref, odd_ref)
    low_ref[...] = sum_ref[0:2048, :].astype(BF16)
    inner_ref[...] = sum_ref[2048:6144, :]
    high_ref[...] = sum_ref[6144:8192, :].astype(BF16)


def inner_apply_body(
    first_ref, cells_ref, factor_ref, start_ref, sum_ref, even_ref, odd_ref
):
    sum_ref[...] = start_ref[...]
    add_halves(first_ref, cells_ref, factor_ref, sum_ref, even_ref, odd_ref)


def exchange(rows, sublanes):
    shape = rows.shape
    rows = rows.reshape(128, shape[0] // (128 * sublanes), sublanes, 128)
    rows = lax.all_to_all(rows, BOTH, split_axis=0, concat_axis=0, tiled=True)
    return rows.reshape(shape)


def shards(estimate, dual, corners, members, thresholds):
    margin = PATCH // 2
    index_x = lax.axis_index("gx")
    index_y = lax.axis_index("gy")
    myself = index_x * 16 + index_y
    mixture = (estimate.astype(F32) + dual.astype(F32)).astype(BF16)

    begin_x = corners[0] - (index_x * 8 - margin)
    begin_y = corners[1] - (index_y * 8 - margin)
    first = (begin_x * 16 + begin_y) * 32 + corners[2]
    low_half = begin_x <= margin
    first_edge = first + jnp.where(low_half, 0, 2048)
    first_inner = first + jnp.where(low_half, 0, -2048)
    code = ((corners[0] * 128 + corners[1]) * 32 + corners[2]).astype(F32)
    code = jnp.concatenate([jnp.zeros((64,), F32), code]).reshape(1, 128)

    yb, ya = neighbors(mixture, "gy", mixture[:, :margin], mixture[:, 8 - margin :])
    inner_cells, half_grams = call(
        inner_gram_body,
        (jax.ShapeDtypeStruct((4096, 128), F32), jax.ShapeDtypeStruct((64, 128, 128), F32)),
        first_inner,
        mixture,
        yb,
        ya,
        specs=[SMEM] + [VMEM] * 3,
        flops=2 * 64 * 256 * 128 * 128,
        nbytes=8 << 20,
    )
    wide = jnp.concatenate(
        [
            jnp.concatenate([yb[:margin], mixture[:margin], ya[:margin]], 1),
            jnp.concatenate([yb[margin:], mixture[margin:], ya[margin:]], 1),
        ],
        0,
    )
    xb, xa = neighbors(wide, "gx", wide[:margin], wide[8 - margin :])
    side = (myself // 64).reshape(1)
    table = call(
        group_table_body,
        jax.ShapeDtypeStruct((32, 128), jnp.int32),
        side,
        members.reshape(256, 128),
        specs=[SMEM, VMEM],
        flops=2 * 128 * 32768 * 64,
        nbytes=1 << 17,
    )
    base = jnp.stack([index_x * 8, index_y * 8])
    cells, grams = call(
        gram_body,
        (jax.ShapeDtypeStruct((8192, 128), F32), jax.ShapeDtypeStruct((128 * 33, 128), F32)),
        first_edge,
        code,
        inner_cells,
        xb,
        xa,
        half_grams,
        specs=[SMEM] + [VMEM] * 5,
        scratch=[pltpu.VMEM((128, 128), F32)],
        flops=2 * 64 * 256 * 128 * 128,
        nbytes=10 << 20,
    )
    rows = exchange(grams, 1)
    offset = jnp.arange(9, dtype=jnp.int32)
    near_x = index_x + offset // 3 - 1
    near_y = index_y + offset % 3 - 1
    exists = (near_x >= 0) & (near_x < 8) & (near_y >= 0) & (near_y < 16)
    sums, near = call(
        group_sum_body,
        (jax.ShapeDtypeStruct((128 * 17, 128), F32), jax.ShapeDtypeStruct((8, 128), F32)),
        jnp.where(exists, near_x * 16 + near_y, -1),
        table,
        rows,
        specs=[SMEM, VMEM, VMEM],
        scratch=[pltpu.VMEM((4096, 256), BF16)],
        flops=2 * 2048 * 4096 * 256,
        nbytes=5 << 20,
    )
    inverse_counts = call(
        counts_body,
        jax.ShapeDtypeStruct((2048, 128), F32),
        near,
        base,
        specs=[VMEM, SMEM],
        flops=2 * 2048 * 640 * 128,
        nbytes=1 << 20,
    )
    mine = exchange(sums, 1)
    tau = lax.dynamic_slice_in_dim(thresholds, myself * 16, 16)
    factors = call(
        shrink_body,
        jax.ShapeDtypeStruct((128 * 18, 128), BF16),
        tau,
        mine,
        specs=[SMEM, VMEM],
        scratch=[pltpu.VMEM((16, 128, 128), F32), pltpu.VMEM((64 * 18, 128), F32)],
        flops=2 * 16 * 8 * 6 * 128**3,
        nbytes=2 << 20,
    )
    factor_rows = exchange(factors, 2)
    patch_rows = call(
        expand_body,
        jax.ShapeDtypeStruct((128 * 34, 128), BF16),
        table,
        factor_rows,
        scratch=[
            pltpu.VMEM((128, 32), jnp.int32),
            pltpu.VMEM((128 * 18, 128), F32),
            pltpu.VMEM((512, 512), BF16),
            pltpu.VMEM((128 * 34, 128), F32),
        ],
        flops=2 * 2048 * 4096 * 256,
        nbytes=3 << 20,
    )
    patch_factors = exchange(patch_rows, 2)
    edge = jax.ShapeDtypeStruct((2048, 128), BF16)
    half_result = pltpu.VMEM((1024, 128), F32)
    partial, low, high, patch_factors = call(
        edge_apply_body,
        (
            jax.ShapeDtypeStruct((4096, 128), F32),
            edge,
            edge,
            jax.ShapeDtypeStruct((64, 128, 128), BF16),
        ),
        first_edge,
        cells,
        patch_factors,
        specs=[SMEM, VMEM, VMEM],
        scratch=[
            pltpu.VMEM((128 * 34, 128), F32),
            pltpu.VMEM((8192, 128), F32),
            half_result,
            half_result,
            pltpu.VMEM((128, 128), F32),
        ],
        flops=2 * 64 * 256 * 128 * 128,
        nbytes=10 << 20,
    )
    from_low, from_high = neighbors(
        partial, "gx", low.reshape(4, 16, 32, 128), high.reshape(4, 16, 32, 128)
    )
    inner = call(
        inner_apply_body,
        jax.ShapeDtypeStruct((4096, 128), F32),
        first_inner,
        inner_cells,
        patch_factors,
        partial,
        specs=[SMEM, VMEM, VMEM, VMEM],
        scratch=[half_result, half_result],
        flops=2 * 64 * 256 * 128 * 128,
        nbytes=8 << 20,
    )
    inner = inner.reshape(8, 16, 32, 128)
    inner = jnp.concatenate(
        [inner[:margin] + from_low.astype(F32), inner[margin:] + from_high.astype(F32)], 0
    )
    from_low, from_high = neighbors(
        inner, "gy", inner[:, :margin].astype(BF16), inner[:, 16 - margin :].astype(BF16)
    )
    sums = inner[:, margin : 16 - margin]
    sums = jnp.concatenate(
        [sums[:, :margin] + from_low.astype(F32), sums[:, margin:] + from_high.astype(F32)], 1
    )
    lowrank = (sums + DATA_WEIGHT * mixture.astype(F32)) * inverse_counts.reshape(8, 8, 32, 128)
    dual_next = dual.astype(F32) + estimate.astype(F32) - lowrank
    return lowrank, dual_next


def solution(mesh):
    in_specs = (
        P("gx", "gy", None, None),
        P("gx", "gy", None, None),
        P(None, ("gx", "gy")),
        P(),
        P(),
    )
    out_specs = (P("gx", "gy", None, None), P("gx", "gy", None, None))
    return jax.shard_map(shards, mesh=mesh, in_specs=in_specs, out_specs=out_specs, check_vma=False)
```

```python
import functools

import jax
import jax.numpy as jnp
from jax import lax
from jax.experimental import pallas as pl
from jax.experimental.pallas import tpu as pltpu
from jax.sharding import PartitionSpec as P

PATCH = 8
DATA_WEIGHT = 2.0
F32 = jnp.float32
BF16 = jnp.bfloat16
BOTH = ("gx", "gy")
NB = 16

VMEM = pl.BlockSpec(memory_space=pltpu.VMEM)
SMEM = pl.BlockSpec(memory_space=pltpu.SMEM)
PARAMS = pltpu.CompilerParams(vmem_limit_bytes=20 * 1024 * 1024)


def call(body, out_shape, *args, specs=None, scratch=(), flops=0, nbytes=0):
    outs = jax.tree.map(lambda _: VMEM, out_shape)
    return pl.pallas_call(
        body,
        out_shape=out_shape,
        in_specs=specs or [VMEM] * len(args),
        out_specs=outs,
        scratch_shapes=list(scratch),
        compiler_params=PARAMS,
        cost_estimate=pl.CostEstimate(flops=flops, bytes_accessed=nbytes, transcendentals=0),
    )(*args)


def neighbors(value, axis, first, last):
    size = lax.axis_size(axis)
    up = [(i, i + 1) for i in range(size - 1)]
    down = [(j, i) for i, j in up]
    before = lax.ppermute(last, axis, up)
    after = lax.ppermute(first, axis, down)
    return before, after


def packed_masks():
    row = lax.broadcasted_iota(jnp.int32, (64, 128), 0)
    lane = lax.broadcasted_iota(jnp.int32, (64, 128), 1)
    return (lane < 64) & (row > lane), row == lane, lane == row + 64


def pack_symmetric(matrix, masks):
    moved, _, low_diagonal = masks
    top, bottom = matrix[:64], matrix[64:]
    packed = jnp.where(moved, pltpu.roll(bottom, 64, axis=1), top)
    return packed, jnp.where(low_diagonal, bottom, 0.0)


def unpack_symmetric(packed, diagonal, masks, dtype):
    moved, top_diagonal, low_diagonal = masks
    top = jnp.where(moved, 0.0, jnp.where(top_diagonal, 0.5 * packed, packed))
    bottom = pltpu.roll(jnp.where(moved, packed, 0.0), 64, axis=1)
    bottom = bottom + jnp.where(low_diagonal, 0.5 * diagonal, 0.0)
    half = jnp.concatenate([top, bottom], 0).astype(dtype)
    return half + half.T


def group_table_body(side_ref, members_ref, out_ref):
    groups = members_ref.shape[1]
    high = lax.broadcasted_iota(jnp.int32, (32, 128), 0)
    low = lax.broadcasted_iota(jnp.int32, (128, 128), 0)
    lane = lax.broadcasted_iota(jnp.int32, (1, 128), 1)
    side = side_ref[0]

    def step(i, acc):
        block = members_ref[:, pl.ds(pl.multiple_of(i * 128, 128), 128)]
        group = i * 128 + lane
        group_high = jnp.broadcast_to((group >> 4).astype(F32), (32, 128))
        group_low = jnp.broadcast_to((group & 15).astype(F32), (32, 128))
        coarse, fine, lows = [], [], []
        for j in range(16):
            entry = block[j : j + 1, :]
            at_high = jnp.where(((entry >> 5) & 1) == side, entry >> 8, -1)
            at_low = ((entry >> 6) & 3) * 32 + (entry & 31)
            on = high == at_high
            coarse.append(jnp.where(on, group_high, 0.0))
            fine.append(jnp.where(on, group_low, 0.0))
            lows.append(jnp.where(low == at_low, 1.0, 0.0))
        left = jnp.concatenate(
            [jnp.concatenate(coarse, 1), jnp.concatenate(fine, 1)], 0
        ).astype(BF16)
        right = jnp.concatenate(lows, 1).astype(BF16)
        return acc + lax.dot_general(
            left, right, (((1,), (1,)), ((), ())), preferred_element_type=F32
        )

    acc = lax.fori_loop(0, groups // 128, step, jnp.zeros((64, 128), F32))
    out_ref[...] = (acc[:32] * 16.0 + acc[32:]).astype(jnp.int32)


def counts_body(near_ref, base_ref, out_ref):
    code = jnp.concatenate([near_ref[m : m + 1, :] for m in range(5)], 1).astype(jnp.int32)
    lanes = code.shape[1]
    px = jnp.where(code < 0, -1000, code >> 12) - base_ref[0]
    py = ((code >> 5) & 127) - base_ref[1]
    pz = code & 31
    z = lax.broadcasted_iota(jnp.int32, (32, lanes), 0)
    in_z = jnp.where((z >= pz) & (z < pz + PATCH), 1.0, 0.0)
    ones = jnp.ones((lanes, 128), BF16)

    def column(x, _):
        in_x = (px <= x) & (px > x - PATCH)
        parts = []
        for y in range(8):
            hit = jnp.where(in_x & (py <= y) & (py > y - PATCH), 1.0, 0.0)
            parts.append((hit * in_z).astype(BF16))
        cover = jnp.dot(jnp.concatenate(parts, 0), ones, preferred_element_type=F32)
        out_ref[pl.ds(pl.multiple_of(x * 256, 256), 256), :] = 1.0 / (cover + DATA_WEIGHT)
        return 0

    lax.fori_loop(0, 8, column, 0)


def load_half(cells_ref, first):
    rows = []
    for a in range(PATCH // 2):
        for b in range(PATCH):
            rows.append(cells_ref[pl.ds(first + (a * 16 + b) * 32, PATCH), :])
    return jnp.concatenate(rows, 0).astype(BF16)


def half_gram(cells_ref, first):
    values = load_half(cells_ref, first)
    return lax.dot_general(values, values, (((0,), (0,)), ((), ())), preferred_element_type=F32)


def inner_gram_body(first_ref, own_ref, yb_ref, ya_ref, cells_ref, gram_ref):
    def fill(x, _):
        row = pl.multiple_of(x * 512, 512)
        cells_ref[pl.ds(row, 128), :] = yb_ref[x].reshape(128, 128).astype(F32)
        cells_ref[pl.ds(row + 128, 256), :] = own_ref[x].reshape(256, 128).astype(F32)
        cells_ref[pl.ds(row + 384, 128), :] = ya_ref[x].reshape(128, 128).astype(F32)
        return 0

    lax.fori_loop(0, 8, fill, 0)

    def patch(p, _):
        gram_ref[p] = half_gram(cells_ref, first_ref[p])
        return 0

    lax.fori_loop(0, 64, patch, 0, unroll=8)


def gram_body(
    first_ref, code_ref, inner_ref, xb_ref, xa_ref, half_ref, cells_ref, out_ref, diag_ref
):
    cells_ref[0:2048, :] = xb_ref[...].reshape(2048, 128).astype(F32)
    cells_ref[2048:6144, :] = inner_ref[...]
    cells_ref[6144:8192, :] = xa_ref[...].reshape(2048, 128).astype(F32)
    diag_ref[...] = jnp.zeros_like(diag_ref)
    masks = packed_masks()

    def patch(p, _):
        gram = half_ref[p] + half_gram(cells_ref, first_ref[p])
        packed, rest = pack_symmetric(gram, masks)
        out_ref[pl.ds((p // 32) * (64 * 33 - 32) + p, 64, stride=33), :] = packed
        diag_ref[pl.ds(p, 1), :] = jnp.sum(rest, axis=0, keepdims=True)
        return 0

    lax.fori_loop(0, 64, patch, 0, unroll=8)
    left = lax.broadcasted_iota(jnp.int32, (64, 128), 1) < 64
    turned = diag_ref[...].T[64:]
    out_ref[pl.ds(32, 64, stride=33), :] = jnp.where(left, turned, code_ref[...])
    out_ref[pl.ds(64 * 33 + 32, 64, stride=33), :] = jnp.where(
        left, pltpu.roll(turned, 96, axis=1), code_ref[...]
    )


def group_sum_body(near_id_ref, group_ref, rows_ref, out_ref, near_ref, limbs_ref):
    right_half = lax.broadcasted_iota(jnp.int32, (1, 128), 1) >= 64
    codes = []
    for n in range(10):
        code = jnp.full((1, 128), -1.0, F32)
        if n < 9:
            source = near_id_ref[n]
            row = rows_ref[pl.ds(jnp.maximum(source, 0) * 33 + 32, 1), :]
            code = jnp.where(source >= 0, row, code)
        codes.append(code)
    near_ref[...] = jnp.concatenate(
        [
            jnp.where(right_half, codes[2 * m], pltpu.roll(codes[2 * m + 1], 64, axis=1))
            for m in range(5)
        ]
        + [jnp.full((3, 128), -1.0, F32)],
        0,
    )

    def split(i, _):
        value = rows_ref[pl.ds(i * 33, 32), :]
        high = value.astype(BF16)
        row = pl.multiple_of(i * 32, 32)
        limbs_ref[pl.ds(row, 32), 0:128] = high
        limbs_ref[pl.ds(row, 32), 128:256] = (value - high.astype(F32)).astype(BF16)
        return 0

    lax.fori_loop(0, 128, split, 0, unroll=8)
    one = jnp.ones((128, 128), BF16)
    zero = jnp.zeros((128, 128), BF16)
    sub = lax.broadcasted_iota(jnp.int32, (128, 128), 0)
    sub16 = sub.astype(F32).astype(BF16)

    used = lax.broadcasted_iota(jnp.int32, (32, 128), 1) < 32
    diagonal = jnp.zeros((32, 128), F32)
    for c in range(4):
        part = jnp.where(used, rows_ref[pl.ds(32 + 33 * c, 32, stride=132), :], 0.0)
        diagonal = diagonal + (pltpu.roll(part, 32 * c, axis=1) if c else part)
    group = group_ref[...]
    owner, place = group >> 4, (group & 15).astype(F32).astype(BF16)
    left, right = [], []
    for t in range(32):
        value = jnp.where(sub == owner[t : t + 1, :], diagonal[t : t + 1, :], 0.0)
        high = value.astype(BF16)
        left.append(jnp.concatenate([high, (value - high.astype(F32)).astype(BF16)], 0))
        spot = jnp.broadcast_to(place[t : t + 1, :], (128, 128))
        right.append(jnp.where(sub16 == spot, one, zero))
    extra = lax.dot_general(
        jnp.concatenate(left, 1),
        jnp.concatenate(right, 1),
        (((1,), (1,)), ((), ())),
        preferred_element_type=F32,
    )
    out_ref[pl.ds(16, 128, stride=17), :] = extra[:128] + extra[128:]

    def chunk(i, _):
        local = group_ref[...] - i * 256
        local = jnp.where((local >= 0) & (local < 256), local, 512).astype(F32).astype(BF16)
        hot = []
        for t in range(32):
            entry = jnp.broadcast_to(local[t : t + 1, :], (128, 128))
            hot.append(
                jnp.concatenate(
                    [
                        jnp.where(sub16 == entry, one, zero),
                        jnp.where(sub16 + jnp.asarray(128, BF16) == entry, one, zero),
                    ],
                    0,
                )
            )
        total = jnp.dot(jnp.concatenate(hot, 1), limbs_ref[...], preferred_element_type=F32)
        total = total[:, :128] + total[:, 128:]
        for d in range(16):
            out_ref[pl.ds((i * 16 + d) * 17, 16), :] = total[d * 16 : d * 16 + 16]
        return 0

    lax.fori_loop(0, 8, chunk, 0)


def shrink_body(tau_ref, rows_ref, out_ref, sys_ref, stage_ref):
    per = 16
    row_id = lax.broadcasted_iota(jnp.int32, (128, 128), 0)
    lane_id = lax.broadcasted_iota(jnp.int32, (128, 128), 1)
    eye = jnp.where(row_id == lane_id, 1.0, 0.0)
    masks = packed_masks()
    half = 64 * 17
    diagonals = rows_ref[pl.ds(16, 64, stride=17), :] + rows_ref[pl.ds(half + 16, 64, stride=17), :]
    diagonals = jnp.concatenate([jnp.zeros((64, 128), F32), diagonals], 0).T
    for g in range(per):
        packed = rows_ref[pl.ds(g, 64, stride=17), :] + rows_ref[pl.ds(half + g, 64, stride=17), :]
        sys_ref[g] = unpack_symmetric(packed, diagonals[g : g + 1], masks, F32) + tau_ref[g] * eye
    lane16 = lax.broadcasted_iota(jnp.int32, (NB, 128), 1)
    sub16 = lax.broadcasted_iota(jnp.int32, (NB, 128), 0)
    same = (row_id >> 4) == (lane_id >> 4)
    segment = (lane_id >> 4).astype(F32).astype(BF16)
    first_lanes = segment < jnp.asarray(3, BF16)
    second_lanes = segment < jnp.asarray(5, BF16)

    def block(b, _):
        start = pl.multiple_of(b * NB, NB)
        panels = [sys_ref[g, pl.ds(start, NB), :] for g in range(per)]
        pivots = []
        for h in range(2):
            joined = jnp.zeros((NB, 128), F32)
            for k in range(8):
                moved = pltpu.roll(panels[h * 8 + k], lax.rem(128 + k * NB - start, 128), axis=1)
                joined = jnp.where((lane16 >> 4) == k, moved, joined)
            pivots.append(joined)
        pivots = invert_blocks(jnp.concatenate(pivots, 0))
        in_block = (lane16 >= start) & (lane16 < start + NB)
        identity = jnp.where(lane16 - start == sub16, 1.0, 0.0)
        in_lanes = (lane_id >= start) & (lane_id < start + NB)
        scaled = []
        for h in range(2):
            left = jnp.where(same, jnp.concatenate([pivots[h * NB : (h + 1) * NB]] * 8, 0), 0.0)
            right = jnp.concatenate(
                [jnp.where(in_block, identity, panels[h * 8 + k]) for k in range(8)], 0
            )
            product = wide_product(left, right)
            scaled += [product[k * NB : (k + 1) * NB] for k in range(8)]
        pick = start + (lane_id & (NB - 1))
        for g in range(per):
            matrix = sys_ref[g]
            columns = jnp.take_along_axis(matrix, pick, axis=1, mode="promise_in_bounds")
            c0, c1, c2 = limbs(columns)
            w0, w1, w2 = limbs(scaled[g])
            none = jnp.zeros_like(w0)
            update = jnp.dot(
                jnp.where(first_lanes, c0, jnp.where(second_lanes, c1, c2)),
                jnp.concatenate([w2, w1, w0, w1, w0, w0, none, none], 0),
                preferred_element_type=F32,
            )
            sys_ref[g] = jnp.where(in_lanes, 0.0, matrix) - update
        for g in range(per):
            sys_ref[g, pl.ds(start, NB), :] = scaled[g]
        return 0

    lax.fori_loop(0, 128 // NB, block, 0)
    extra = []
    for g in range(per):
        packed, rest = pack_symmetric(eye - tau_ref[g] * sys_ref[g], masks)
        stage_ref[pl.ds(g, 64, stride=18), :] = packed
        extra.append(jnp.sum(rest, axis=0, keepdims=True))
    extra = jnp.concatenate(extra + [jnp.zeros((128 - per, 128), F32)], 0)
    stage_ref[pl.ds(16, 64, stride=18), :] = extra.T[64:]
    stage_ref[pl.ds(17, 64, stride=18), :] = jnp.zeros((64, 128), F32)
    result = stage_ref[...].astype(BF16)
    out_ref[0:1152, :] = result
    out_ref[1152:2304, :] = result


def limbs(value):
    first = value.astype(BF16)
    rest = value - first.astype(F32)
    second = rest.astype(BF16)
    return first, second, (rest - second.astype(F32)).astype(BF16)


def wide_product(left, right):
    a0, a1, a2 = limbs(left)
    w0, w1, w2 = limbs(right)
    main = jnp.dot(
        jnp.concatenate([a0, a1], 1),
        jnp.concatenate([jnp.concatenate([w0, w0], 0), jnp.concatenate([w1, w1], 0)], 1),
        preferred_element_type=F32,
    )
    small = jnp.dot(
        jnp.concatenate([a0, a2], 1), jnp.concatenate([w2, w0], 0), preferred_element_type=F32
    )
    return main[:, :128] + (main[:, 128:] + small)


def invert_blocks(value):
    shape = value.shape
    lane = lax.broadcasted_iota(jnp.int32, shape, 1)
    sub = lax.broadcasted_iota(jnp.int32, shape, 0) & (NB - 1)
    within = lane & (NB - 1)
    segment = lane - within

    def spread(x, row):
        parts = [jnp.broadcast_to(x[h * NB + row : h * NB + row + 1], (NB, 128)) for h in range(2)]
        return jnp.concatenate(parts, 0)

    for j in range(0, NB, 2):
        c0 = jnp.take_along_axis(value, segment + j, axis=1, mode="promise_in_bounds")
        c1 = jnp.take_along_axis(value, segment + (j + 1), axis=1, mode="promise_in_bounds")
        at0, at1 = within == j, within == j + 1
        r0, r1 = spread(value, j), spread(value, j + 1)
        inverse = 1.0 / spread(c0, j)
        ratio = spread(c1, j) * inverse
        below = spread(c0, j + 1)
        s0 = jnp.where(at0, inverse, r0 * inverse)
        pivot = 1.0 / (spread(c1, j + 1) - below * ratio)
        rest = jnp.where(at0, 0.0, r1) - below * s0
        s1 = jnp.where(at1, pivot, rest * pivot)
        s0 = jnp.where(at1, 0.0, s0) - ratio * s1
        kept = jnp.where(at0 | at1, 0.0, value)
        c1 = c1 - c0 * ratio
        first = jnp.where(at0, inverse, jnp.where(at1, 0.0, r0 * inverse))
        value = jnp.where(
            sub == j, s0, jnp.where(sub == j + 1, s1, (kept - c0 * first) - c1 * s1)
        )
    return value


def expand_body(group_ref, rows_ref, out_ref, turned_ref, wide_ref, table_ref, stage_ref):
    turned_ref[...] = group_ref[...].astype(F32).T.astype(jnp.int32)
    wide_ref[...] = rows_ref[...].astype(F32)
    for j in range(4):

        def gather(d, _):
            value = wide_ref[pl.ds((d + 32 * j) * 18, 16), :].astype(BF16)
            table_ref[pl.ds(pl.multiple_of(d * 16, 16), 16), j * 128 : (j + 1) * 128] = value
            return 0

        lax.fori_loop(0, 32, gather, 0, unroll=8)
    extras = wide_ref[pl.ds(16, 128, stride=18), :].astype(BF16)
    lane = lax.broadcasted_iota(jnp.int32, (128, 128), 1)
    lane16 = lane.astype(F32).astype(BF16)
    zero = jnp.zeros((128, 128), BF16)
    one = jnp.ones((128, 128), BF16)
    eye = lax.broadcasted_iota(jnp.int32, (32, 128), 0) == lax.broadcasted_iota(
        jnp.int32, (32, 128), 1
    )
    stage_ref[pl.ds(33, 128, stride=34), :] = jnp.zeros((128, 128), F32)
    for u in range(8):
        groups, hot, owners = [], [], []
        for v in range(4):
            group = jnp.broadcast_to(turned_ref[:, u * 4 + v : u * 4 + v + 1], (128, 128))
            groups.append(group)
            low = jnp.where((group & 127).astype(F32).astype(BF16) == lane16, one, zero)
            high = ((group >> 7) & 3).astype(F32).astype(BF16)
            hot.append(
                jnp.concatenate(
                    [jnp.where(high == jnp.full((128, 128), c, BF16), low, zero) for c in range(4)],
                    1,
                )
            )
            owners.append(jnp.where((group >> 4).astype(F32).astype(BF16) == lane16, one, zero))
        wide = jnp.dot(jnp.concatenate(hot, 0), table_ref[...], preferred_element_type=F32)
        spots = jnp.dot(jnp.concatenate(owners, 0), extras, preferred_element_type=F32)
        for v in range(4):
            group = groups[v]
            rows = slice(v * 128, (v + 1) * 128)
            quarter = group >> 9
            piece = wide[rows, 384:512]
            for j in (2, 1, 0):
                piece = jnp.where(quarter == j, wide[rows, j * 128 : (j + 1) * 128], piece)
            spot = jnp.where(lane == (group & 15), spots[rows], 0.0)
            value = jnp.sum(spot, axis=1, keepdims=True)
            for k in range(4):
                row = ((u * 4 + v) * 4 + k) * 34
                part = slice(k * 32, k * 32 + 32)
                stage_ref[row : row + 32, :] = piece[part]
                stage_ref[row + 32 : row + 33, :] = jnp.sum(
                    jnp.where(eye, value[part], 0.0), axis=0, keepdims=True
                )
    out_ref[...] = stage_ref[...].astype(BF16)


def add_halves(first_ref, cells_ref, factor_ref, sum_ref, even_ref, odd_ref):
    odd_ref[...] = jnp.zeros_like(odd_ref)
    count = 4

    def multiply(p, ref):
        for k in range(count):
            values = load_half(cells_ref, first_ref[p + k])
            ref[k * 256 : (k + 1) * 256, :] = jnp.dot(
                values, factor_ref[p + k], preferred_element_type=F32
            )

    def accumulate(p, ref):
        for k in range(count):
            first = first_ref[p + k]
            for a in range(PATCH // 2):
                for b in range(PATCH):
                    at = pl.ds(first + (a * 16 + b) * 32, PATCH)
                    row = k * 256 + (a * PATCH + b) * PATCH
                    sum_ref[at, :] += ref[row : row + PATCH, :]

    def several(i, _):
        p = i * (2 * count)
        multiply(p, even_ref)
        accumulate(jnp.maximum(p - count, 0), odd_ref)
        multiply(p + count, odd_ref)
        accumulate(p, even_ref)
        return 0

    lax.fori_loop(0, 64 // (2 * count), several, 0)
    accumulate(64 - count, odd_ref)


def edge_apply_body(
    first_ref,
    cells_ref,
    rows_ref,
    inner_ref,
    low_ref,
    high_ref,
    factor_ref,
    wide_ref,
    sum_ref,
    even_ref,
    odd_ref,
    diag_ref,
):
    wide_ref[...] = rows_ref[...].astype(F32)
    masks = packed_masks()
    used = lax.broadcasted_iota(jnp.int32, (64, 128), 1) < 32
    first_side = jnp.where(used, wide_ref[pl.ds(32, 64, stride=34), :], 0.0)
    last_side = jnp.where(used, wide_ref[pl.ds(64 * 34 + 32, 64, stride=34), :], 0.0)
    diagonals = first_side + pltpu.roll(last_side, 32, axis=1)
    diag_ref[...] = jnp.concatenate([jnp.zeros((64, 128), F32), diagonals], 0).T

    def unpack(p, _):
        side = p // 32
        packed = wide_ref[pl.ds(side * (64 * 34 - 32) + p, 64, stride=34), :]
        sum_ref[pl.ds(pl.multiple_of(p * 128, 128), 128), :] = jnp.zeros((128, 128), F32)
        factor_ref[p] = unpack_symmetric(packed, diag_ref[pl.ds(p, 1), :], masks, BF16)
        return 0

    lax.fori_loop(0, 64, unpack, 0, unroll=8)
    add_halves(first_ref, cells_ref, factor_ref, sum_ref, even_ref, odd_ref)
    low_ref[...] = sum_ref[0:2048, :].astype(BF16)
    inner_ref[...] = sum_ref[2048:6144, :]
    high_ref[...] = sum_ref[6144:8192, :].astype(BF16)


def inner_apply_body(
    first_ref, cells_ref, factor_ref, start_ref, sum_ref, even_ref, odd_ref
):
    sum_ref[...] = start_ref[...]
    add_halves(first_ref, cells_ref, factor_ref, sum_ref, even_ref, odd_ref)


def exchange(rows, sublanes):
    shape = rows.shape
    rows = rows.reshape(128, shape[0] // (128 * sublanes), sublanes, 128)
    rows = lax.all_to_all(rows, BOTH, split_axis=0, concat_axis=0, tiled=True)
    return rows.reshape(shape)


def shards(estimate, dual, corners, members, thresholds):
    margin = PATCH // 2
    index_x = lax.axis_index("gx")
    index_y = lax.axis_index("gy")
    myself = index_x * 16 + index_y
    mixture = (estimate.astype(F32) + dual.astype(F32)).astype(BF16)

    begin_x = corners[0] - (index_x * 8 - margin)
    begin_y = corners[1] - (index_y * 8 - margin)
    first = (begin_x * 16 + begin_y) * 32 + corners[2]
    low_half = begin_x <= margin
    first_edge = first + jnp.where(low_half, 0, 2048)
    first_inner = first + jnp.where(low_half, 0, -2048)
    code = ((corners[0] * 128 + corners[1]) * 32 + corners[2]).astype(F32)
    code = jnp.concatenate([jnp.zeros((64,), F32), code]).reshape(1, 128)

    side = (myself // 64).reshape(1)
    table = call(
        group_table_body,
        jax.ShapeDtypeStruct((32, 128), jnp.int32),
        side,
        members.T,
        specs=[SMEM, VMEM],
        flops=2 * 128 * 32768 * 64,
        nbytes=1 << 17,
    )
    base = jnp.stack([index_x * 8, index_y * 8])
    offset = jnp.arange(9, dtype=jnp.int32)
    near_x = index_x + offset // 3 - 1
    near_y = index_y + offset % 3 - 1
    exists = (near_x >= 0) & (near_x < 8) & (near_y >= 0) & (near_y < 16)
    near_id = jnp.where(exists, near_x * 16 + near_y, -1)
    tau = lax.dynamic_slice_in_dim(thresholds, myself * 16, 16)
    held, code, table, near_id, tau, base = lax.optimization_barrier(
        (mixture, code, table, near_id, tau, base)
    )
    yb, ya = neighbors(mixture, "gy", mixture[:, :margin], mixture[:, 8 - margin :])
    inner_cells, half_grams = call(
        inner_gram_body,
        (jax.ShapeDtypeStruct((4096, 128), F32), jax.ShapeDtypeStruct((64, 128, 128), F32)),
        first_inner,
        mixture,
        yb,
        ya,
        specs=[SMEM] + [VMEM] * 3,
        flops=2 * 64 * 256 * 128 * 128,
        nbytes=8 << 20,
    )
    wide = jnp.concatenate(
        [
            jnp.concatenate([yb[:margin], held[:margin], ya[:margin]], 1),
            jnp.concatenate([yb[margin:], held[margin:], ya[margin:]], 1),
        ],
        0,
    )
    xb, xa = neighbors(wide, "gx", wide[:margin], wide[8 - margin :])
    cells, grams = call(
        gram_body,
        (jax.ShapeDtypeStruct((8192, 128), F32), jax.ShapeDtypeStruct((128 * 33, 128), F32)),
        first_edge,
        code,
        inner_cells,
        xb,
        xa,
        half_grams,
        specs=[SMEM] + [VMEM] * 5,
        scratch=[pltpu.VMEM((128, 128), F32)],
        flops=2 * 64 * 256 * 128 * 128,
        nbytes=10 << 20,
    )
    rows = exchange(grams, 1)
    sums, near = call(
        group_sum_body,
        (jax.ShapeDtypeStruct((128 * 17, 128), F32), jax.ShapeDtypeStruct((8, 128), F32)),
        near_id,
        table,
        rows,
        specs=[SMEM, VMEM, VMEM],
        scratch=[pltpu.VMEM((4096, 256), BF16)],
        flops=2 * 2048 * 4096 * 256,
        nbytes=5 << 20,
    )
    inverse_counts = call(
        counts_body,
        jax.ShapeDtypeStruct((2048, 128), F32),
        near,
        base,
        specs=[VMEM, SMEM],
        flops=2 * 2048 * 640 * 128,
        nbytes=1 << 20,
    )
    mine = exchange(sums, 1)
    factors = call(
        shrink_body,
        jax.ShapeDtypeStruct((128 * 18, 128), BF16),
        tau,
        mine,
        specs=[SMEM, VMEM],
        scratch=[pltpu.VMEM((16, 128, 128), F32), pltpu.VMEM((64 * 18, 128), F32)],
        flops=2 * 16 * 8 * 6 * 128**3,
        nbytes=2 << 20,
    )
    factor_rows = exchange(factors, 2)
    patch_rows = call(
        expand_body,
        jax.ShapeDtypeStruct((128 * 34, 128), BF16),
        table,
        factor_rows,
        scratch=[
            pltpu.VMEM((128, 32), jnp.int32),
            pltpu.VMEM((128 * 18, 128), F32),
            pltpu.VMEM((512, 512), BF16),
            pltpu.VMEM((128 * 34, 128), F32),
        ],
        flops=2 * 2048 * 4096 * 256,
        nbytes=3 << 20,
    )
    patch_factors = exchange(patch_rows, 2)
    edge = jax.ShapeDtypeStruct((2048, 128), BF16)
    half_result = pltpu.VMEM((1024, 128), F32)
    partial, low, high, patch_factors = call(
        edge_apply_body,
        (
            jax.ShapeDtypeStruct((4096, 128), F32),
            edge,
            edge,
            jax.ShapeDtypeStruct((64, 128, 128), BF16),
        ),
        first_edge,
        cells,
        patch_factors,
        specs=[SMEM, VMEM, VMEM],
        scratch=[
            pltpu.VMEM((128 * 34, 128), F32),
            pltpu.VMEM((8192, 128), F32),
            half_result,
            half_result,
            pltpu.VMEM((128, 128), F32),
        ],
        flops=2 * 64 * 256 * 128 * 128,
        nbytes=10 << 20,
    )
    from_low, from_high = neighbors(
        partial, "gx", low.reshape(4, 16, 32, 128), high.reshape(4, 16, 32, 128)
    )
    inner = call(
        inner_apply_body,
        jax.ShapeDtypeStruct((4096, 128), F32),
        first_inner,
        inner_cells,
        patch_factors,
        partial,
        specs=[SMEM, VMEM, VMEM, VMEM],
        scratch=[half_result, half_result],
        flops=2 * 64 * 256 * 128 * 128,
        nbytes=8 << 20,
    )
    inner = inner.reshape(8, 16, 32, 128)
    inner = jnp.concatenate(
        [inner[:margin] + from_low.astype(F32), inner[margin:] + from_high.astype(F32)], 0
    )
    from_low, from_high = neighbors(
        inner, "gy", inner[:, :margin].astype(BF16), inner[:, 16 - margin :].astype(BF16)
    )
    sums = inner[:, margin : 16 - margin]
    sums = jnp.concatenate(
        [sums[:, :margin] + from_low.astype(F32), sums[:, margin:] + from_high.astype(F32)], 1
    )
    lowrank = (sums + DATA_WEIGHT * mixture.astype(F32)) * inverse_counts.reshape(8, 8, 32, 128)
    dual_next = dual.astype(F32) + estimate.astype(F32) - lowrank
    return lowrank, dual_next


def solution(mesh):
    in_specs = (
        P("gx", "gy", None, None),
        P("gx", "gy", None, None),
        P(None, ("gx", "gy")),
        P(),
        P(),
    )
    out_specs = (P("gx", "gy", None, None), P("gx", "gy", None, None))
    return jax.shard_map(shards, mesh=mesh, in_specs=in_specs, out_specs=out_specs, check_vma=False)
```

```python
import functools

import jax
import jax.numpy as jnp
from jax import lax
from jax.experimental import pallas as pl
from jax.experimental.pallas import tpu as pltpu
from jax.sharding import PartitionSpec as P

PATCH = 8
DATA_WEIGHT = 2.0
F32 = jnp.float32
BF16 = jnp.bfloat16
BOTH = ("gx", "gy")
NB = 16

VMEM = pl.BlockSpec(memory_space=pltpu.VMEM)
SMEM = pl.BlockSpec(memory_space=pltpu.SMEM)
PARAMS = pltpu.CompilerParams(vmem_limit_bytes=20 * 1024 * 1024)


def call(body, out_shape, *args, specs=None, scratch=(), flops=0, nbytes=0):
    outs = jax.tree.map(lambda _: VMEM, out_shape)
    return pl.pallas_call(
        body,
        out_shape=out_shape,
        in_specs=specs or [VMEM] * len(args),
        out_specs=outs,
        scratch_shapes=list(scratch),
        compiler_params=PARAMS,
        cost_estimate=pl.CostEstimate(flops=flops, bytes_accessed=nbytes, transcendentals=0),
    )(*args)


def neighbors(value, axis, first, last):
    size = lax.axis_size(axis)
    up = [(i, i + 1) for i in range(size - 1)]
    down = [(j, i) for i, j in up]
    before = lax.ppermute(last, axis, up)
    after = lax.ppermute(first, axis, down)
    return before, after


def packed_masks():
    row = lax.broadcasted_iota(jnp.int32, (64, 128), 0)
    lane = lax.broadcasted_iota(jnp.int32, (64, 128), 1)
    return (lane < 64) & (row > lane), row == lane, lane == row + 64


def pack_symmetric(matrix, masks):
    moved, _, low_diagonal = masks
    top, bottom = matrix[:64], matrix[64:]
    packed = jnp.where(moved, pltpu.roll(bottom, 64, axis=1), top)
    return packed, jnp.where(low_diagonal, bottom, 0.0)


def unpack_symmetric(packed, diagonal, masks, dtype):
    moved, top_diagonal, low_diagonal = masks
    top = jnp.where(moved, 0.0, jnp.where(top_diagonal, 0.5 * packed, packed))
    bottom = pltpu.roll(jnp.where(moved, packed, 0.0), 64, axis=1)
    bottom = bottom + jnp.where(low_diagonal, 0.5 * diagonal, 0.0)
    half = jnp.concatenate([top, bottom], 0).astype(dtype)
    return half + half.T


def group_table_body(side_ref, members_ref, out_ref):
    groups = members_ref.shape[1]
    high = lax.broadcasted_iota(jnp.int32, (32, 128), 0)
    low = lax.broadcasted_iota(jnp.int32, (128, 128), 0)
    lane = lax.broadcasted_iota(jnp.int32, (1, 128), 1)
    side = side_ref[0]

    def step(i, acc):
        block = members_ref[:, pl.ds(pl.multiple_of(i * 128, 128), 128)]
        group = i * 128 + lane
        group_high = jnp.broadcast_to((group >> 4).astype(F32), (32, 128))
        group_low = jnp.broadcast_to((group & 15).astype(F32), (32, 128))
        coarse, fine, lows = [], [], []
        for j in range(16):
            entry = block[j : j + 1, :]
            at_high = jnp.where(((entry >> 5) & 1) == side, entry >> 8, -1)
            at_low = ((entry >> 6) & 3) * 32 + (entry & 31)
            on = high == at_high
            coarse.append(jnp.where(on, group_high, 0.0))
            fine.append(jnp.where(on, group_low, 0.0))
            lows.append(jnp.where(low == at_low, 1.0, 0.0))
        left = jnp.concatenate(
            [jnp.concatenate(coarse, 1), jnp.concatenate(fine, 1)], 0
        ).astype(BF16)
        right = jnp.concatenate(lows, 1).astype(BF16)
        return acc + lax.dot_general(
            left, right, (((1,), (1,)), ((), ())), preferred_element_type=F32
        )

    acc = lax.fori_loop(0, groups // 128, step, jnp.zeros((64, 128), F32))
    out_ref[...] = (acc[:32] * 16.0 + acc[32:]).astype(jnp.int32)


def counts_body(near_ref, base_ref, out_ref):
    code = jnp.concatenate([near_ref[m : m + 1, :] for m in range(5)], 1).astype(jnp.int32)
    lanes = code.shape[1]
    px = jnp.where(code < 0, -1000, code >> 12) - base_ref[0]
    py = ((code >> 5) & 127) - base_ref[1]
    pz = code & 31
    z = lax.broadcasted_iota(jnp.int32, (32, lanes), 0)
    in_z = jnp.where((z >= pz) & (z < pz + PATCH), 1.0, 0.0)
    ones = jnp.ones((lanes, 128), BF16)

    def column(x, _):
        in_x = (px <= x) & (px > x - PATCH)
        parts = []
        for y in range(8):
            hit = jnp.where(in_x & (py <= y) & (py > y - PATCH), 1.0, 0.0)
            parts.append((hit * in_z).astype(BF16))
        cover = jnp.dot(jnp.concatenate(parts, 0), ones, preferred_element_type=F32)
        out_ref[pl.ds(pl.multiple_of(x * 256, 256), 256), :] = 1.0 / (cover + DATA_WEIGHT)
        return 0

    lax.fori_loop(0, 8, column, 0)


def load_half(cells_ref, first):
    rows = []
    for a in range(PATCH // 2):
        for b in range(PATCH):
            rows.append(cells_ref[pl.ds(first + (a * 16 + b) * 32, PATCH), :])
    return jnp.concatenate(rows, 0).astype(BF16)


def half_gram(cells_ref, first):
    values = load_half(cells_ref, first)
    return lax.dot_general(values, values, (((0,), (0,)), ((), ())), preferred_element_type=F32)


def inner_gram_body(first_ref, own_ref, yb_ref, ya_ref, cells_ref, gram_ref):
    def fill(x, _):
        row = pl.multiple_of(x * 512, 512)
        cells_ref[pl.ds(row, 128), :] = yb_ref[x].reshape(128, 128).astype(F32)
        cells_ref[pl.ds(row + 128, 256), :] = own_ref[x].reshape(256, 128).astype(F32)
        cells_ref[pl.ds(row + 384, 128), :] = ya_ref[x].reshape(128, 128).astype(F32)
        return 0

    lax.fori_loop(0, 8, fill, 0)

    def patch(p, _):
        gram_ref[p] = half_gram(cells_ref, first_ref[p])
        return 0

    lax.fori_loop(0, 64, patch, 0, unroll=16)


def gram_body(
    first_ref, code_ref, inner_ref, xb_ref, xa_ref, half_ref, cells_ref, out_ref, diag_ref
):
    cells_ref[0:2048, :] = xb_ref[...].reshape(2048, 128).astype(F32)
    cells_ref[2048:6144, :] = inner_ref[...]
    cells_ref[6144:8192, :] = xa_ref[...].reshape(2048, 128).astype(F32)
    diag_ref[...] = jnp.zeros_like(diag_ref)
    masks = packed_masks()

    def patch(p, _):
        gram = half_ref[p] + half_gram(cells_ref, first_ref[p])
        packed, rest = pack_symmetric(gram, masks)
        out_ref[pl.ds((p // 32) * (64 * 33 - 32) + p, 64, stride=33), :] = packed
        diag_ref[pl.ds(p, 1), :] = jnp.sum(rest, axis=0, keepdims=True)
        return 0

    lax.fori_loop(0, 64, patch, 0, unroll=16)
    left = lax.broadcasted_iota(jnp.int32, (64, 128), 1) < 64
    turned = diag_ref[...].T[64:]
    out_ref[pl.ds(32, 64, stride=33), :] = jnp.where(left, turned, code_ref[...])
    out_ref[pl.ds(64 * 33 + 32, 64, stride=33), :] = jnp.where(
        left, pltpu.roll(turned, 96, axis=1), code_ref[...]
    )


def group_sum_body(near_id_ref, group_ref, rows_ref, out_ref, near_ref, limbs_ref):
    right_half = lax.broadcasted_iota(jnp.int32, (1, 128), 1) >= 64
    codes = []
    for n in range(10):
        code = jnp.full((1, 128), -1.0, F32)
        if n < 9:
            source = near_id_ref[n]
            row = rows_ref[pl.ds(jnp.maximum(source, 0) * 33 + 32, 1), :]
            code = jnp.where(source >= 0, row, code)
        codes.append(code)
    near_ref[...] = jnp.concatenate(
        [
            jnp.where(right_half, codes[2 * m], pltpu.roll(codes[2 * m + 1], 64, axis=1))
            for m in range(5)
        ]
        + [jnp.full((3, 128), -1.0, F32)],
        0,
    )

    def split(i, _):
        value = rows_ref[pl.ds(i * 33, 32), :]
        high = value.astype(BF16)
        row = pl.multiple_of(i * 32, 32)
        limbs_ref[pl.ds(row, 32), 0:128] = high
        limbs_ref[pl.ds(row, 32), 128:256] = (value - high.astype(F32)).astype(BF16)
        return 0

    lax.fori_loop(0, 128, split, 0, unroll=8)
    one = jnp.ones((128, 128), BF16)
    zero = jnp.zeros((128, 128), BF16)
    sub16 = lax.broadcasted_iota(jnp.int32, (128, 128), 0).astype(F32).astype(BF16)

    used = lax.broadcasted_iota(jnp.int32, (32, 128), 1) < 32
    diagonal = jnp.zeros((32, 128), F32)
    for c in range(4):
        part = jnp.where(used, rows_ref[pl.ds(32 + 33 * c, 32, stride=132), :], 0.0)
        diagonal = diagonal + (pltpu.roll(part, 32 * c, axis=1) if c else part)
    diagonal_high = diagonal.astype(BF16)
    diagonal_low = (diagonal - diagonal_high.astype(F32)).astype(BF16)
    group = group_ref[...]
    owner, place = (group >> 4).astype(F32).astype(BF16), (group & 15).astype(F32).astype(BF16)
    left, right = [], []

    def rows_of(x, t):
        return jnp.broadcast_to(x[t : t + 1, :], (128, 128))

    for t in range(32):
        on = sub16 == rows_of(owner, t)
        left.append(
            jnp.concatenate(
                [
                    jnp.where(on, rows_of(diagonal_high, t), zero),
                    jnp.where(on, rows_of(diagonal_low, t), zero),
                ],
                0,
            )
        )
        right.append(jnp.where(sub16 == rows_of(place, t), one, zero))
    extra = lax.dot_general(
        jnp.concatenate(left, 1),
        jnp.concatenate(right, 1),
        (((1,), (1,)), ((), ())),
        preferred_element_type=F32,
    )
    out_ref[pl.ds(16, 128, stride=17), :] = extra[:128] + extra[128:]

    def chunk(i, _):
        local = group_ref[...] - i * 256
        local = jnp.where((local >= 0) & (local < 256), local, 512).astype(F32).astype(BF16)
        hot = []
        for t in range(32):
            entry = jnp.broadcast_to(local[t : t + 1, :], (128, 128))
            hot.append(
                jnp.concatenate(
                    [
                        jnp.where(sub16 == entry, one, zero),
                        jnp.where(sub16 + jnp.asarray(128, BF16) == entry, one, zero),
                    ],
                    0,
                )
            )
        total = jnp.dot(jnp.concatenate(hot, 1), limbs_ref[...], preferred_element_type=F32)
        total = total[:, :128] + total[:, 128:]
        for d in range(16):
            out_ref[pl.ds((i * 16 + d) * 17, 16), :] = total[d * 16 : d * 16 + 16]
        return 0

    lax.fori_loop(0, 8, chunk, 0)


def shrink_body(tau_ref, rows_ref, out_ref, sys_ref, stage_ref):
    per = 16
    row_id = lax.broadcasted_iota(jnp.int32, (128, 128), 0)
    lane_id = lax.broadcasted_iota(jnp.int32, (128, 128), 1)
    eye = jnp.where(row_id == lane_id, 1.0, 0.0)
    masks = packed_masks()
    half = 64 * 17
    diagonals = rows_ref[pl.ds(16, 64, stride=17), :] + rows_ref[pl.ds(half + 16, 64, stride=17), :]
    diagonals = jnp.concatenate([jnp.zeros((64, 128), F32), diagonals], 0).T
    for g in range(per):
        packed = rows_ref[pl.ds(g, 64, stride=17), :] + rows_ref[pl.ds(half + g, 64, stride=17), :]
        sys_ref[g] = unpack_symmetric(packed, diagonals[g : g + 1], masks, F32) + tau_ref[g] * eye
    lane16 = lax.broadcasted_iota(jnp.int32, (NB, 128), 1)
    sub16 = lax.broadcasted_iota(jnp.int32, (NB, 128), 0)
    same = (row_id >> 4) == (lane_id >> 4)
    segment = (lane_id >> 4).astype(F32).astype(BF16)
    first_lanes = segment < jnp.asarray(3, BF16)
    second_lanes = segment < jnp.asarray(5, BF16)

    def block(b, _):
        start = pl.multiple_of(b * NB, NB)
        panels = [sys_ref[g, pl.ds(start, NB), :] for g in range(per)]
        pivots = []
        for h in range(2):
            joined = jnp.zeros((NB, 128), F32)
            for k in range(8):
                moved = pltpu.roll(panels[h * 8 + k], lax.rem(128 + k * NB - start, 128), axis=1)
                joined = jnp.where((lane16 >> 4) == k, moved, joined)
            pivots.append(joined)
        pivots = invert_blocks(jnp.concatenate(pivots, 0))
        in_block = (lane16 >= start) & (lane16 < start + NB)
        identity = jnp.where(lane16 - start == sub16, 1.0, 0.0)
        in_lanes = (lane_id >= start) & (lane_id < start + NB)
        scaled = []
        for h in range(2):
            left = jnp.where(same, jnp.concatenate([pivots[h * NB : (h + 1) * NB]] * 8, 0), 0.0)
            right = jnp.concatenate(
                [jnp.where(in_block, identity, panels[h * 8 + k]) for k in range(8)], 0
            )
            product = wide_product(left, right)
            scaled += [product[k * NB : (k + 1) * NB] for k in range(8)]
        pick = start + (lane_id & (NB - 1))
        for g in range(per):
            matrix = sys_ref[g]
            columns = jnp.take_along_axis(matrix, pick, axis=1, mode="promise_in_bounds")
            c0, c1, c2 = limbs(columns)
            w0, w1, w2 = limbs(scaled[g])
            none = jnp.zeros_like(w0)
            update = jnp.dot(
                jnp.where(first_lanes, c0, jnp.where(second_lanes, c1, c2)),
                jnp.concatenate([w2, w1, w0, w1, w0, w0, none, none], 0),
                preferred_element_type=F32,
            )
            sys_ref[g] = jnp.where(in_lanes, 0.0, matrix) - update
        for g in range(per):
            sys_ref[g, pl.ds(start, NB), :] = scaled[g]
        return 0

    lax.fori_loop(0, 128 // NB, block, 0)
    extra = []
    for g in range(per):
        packed, rest = pack_symmetric(eye - tau_ref[g] * sys_ref[g], masks)
        stage_ref[pl.ds(g, 64, stride=18), :] = packed
        extra.append(jnp.sum(rest, axis=0, keepdims=True))
    extra = jnp.concatenate(extra + [jnp.zeros((128 - per, 128), F32)], 0)
    stage_ref[pl.ds(16, 64, stride=18), :] = extra.T[64:]
    stage_ref[pl.ds(17, 64, stride=18), :] = jnp.zeros((64, 128), F32)
    result = stage_ref[...].astype(BF16)
    out_ref[0:1152, :] = result
    out_ref[1152:2304, :] = result


def limbs(value):
    first = value.astype(BF16)
    rest = value - first.astype(F32)
    second = rest.astype(BF16)
    return first, second, (rest - second.astype(F32)).astype(BF16)


def wide_product(left, right):
    a0, a1, a2 = limbs(left)
    w0, w1, w2 = limbs(right)
    main = jnp.dot(
        jnp.concatenate([a0, a1], 1),
        jnp.concatenate([jnp.concatenate([w0, w0], 0), jnp.concatenate([w1, w1], 0)], 1),
        preferred_element_type=F32,
    )
    small = jnp.dot(
        jnp.concatenate([a0, a2], 1), jnp.concatenate([w2, w0], 0), preferred_element_type=F32
    )
    return main[:, :128] + (main[:, 128:] + small)


def invert_blocks(value):
    shape = value.shape
    lane = lax.broadcasted_iota(jnp.int32, shape, 1)
    sub = lax.broadcasted_iota(jnp.int32, shape, 0) & (NB - 1)
    within = lane & (NB - 1)
    segment = lane - within

    def spread(x, row):
        parts = [jnp.broadcast_to(x[h * NB + row : h * NB + row + 1], (NB, 128)) for h in range(2)]
        return jnp.concatenate(parts, 0)

    for j in range(0, NB, 2):
        c0 = jnp.take_along_axis(value, segment + j, axis=1, mode="promise_in_bounds")
        c1 = jnp.take_along_axis(value, segment + (j + 1), axis=1, mode="promise_in_bounds")
        at0, at1 = within == j, within == j + 1
        r0, r1 = spread(value, j), spread(value, j + 1)
        inverse = 1.0 / spread(c0, j)
        ratio = spread(c1, j) * inverse
        below = spread(c0, j + 1)
        s0 = jnp.where(at0, inverse, r0 * inverse)
        pivot = 1.0 / (spread(c1, j + 1) - below * ratio)
        rest = jnp.where(at0, 0.0, r1) - below * s0
        s1 = jnp.where(at1, pivot, rest * pivot)
        s0 = jnp.where(at1, 0.0, s0) - ratio * s1
        kept = jnp.where(at0 | at1, 0.0, value)
        c1 = c1 - c0 * ratio
        first = jnp.where(at0, inverse, jnp.where(at1, 0.0, r0 * inverse))
        value = jnp.where(
            sub == j, s0, jnp.where(sub == j + 1, s1, (kept - c0 * first) - c1 * s1)
        )
    return value


def expand_body(group_ref, rows_ref, out_ref, turned_ref, wide_ref, table_ref, stage_ref):
    turned_ref[...] = group_ref[...].astype(F32).T.astype(jnp.int32)
    wide_ref[...] = rows_ref[...].astype(F32)
    for j in range(4):

        def gather(d, _):
            value = wide_ref[pl.ds((d + 32 * j) * 18, 16), :].astype(BF16)
            table_ref[pl.ds(pl.multiple_of(d * 16, 16), 16), j * 128 : (j + 1) * 128] = value
            return 0

        lax.fori_loop(0, 32, gather, 0, unroll=8)
    extras = wide_ref[pl.ds(16, 128, stride=18), :].astype(BF16)
    lane = lax.broadcasted_iota(jnp.int32, (128, 128), 1)
    lane16 = lane.astype(F32).astype(BF16)
    zero = jnp.zeros((128, 128), BF16)
    one = jnp.ones((128, 128), BF16)
    eye = lax.broadcasted_iota(jnp.int32, (32, 128), 0) == lax.broadcasted_iota(
        jnp.int32, (32, 128), 1
    )
    stage_ref[pl.ds(33, 128, stride=34), :] = jnp.zeros((128, 128), F32)
    for u in range(8):
        groups, hot, owners = [], [], []
        for v in range(4):
            group = jnp.broadcast_to(turned_ref[:, u * 4 + v : u * 4 + v + 1], (128, 128))
            groups.append(group)
            low = jnp.where((group & 127).astype(F32).astype(BF16) == lane16, one, zero)
            high = ((group >> 7) & 3).astype(F32).astype(BF16)
            hot.append(
                jnp.concatenate(
                    [jnp.where(high == jnp.full((128, 128), c, BF16), low, zero) for c in range(4)],
                    1,
                )
            )
            owners.append(jnp.where((group >> 4).astype(F32).astype(BF16) == lane16, one, zero))
        wide = jnp.dot(jnp.concatenate(hot, 0), table_ref[...], preferred_element_type=F32)
        spots = jnp.dot(jnp.concatenate(owners, 0), extras, preferred_element_type=F32)
        for v in range(4):
            group = groups[v]
            rows = slice(v * 128, (v + 1) * 128)
            quarter = group >> 9
            piece = wide[rows, 384:512]
            for j in (2, 1, 0):
                piece = jnp.where(quarter == j, wide[rows, j * 128 : (j + 1) * 128], piece)
            spot = jnp.where(lane == (group & 15), spots[rows], 0.0)
            value = jnp.sum(spot, axis=1, keepdims=True)
            for k in range(4):
                row = ((u * 4 + v) * 4 + k) * 34
                part = slice(k * 32, k * 32 + 32)
                stage_ref[row : row + 32, :] = piece[part]
                stage_ref[row + 32 : row + 33, :] = jnp.sum(
                    jnp.where(eye, value[part], 0.0), axis=0, keepdims=True
                )
    out_ref[...] = stage_ref[...].astype(BF16)


def add_halves(first_ref, cells_ref, factor_ref, sum_ref, even_ref, odd_ref):
    odd_ref[...] = jnp.zeros_like(odd_ref)
    count = 4

    def multiply(p, ref):
        for k in range(count):
            values = load_half(cells_ref, first_ref[p + k])
            ref[k * 256 : (k + 1) * 256, :] = jnp.dot(
                values, factor_ref[p + k], preferred_element_type=F32
            )

    def accumulate(p, ref):
        for k in range(count):
            first = first_ref[p + k]
            spots, sums = [], []
            for a in range(PATCH // 2):
                for b in range(PATCH):
                    at = pl.ds(first + (a * 16 + b) * 32, PATCH)
                    row = k * 256 + (a * PATCH + b) * PATCH
                    spots.append(at)
                    sums.append(sum_ref[at, :] + ref[row : row + PATCH, :])
            for at, value in zip(spots, sums):
                sum_ref[at, :] = value

    def several(i, _):
        p = i * (2 * count)
        multiply(p, even_ref)
        accumulate(jnp.maximum(p - count, 0), odd_ref)
        multiply(p + count, odd_ref)
        accumulate(p, even_ref)
        return 0

    lax.fori_loop(0, 64 // (2 * count), several, 0)
    accumulate(64 - count, odd_ref)


def edge_apply_body(
    first_ref,
    cells_ref,
    rows_ref,
    inner_ref,
    low_ref,
    high_ref,
    factor_ref,
    wide_ref,
    sum_ref,
    even_ref,
    odd_ref,
    diag_ref,
):
    wide_ref[...] = rows_ref[...].astype(F32)
    masks = packed_masks()
    used = lax.broadcasted_iota(jnp.int32, (64, 128), 1) < 32
    first_side = jnp.where(used, wide_ref[pl.ds(32, 64, stride=34), :], 0.0)
    last_side = jnp.where(used, wide_ref[pl.ds(64 * 34 + 32, 64, stride=34), :], 0.0)
    diagonals = first_side + pltpu.roll(last_side, 32, axis=1)
    diag_ref[...] = jnp.concatenate([jnp.zeros((64, 128), F32), diagonals], 0).T

    def unpack(p, _):
        side = p // 32
        packed = wide_ref[pl.ds(side * (64 * 34 - 32) + p, 64, stride=34), :]
        sum_ref[pl.ds(pl.multiple_of(p * 128, 128), 128), :] = jnp.zeros((128, 128), F32)
        factor_ref[p] = unpack_symmetric(packed, diag_ref[pl.ds(p, 1), :], masks, BF16)
        return 0

    lax.fori_loop(0, 64, unpack, 0, unroll=8)
    add_halves(first_ref, cells_ref, factor_ref, sum_ref, even_ref, odd_ref)
    low_ref[...] = sum_ref[0:2048, :].astype(BF16)
    inner_ref[...] = sum_ref[2048:6144, :]
    high_ref[...] = sum_ref[6144:8192, :].astype(BF16)


def inner_apply_body(
    first_ref, cells_ref, factor_ref, start_ref, sum_ref, even_ref, odd_ref
):
    sum_ref[...] = start_ref[...]
    add_halves(first_ref, cells_ref, factor_ref, sum_ref, even_ref, odd_ref)


def exchange(rows, sublanes):
    shape = rows.shape
    rows = rows.reshape(128, shape[0] // (128 * sublanes), sublanes, 128)
    rows = lax.all_to_all(rows, BOTH, split_axis=0, concat_axis=0, tiled=True)
    return rows.reshape(shape)


def shards(estimate, dual, corners, members, thresholds):
    margin = PATCH // 2
    index_x = lax.axis_index("gx")
    index_y = lax.axis_index("gy")
    myself = index_x * 16 + index_y
    mixture = (estimate.astype(F32) + dual.astype(F32)).astype(BF16)

    begin_x = corners[0] - (index_x * 8 - margin)
    begin_y = corners[1] - (index_y * 8 - margin)
    first = (begin_x * 16 + begin_y) * 32 + corners[2]
    low_half = begin_x <= margin
    first_edge = first + jnp.where(low_half, 0, 2048)
    first_inner = first + jnp.where(low_half, 0, -2048)
    code = ((corners[0] * 128 + corners[1]) * 32 + corners[2]).astype(F32)
    code = jnp.concatenate([jnp.zeros((64,), F32), code]).reshape(1, 128)

    side = (myself // 64).reshape(1)
    table = call(
        group_table_body,
        jax.ShapeDtypeStruct((32, 128), jnp.int32),
        side,
        members.T,
        specs=[SMEM, VMEM],
        flops=2 * 128 * 32768 * 64,
        nbytes=1 << 17,
    )
    base = jnp.stack([index_x * 8, index_y * 8])
    offset = jnp.arange(9, dtype=jnp.int32)
    near_x = index_x + offset // 3 - 1
    near_y = index_y + offset % 3 - 1
    exists = (near_x >= 0) & (near_x < 8) & (near_y >= 0) & (near_y < 16)
    near_id = jnp.where(exists, near_x * 16 + near_y, -1)
    tau = lax.dynamic_slice_in_dim(thresholds, myself * 16, 16)
    held, code, table, near_id, tau, base = lax.optimization_barrier(
        (mixture, code, table, near_id, tau, base)
    )
    yb, ya = neighbors(mixture, "gy", mixture[:, :margin], mixture[:, 8 - margin :])
    inner_cells, half_grams = call(
        inner_gram_body,
        (jax.ShapeDtypeStruct((4096, 128), F32), jax.ShapeDtypeStruct((64, 128, 128), F32)),
        first_inner,
        mixture,
        yb,
        ya,
        specs=[SMEM] + [VMEM] * 3,
        flops=2 * 64 * 256 * 128 * 128,
        nbytes=8 << 20,
    )
    wide = jnp.concatenate(
        [
            jnp.concatenate([yb[:margin], held[:margin], ya[:margin]], 1),
            jnp.concatenate([yb[margin:], held[margin:], ya[margin:]], 1),
        ],
        0,
    )
    xb, xa = neighbors(wide, "gx", wide[:margin], wide[8 - margin :])
    cells, grams = call(
        gram_body,
        (jax.ShapeDtypeStruct((8192, 128), F32), jax.ShapeDtypeStruct((128 * 33, 128), F32)),
        first_edge,
        code,
        inner_cells,
        xb,
        xa,
        half_grams,
        specs=[SMEM] + [VMEM] * 5,
        scratch=[pltpu.VMEM((128, 128), F32)],
        flops=2 * 64 * 256 * 128 * 128,
        nbytes=10 << 20,
    )
    rows = exchange(grams, 1)
    sums, near = call(
        group_sum_body,
        (jax.ShapeDtypeStruct((128 * 17, 128), F32), jax.ShapeDtypeStruct((8, 128), F32)),
        near_id,
        table,
        rows,
        specs=[SMEM, VMEM, VMEM],
        scratch=[pltpu.VMEM((4096, 256), BF16)],
        flops=2 * 2048 * 4096 * 256,
        nbytes=5 << 20,
    )
    inverse_counts = call(
        counts_body,
        jax.ShapeDtypeStruct((2048, 128), F32),
        near,
        base,
        specs=[VMEM, SMEM],
        flops=2 * 2048 * 640 * 128,
        nbytes=1 << 20,
    )
    mine = exchange(sums, 1)
    factors = call(
        shrink_body,
        jax.ShapeDtypeStruct((128 * 18, 128), BF16),
        tau,
        mine,
        specs=[SMEM, VMEM],
        scratch=[pltpu.VMEM((16, 128, 128), F32), pltpu.VMEM((64 * 18, 128), F32)],
        flops=2 * 16 * 8 * 6 * 128**3,
        nbytes=2 << 20,
    )
    factor_rows = exchange(factors, 2)
    patch_rows = call(
        expand_body,
        jax.ShapeDtypeStruct((128 * 34, 128), BF16),
        table,
        factor_rows,
        scratch=[
            pltpu.VMEM((128, 32), jnp.int32),
            pltpu.VMEM((128 * 18, 128), F32),
            pltpu.VMEM((512, 512), BF16),
            pltpu.VMEM((128 * 34, 128), F32),
        ],
        flops=2 * 2048 * 4096 * 256,
        nbytes=3 << 20,
    )
    patch_factors = exchange(patch_rows, 2)
    edge = jax.ShapeDtypeStruct((2048, 128), BF16)
    half_result = pltpu.VMEM((1024, 128), F32)
    partial, low, high, patch_factors = call(
        edge_apply_body,
        (
            jax.ShapeDtypeStruct((4096, 128), F32),
            edge,
            edge,
            jax.ShapeDtypeStruct((64, 128, 128), BF16),
        ),
        first_edge,
        cells,
        patch_factors,
        specs=[SMEM, VMEM, VMEM],
        scratch=[
            pltpu.VMEM((128 * 34, 128), F32),
            pltpu.VMEM((8192, 128), F32),
            half_result,
            half_result,
            pltpu.VMEM((128, 128), F32),
        ],
        flops=2 * 64 * 256 * 128 * 128,
        nbytes=10 << 20,
    )
    from_low, from_high = neighbors(
        partial, "gx", low.reshape(4, 16, 32, 128), high.reshape(4, 16, 32, 128)
    )
    inner = call(
        inner_apply_body,
        jax.ShapeDtypeStruct((4096, 128), F32),
        first_inner,
        inner_cells,
        patch_factors,
        partial,
        specs=[SMEM, VMEM, VMEM, VMEM],
        scratch=[half_result, half_result],
        flops=2 * 64 * 256 * 128 * 128,
        nbytes=8 << 20,
    )
    inner = inner.reshape(8, 16, 32, 128)
    inner = jnp.concatenate(
        [inner[:margin] + from_low.astype(F32), inner[margin:] + from_high.astype(F32)], 0
    )
    from_low, from_high = neighbors(
        inner, "gy", inner[:, :margin].astype(BF16), inner[:, 16 - margin :].astype(BF16)
    )
    sums = inner[:, margin : 16 - margin]
    sums = jnp.concatenate(
        [sums[:, :margin] + from_low.astype(F32), sums[:, margin:] + from_high.astype(F32)], 1
    )
    lowrank = (sums + DATA_WEIGHT * mixture.astype(F32)) * inverse_counts.reshape(8, 8, 32, 128)
    dual_next = dual.astype(F32) + estimate.astype(F32) - lowrank
    return lowrank, dual_next


def solution(mesh):
    in_specs = (
        P("gx", "gy", None, None),
        P("gx", "gy", None, None),
        P(None, ("gx", "gy")),
        P(),
        P(),
    )
    out_specs = (P("gx", "gy", None, None), P("gx", "gy", None, None))
    return jax.shard_map(shards, mesh=mesh, in_specs=in_specs, out_specs=out_specs, check_vma=False)
```

```python
import functools

import jax
import jax.numpy as jnp
from jax import lax
from jax.experimental import pallas as pl
from jax.experimental.pallas import tpu as pltpu
from jax.sharding import PartitionSpec as P

PATCH = 8
DATA_WEIGHT = 2.0
F32 = jnp.float32
BF16 = jnp.bfloat16
BOTH = ("gx", "gy")
NB = 16

VMEM = pl.BlockSpec(memory_space=pltpu.VMEM)
SMEM = pl.BlockSpec(memory_space=pltpu.SMEM)
PARAMS = pltpu.CompilerParams(vmem_limit_bytes=20 * 1024 * 1024)


def call(body, out_shape, *args, specs=None, scratch=(), flops=0, nbytes=0):
    outs = jax.tree.map(lambda _: VMEM, out_shape)
    return pl.pallas_call(
        body,
        out_shape=out_shape,
        in_specs=specs or [VMEM] * len(args),
        out_specs=outs,
        scratch_shapes=list(scratch),
        compiler_params=PARAMS,
        cost_estimate=pl.CostEstimate(flops=flops, bytes_accessed=nbytes, transcendentals=0),
    )(*args)


def neighbors(value, axis, first, last):
    size = lax.axis_size(axis)
    up = [(i, i + 1) for i in range(size - 1)]
    down = [(j, i) for i, j in up]
    before = lax.ppermute(last, axis, up)
    after = lax.ppermute(first, axis, down)
    return before, after


def packed_masks():
    row = lax.broadcasted_iota(jnp.int32, (64, 128), 0)
    lane = lax.broadcasted_iota(jnp.int32, (64, 128), 1)
    return (lane < 64) & (row > lane), row == lane, lane == row + 64


def pack_symmetric(matrix, masks):
    moved, _, low_diagonal = masks
    top, bottom = matrix[:64], matrix[64:]
    packed = jnp.where(moved, pltpu.roll(bottom, 64, axis=1), top)
    return packed, jnp.where(low_diagonal, bottom, 0.0)


def unpack_symmetric(packed, diagonal, masks, dtype):
    moved, top_diagonal, low_diagonal = masks
    top = jnp.where(moved, 0.0, jnp.where(top_diagonal, 0.5 * packed, packed))
    bottom = pltpu.roll(jnp.where(moved, packed, 0.0), 64, axis=1)
    bottom = bottom + jnp.where(low_diagonal, 0.5 * diagonal, 0.0)
    half = jnp.concatenate([top, bottom], 0).astype(dtype)
    return half + half.T


def group_table_body(side_ref, members_ref, out_ref):
    groups = members_ref.shape[1]
    high = lax.broadcasted_iota(jnp.int32, (32, 128), 0)
    low = lax.broadcasted_iota(jnp.int32, (128, 128), 0)
    lane = lax.broadcasted_iota(jnp.int32, (1, 128), 1)
    side = side_ref[0]

    def step(i, acc):
        block = members_ref[:, pl.ds(pl.multiple_of(i * 128, 128), 128)]
        group = i * 128 + lane
        group_high = jnp.broadcast_to((group >> 4).astype(F32), (32, 128))
        group_low = jnp.broadcast_to((group & 15).astype(F32), (32, 128))
        coarse, fine, lows = [], [], []
        for j in range(16):
            entry = block[j : j + 1, :]
            at_high = jnp.where(((entry >> 5) & 1) == side, entry >> 8, -1)
            at_low = ((entry >> 6) & 3) * 32 + (entry & 31)
            on = high == at_high
            coarse.append(jnp.where(on, group_high, 0.0))
            fine.append(jnp.where(on, group_low, 0.0))
            lows.append(jnp.where(low == at_low, 1.0, 0.0))
        left = jnp.concatenate(
            [jnp.concatenate(coarse, 1), jnp.concatenate(fine, 1)], 0
        ).astype(BF16)
        right = jnp.concatenate(lows, 1).astype(BF16)
        return acc + lax.dot_general(
            left, right, (((1,), (1,)), ((), ())), preferred_element_type=F32
        )

    acc = lax.fori_loop(0, groups // 128, step, jnp.zeros((64, 128), F32))
    out_ref[...] = (acc[:32] * 16.0 + acc[32:]).astype(jnp.int32)


def counts_body(near_ref, base_ref, out_ref):
    code = jnp.concatenate([near_ref[m : m + 1, :] for m in range(5)], 1).astype(jnp.int32)
    lanes = code.shape[1]
    px = jnp.where(code < 0, -1000, code >> 12) - base_ref[0]
    py = ((code >> 5) & 127) - base_ref[1]
    pz = code & 31
    z = lax.broadcasted_iota(jnp.int32, (32, lanes), 0)
    in_z = jnp.where((z >= pz) & (z < pz + PATCH), 1.0, 0.0).astype(BF16)
    ones = jnp.ones((lanes, 128), BF16)

    def column(x, _):
        in_x = (px <= x) & (px > x - PATCH)
        parts = []
        for y in range(8):
            hit = jnp.where(in_x & (py <= y) & (py > y - PATCH), 1.0, 0.0).astype(BF16)
            parts.append(jnp.broadcast_to(hit, in_z.shape) * in_z)
        cover = jnp.dot(jnp.concatenate(parts, 0), ones, preferred_element_type=F32)
        out_ref[pl.ds(pl.multiple_of(x * 256, 256), 256), :] = 1.0 / (cover + DATA_WEIGHT)
        return 0

    lax.fori_loop(0, 8, column, 0, unroll=4)


def load_half(cells_ref, first):
    rows = []
    for a in range(PATCH // 2):
        for b in range(PATCH):
            rows.append(cells_ref[pl.ds(first + (a * 16 + b) * 32, PATCH), :])
    return jnp.concatenate(rows, 0).astype(BF16)


def half_gram(cells_ref, first):
    values = load_half(cells_ref, first)
    return lax.dot_general(values, values, (((0,), (0,)), ((), ())), preferred_element_type=F32)


def inner_gram_body(first_ref, own_ref, yb_ref, ya_ref, cells_ref, gram_ref):
    def fill(x, _):
        row = pl.multiple_of(x * 512, 512)
        cells_ref[pl.ds(row, 128), :] = yb_ref[x].reshape(128, 128).astype(F32)
        cells_ref[pl.ds(row + 128, 256), :] = own_ref[x].reshape(256, 128).astype(F32)
        cells_ref[pl.ds(row + 384, 128), :] = ya_ref[x].reshape(128, 128).astype(F32)
        return 0

    lax.fori_loop(0, 8, fill, 0)

    def patch(p, _):
        gram_ref[p] = half_gram(cells_ref, first_ref[p])
        return 0

    lax.fori_loop(0, 64, patch, 0, unroll=16)


def gram_body(
    first_ref, code_ref, inner_ref, xb_ref, xa_ref, half_ref, cells_ref, out_ref, diag_ref
):
    cells_ref[0:2048, :] = xb_ref[...].reshape(2048, 128).astype(F32)
    cells_ref[2048:6144, :] = inner_ref[...]
    cells_ref[6144:8192, :] = xa_ref[...].reshape(2048, 128).astype(F32)
    diag_ref[...] = jnp.zeros_like(diag_ref)
    masks = packed_masks()

    def patch(p, _):
        gram = half_ref[p] + half_gram(cells_ref, first_ref[p])
        packed, rest = pack_symmetric(gram, masks)
        out_ref[pl.ds((p // 32) * (64 * 33 - 32) + p, 64, stride=33), :] = packed
        diag_ref[pl.ds(p, 1), :] = jnp.sum(rest, axis=0, keepdims=True)
        return 0

    lax.fori_loop(0, 64, patch, 0, unroll=16)
    left = lax.broadcasted_iota(jnp.int32, (64, 128), 1) < 64
    turned = diag_ref[...].T[64:]
    out_ref[pl.ds(32, 64, stride=33), :] = jnp.where(left, turned, code_ref[...])
    out_ref[pl.ds(64 * 33 + 32, 64, stride=33), :] = jnp.where(
        left, pltpu.roll(turned, 96, axis=1), code_ref[...]
    )


def group_sum_body(near_id_ref, group_ref, rows_ref, out_ref, near_ref, limbs_ref):
    right_half = lax.broadcasted_iota(jnp.int32, (1, 128), 1) >= 64
    codes = []
    for n in range(10):
        code = jnp.full((1, 128), -1.0, F32)
        if n < 9:
            source = near_id_ref[n]
            row = rows_ref[pl.ds(jnp.maximum(source, 0) * 33 + 32, 1), :]
            code = jnp.where(source >= 0, row, code)
        codes.append(code)
    near_ref[...] = jnp.concatenate(
        [
            jnp.where(right_half, codes[2 * m], pltpu.roll(codes[2 * m + 1], 64, axis=1))
            for m in range(5)
        ]
        + [jnp.full((3, 128), -1.0, F32)],
        0,
    )

    def split(i, _):
        value = rows_ref[pl.ds(i * 33, 32), :]
        high = value.astype(BF16)
        row = pl.multiple_of(i * 32, 32)
        limbs_ref[pl.ds(row, 32), 0:128] = high
        limbs_ref[pl.ds(row, 32), 128:256] = (value - high.astype(F32)).astype(BF16)
        return 0

    lax.fori_loop(0, 128, split, 0, unroll=8)
    one = jnp.ones((128, 128), BF16)
    zero = jnp.zeros((128, 128), BF16)
    sub16 = lax.broadcasted_iota(jnp.int32, (128, 128), 0).astype(F32).astype(BF16)

    used = lax.broadcasted_iota(jnp.int32, (32, 128), 1) < 32
    diagonal = jnp.zeros((32, 128), F32)
    for c in range(4):
        part = jnp.where(used, rows_ref[pl.ds(32 + 33 * c, 32, stride=132), :], 0.0)
        diagonal = diagonal + (pltpu.roll(part, 32 * c, axis=1) if c else part)
    diagonal_high = diagonal.astype(BF16)
    diagonal_low = (diagonal - diagonal_high.astype(F32)).astype(BF16)
    group = group_ref[...]
    owner, place = (group >> 4).astype(F32).astype(BF16), (group & 15).astype(F32).astype(BF16)
    left, right = [], []

    def rows_of(x, t):
        return jnp.broadcast_to(x[t : t + 1, :], (128, 128))

    for t in range(32):
        on = sub16 == rows_of(owner, t)
        left.append(
            jnp.concatenate(
                [
                    jnp.where(on, rows_of(diagonal_high, t), zero),
                    jnp.where(on, rows_of(diagonal_low, t), zero),
                ],
                0,
            )
        )
        right.append(jnp.where(sub16 == rows_of(place, t), one, zero))
    extra = lax.dot_general(
        jnp.concatenate(left, 1),
        jnp.concatenate(right, 1),
        (((1,), (1,)), ((), ())),
        preferred_element_type=F32,
    )
    out_ref[pl.ds(16, 128, stride=17), :] = extra[:128] + extra[128:]

    def chunk(i, _):
        locals_ = []
        for k in range(8):
            local = group_ref[...] - (i * 8 + k) * 128
            inside = (local >= 0) & (local < 128)
            locals_.append(jnp.where(inside, local, 128).astype(F32).astype(BF16))
        hot = []
        for t in range(32):
            hot.append(
                jnp.concatenate(
                    [jnp.where(sub16 == rows_of(local, t), one, zero) for local in locals_], 0
                )
            )
        total = jnp.dot(jnp.concatenate(hot, 1), limbs_ref[...], preferred_element_type=F32)
        total = total[:, :128] + total[:, 128:]
        for d in range(8 * 8):
            out_ref[pl.ds((i * 8 * 8 + d) * 17, 16), :] = total[d * 16 : d * 16 + 16]
        return 0

    lax.fori_loop(0, 16 // 8, chunk, 0)


def shrink_body(tau_ref, rows_ref, out_ref, sys_ref, stage_ref):
    per = 16
    row_id = lax.broadcasted_iota(jnp.int32, (128, 128), 0)
    lane_id = lax.broadcasted_iota(jnp.int32, (128, 128), 1)
    eye = jnp.where(row_id == lane_id, 1.0, 0.0)
    masks = packed_masks()
    half = 64 * 17
    diagonals = rows_ref[pl.ds(16, 64, stride=17), :] + rows_ref[pl.ds(half + 16, 64, stride=17), :]
    diagonals = jnp.concatenate([jnp.zeros((64, 128), F32), diagonals], 0).T
    for g in range(per):
        packed = rows_ref[pl.ds(g, 64, stride=17), :] + rows_ref[pl.ds(half + g, 64, stride=17), :]
        sys_ref[g] = unpack_symmetric(packed, diagonals[g : g + 1], masks, F32) + tau_ref[g] * eye
    lane16 = lax.broadcasted_iota(jnp.int32, (NB, 128), 1)
    sub16 = lax.broadcasted_iota(jnp.int32, (NB, 128), 0)
    same = (row_id >> 4) == (lane_id >> 4)
    segment = (lane_id >> 4).astype(F32).astype(BF16)
    first_lanes = segment < jnp.asarray(3, BF16)
    second_lanes = segment < jnp.asarray(5, BF16)

    def block(b, _):
        start = pl.multiple_of(b * NB, NB)
        panels = [sys_ref[g, pl.ds(start, NB), :] for g in range(per)]
        pivots = []
        for h in range(2):
            joined = jnp.zeros((NB, 128), F32)
            for k in range(8):
                moved = pltpu.roll(panels[h * 8 + k], lax.rem(128 + k * NB - start, 128), axis=1)
                joined = jnp.where((lane16 >> 4) == k, moved, joined)
            pivots.append(joined)
        pivots = invert_blocks(jnp.concatenate(pivots, 0))
        in_block = (lane16 >= start) & (lane16 < start + NB)
        identity = jnp.where(lane16 - start == sub16, 1.0, 0.0)
        in_lanes = (lane_id >= start) & (lane_id < start + NB)
        scaled = []
        for h in range(2):
            left = jnp.where(same, jnp.concatenate([pivots[h * NB : (h + 1) * NB]] * 8, 0), 0.0)
            right = jnp.concatenate(
                [jnp.where(in_block, identity, panels[h * 8 + k]) for k in range(8)], 0
            )
            product = wide_product(left, right)
            scaled += [product[k * NB : (k + 1) * NB] for k in range(8)]
        pick = start + (lane_id & (NB - 1))
        for g in range(per):
            matrix = sys_ref[g]
            columns = jnp.take_along_axis(matrix, pick, axis=1, mode="promise_in_bounds")
            c0, c1, c2 = limbs(columns)
            w0, w1, w2 = limbs(scaled[g])
            none = jnp.zeros_like(w0)
            update = jnp.dot(
                jnp.where(first_lanes, c0, jnp.where(second_lanes, c1, c2)),
                jnp.concatenate([w2, w1, w0, w1, w0, w0, none, none], 0),
                preferred_element_type=F32,
            )
            sys_ref[g] = jnp.where(in_lanes, 0.0, matrix) - update
        for g in range(per):
            sys_ref[g, pl.ds(start, NB), :] = scaled[g]
        return 0

    lax.fori_loop(0, 128 // NB, block, 0)
    extra = []
    for g in range(per):
        packed, rest = pack_symmetric(eye - tau_ref[g] * sys_ref[g], masks)
        stage_ref[pl.ds(g, 64, stride=18), :] = packed
        extra.append(jnp.sum(rest, axis=0, keepdims=True))
    extra = jnp.concatenate(extra + [jnp.zeros((128 - per, 128), F32)], 0)
    stage_ref[pl.ds(16, 64, stride=18), :] = extra.T[64:]
    stage_ref[pl.ds(17, 64, stride=18), :] = jnp.zeros((64, 128), F32)
    result = stage_ref[...].astype(BF16)
    out_ref[0:1152, :] = result
    out_ref[1152:2304, :] = result


def limbs(value):
    first = value.astype(BF16)
    rest = value - first.astype(F32)
    second = rest.astype(BF16)
    return first, second, (rest - second.astype(F32)).astype(BF16)


def wide_product(left, right):
    a0, a1, a2 = limbs(left)
    w0, w1, w2 = limbs(right)
    main = jnp.dot(
        jnp.concatenate([a0, a1], 1),
        jnp.concatenate([jnp.concatenate([w0, w0], 0), jnp.concatenate([w1, w1], 0)], 1),
        preferred_element_type=F32,
    )
    small = jnp.dot(
        jnp.concatenate([a0, a2], 1), jnp.concatenate([w2, w0], 0), preferred_element_type=F32
    )
    return main[:, :128] + (main[:, 128:] + small)


def invert_blocks(value):
    shape = value.shape
    lane = lax.broadcasted_iota(jnp.int32, shape, 1)
    sub = lax.broadcasted_iota(jnp.int32, shape, 0) & (NB - 1)
    within = lane & (NB - 1)
    segment = lane - within

    def spread(x, row):
        parts = [jnp.broadcast_to(x[h * NB + row : h * NB + row + 1], (NB, 128)) for h in range(2)]
        return jnp.concatenate(parts, 0)

    for j in range(0, NB, 2):
        c0 = jnp.take_along_axis(value, segment + j, axis=1, mode="promise_in_bounds")
        c1 = jnp.take_along_axis(value, segment + (j + 1), axis=1, mode="promise_in_bounds")
        at0, at1 = within == j, within == j + 1
        r0, r1 = spread(value, j), spread(value, j + 1)
        inverse = 1.0 / spread(c0, j)
        ratio = spread(c1, j) * inverse
        below = spread(c0, j + 1)
        s0 = jnp.where(at0, inverse, r0 * inverse)
        pivot = 1.0 / (spread(c1, j + 1) - below * ratio)
        rest = jnp.where(at0, 0.0, r1) - below * s0
        s1 = jnp.where(at1, pivot, rest * pivot)
        s0 = jnp.where(at1, 0.0, s0) - ratio * s1
        kept = jnp.where(at0 | at1, 0.0, value)
        c1 = c1 - c0 * ratio
        first = jnp.where(at0, inverse, jnp.where(at1, 0.0, r0 * inverse))
        value = jnp.where(
            sub == j, s0, jnp.where(sub == j + 1, s1, (kept - c0 * first) - c1 * s1)
        )
    return value


def expand_body(group_ref, rows_ref, out_ref, turned_ref, wide_ref, table_ref, stage_ref):
    turned_ref[...] = group_ref[...].astype(F32).T.astype(jnp.int32)
    wide_ref[...] = rows_ref[...].astype(F32)
    for j in range(4):

        def gather(d, _):
            value = wide_ref[pl.ds((d + 32 * j) * 18, 16), :].astype(BF16)
            table_ref[pl.ds(pl.multiple_of(d * 16, 16), 16), j * 128 : (j + 1) * 128] = value
            return 0

        lax.fori_loop(0, 32, gather, 0, unroll=8)
    extras = wide_ref[pl.ds(16, 128, stride=18), :].astype(BF16)
    lane = lax.broadcasted_iota(jnp.int32, (128, 128), 1)
    lane16 = lane.astype(F32).astype(BF16)
    zero = jnp.zeros((128, 128), BF16)
    one = jnp.ones((128, 128), BF16)
    eye = lax.broadcasted_iota(jnp.int32, (32, 128), 0) == lax.broadcasted_iota(
        jnp.int32, (32, 128), 1
    )
    stage_ref[pl.ds(33, 128, stride=34), :] = jnp.zeros((128, 128), F32)
    for u in range(4):
        groups, hot, owners = [], [], []
        for v in range(8):
            group = jnp.broadcast_to(turned_ref[:, u * 8 + v : u * 8 + v + 1], (128, 128))
            groups.append(group)
            low = jnp.where((group & 127).astype(F32).astype(BF16) == lane16, one, zero)
            high = ((group >> 7) & 3).astype(F32).astype(BF16)
            hot.append(
                jnp.concatenate(
                    [jnp.where(high == jnp.full((128, 128), c, BF16), low, zero) for c in range(4)],
                    1,
                )
            )
            owners.append(jnp.where((group >> 4).astype(F32).astype(BF16) == lane16, one, zero))
        wide = jnp.dot(jnp.concatenate(hot, 0), table_ref[...], preferred_element_type=F32)
        spots = jnp.dot(jnp.concatenate(owners, 0), extras, preferred_element_type=F32)
        for v in range(8):
            group = groups[v]
            rows = slice(v * 128, (v + 1) * 128)
            quarter = group >> 9
            piece = wide[rows, 384:512]
            for j in (2, 1, 0):
                piece = jnp.where(quarter == j, wide[rows, j * 128 : (j + 1) * 128], piece)
            spot = jnp.where(lane == (group & 15), spots[rows], 0.0)
            value = jnp.sum(spot, axis=1, keepdims=True)
            for k in range(4):
                row = ((u * 8 + v) * 4 + k) * 34
                part = slice(k * 32, k * 32 + 32)
                stage_ref[row : row + 32, :] = piece[part]
                stage_ref[row + 32 : row + 33, :] = jnp.sum(
                    jnp.where(eye, value[part], 0.0), axis=0, keepdims=True
                )
    out_ref[...] = stage_ref[...].astype(BF16)


def add_halves(first_ref, cells_ref, factor_ref, sum_ref, even_ref, odd_ref):
    odd_ref[...] = jnp.zeros_like(odd_ref)
    count = 4

    def multiply(p, ref):
        for k in range(count):
            values = load_half(cells_ref, first_ref[p + k])
            ref[k * 256 : (k + 1) * 256, :] = jnp.dot(
                values, factor_ref[p + k], preferred_element_type=F32
            )

    def accumulate(p, ref):
        for k in range(count):
            first = first_ref[p + k]
            spots, sums = [], []
            for a in range(PATCH // 2):
                for b in range(PATCH):
                    at = pl.ds(first + (a * 16 + b) * 32, PATCH)
                    row = k * 256 + (a * PATCH + b) * PATCH
                    spots.append(at)
                    sums.append(sum_ref[at, :] + ref[row : row + PATCH, :])
            for at, value in zip(spots, sums):
                sum_ref[at, :] = value

    def several(i, _):
        p = i * (2 * count)
        multiply(p, even_ref)
        accumulate(jnp.maximum(p - count, 0), odd_ref)
        multiply(p + count, odd_ref)
        accumulate(p, even_ref)
        return 0

    lax.fori_loop(0, 64 // (2 * count), several, 0)
    accumulate(64 - count, odd_ref)


def edge_apply_body(
    first_ref,
    cells_ref,
    rows_ref,
    inner_ref,
    low_ref,
    high_ref,
    factor_ref,
    wide_ref,
    sum_ref,
    even_ref,
    odd_ref,
    diag_ref,
):
    wide_ref[...] = rows_ref[...].astype(F32)
    masks = packed_masks()
    used = lax.broadcasted_iota(jnp.int32, (64, 128), 1) < 32
    first_side = jnp.where(used, wide_ref[pl.ds(32, 64, stride=34), :], 0.0)
    last_side = jnp.where(used, wide_ref[pl.ds(64 * 34 + 32, 64, stride=34), :], 0.0)
    diagonals = first_side + pltpu.roll(last_side, 32, axis=1)
    diag_ref[...] = jnp.concatenate([jnp.zeros((64, 128), F32), diagonals], 0).T

    def unpack(p, _):
        side = p // 32
        packed = wide_ref[pl.ds(side * (64 * 34 - 32) + p, 64, stride=34), :]
        sum_ref[pl.ds(pl.multiple_of(p * 128, 128), 128), :] = jnp.zeros((128, 128), F32)
        factor_ref[p] = unpack_symmetric(packed, diag_ref[pl.ds(p, 1), :], masks, BF16)
        return 0

    lax.fori_loop(0, 64, unpack, 0, unroll=8)
    add_halves(first_ref, cells_ref, factor_ref, sum_ref, even_ref, odd_ref)
    low_ref[...] = sum_ref[0:2048, :].astype(BF16)
    inner_ref[...] = sum_ref[2048:6144, :]
    high_ref[...] = sum_ref[6144:8192, :].astype(BF16)


def inner_apply_body(
    first_ref, cells_ref, factor_ref, start_ref, sum_ref, even_ref, odd_ref
):
    sum_ref[...] = start_ref[...]
    add_halves(first_ref, cells_ref, factor_ref, sum_ref, even_ref, odd_ref)


def exchange(rows, sublanes):
    shape = rows.shape
    rows = rows.reshape(128, shape[0] // (128 * sublanes), sublanes, 128)
    rows = lax.all_to_all(rows, BOTH, split_axis=0, concat_axis=0, tiled=True)
    return rows.reshape(shape)


def shards(estimate, dual, corners, members, thresholds):
    margin = PATCH // 2
    index_x = lax.axis_index("gx")
    index_y = lax.axis_index("gy")
    myself = index_x * 16 + index_y
    mixture = (estimate.astype(F32) + dual.astype(F32)).astype(BF16)

    begin_x = corners[0] - (index_x * 8 - margin)
    begin_y = corners[1] - (index_y * 8 - margin)
    first = (begin_x * 16 + begin_y) * 32 + corners[2]
    low_half = begin_x <= margin
    first_edge = first + jnp.where(low_half, 0, 2048)
    first_inner = first + jnp.where(low_half, 0, -2048)
    code = ((corners[0] * 128 + corners[1]) * 32 + corners[2]).astype(F32)
    code = jnp.concatenate([jnp.zeros((64,), F32), code]).reshape(1, 128)

    side = (myself // 64).reshape(1)
    table = call(
        group_table_body,
        jax.ShapeDtypeStruct((32, 128), jnp.int32),
        side,
        members.T,
        specs=[SMEM, VMEM],
        flops=2 * 128 * 32768 * 64,
        nbytes=1 << 17,
    )
    base = jnp.stack([index_x * 8, index_y * 8])
    offset = jnp.arange(9, dtype=jnp.int32)
    near_x = index_x + offset // 3 - 1
    near_y = index_y + offset % 3 - 1
    exists = (near_x >= 0) & (near_x < 8) & (near_y >= 0) & (near_y < 16)
    near_id = jnp.where(exists, near_x * 16 + near_y, -1)
    tau = lax.dynamic_slice_in_dim(thresholds, myself * 16, 16)
    held, code, table, near_id, tau, base = lax.optimization_barrier(
        (mixture, code, table, near_id, tau, base)
    )
    yb, ya = neighbors(mixture, "gy", mixture[:, :margin], mixture[:, 8 - margin :])
    inner_cells, half_grams = call(
        inner_gram_body,
        (jax.ShapeDtypeStruct((4096, 128), F32), jax.ShapeDtypeStruct((64, 128, 128), F32)),
        first_inner,
        mixture,
        yb,
        ya,
        specs=[SMEM] + [VMEM] * 3,
        flops=2 * 64 * 256 * 128 * 128,
        nbytes=8 << 20,
    )
    wide = jnp.concatenate(
        [
            jnp.concatenate([yb[:margin], held[:margin], ya[:margin]], 1),
            jnp.concatenate([yb[margin:], held[margin:], ya[margin:]], 1),
        ],
        0,
    )
    xb, xa = neighbors(wide, "gx", wide[:margin], wide[8 - margin :])
    cells, grams = call(
        gram_body,
        (jax.ShapeDtypeStruct((8192, 128), F32), jax.ShapeDtypeStruct((128 * 33, 128), F32)),
        first_edge,
        code,
        inner_cells,
        xb,
        xa,
        half_grams,
        specs=[SMEM] + [VMEM] * 5,
        scratch=[pltpu.VMEM((128, 128), F32)],
        flops=2 * 64 * 256 * 128 * 128,
        nbytes=10 << 20,
    )
    rows = exchange(grams, 1)
    sums, near = call(
        group_sum_body,
        (jax.ShapeDtypeStruct((128 * 17, 128), F32), jax.ShapeDtypeStruct((8, 128), F32)),
        near_id,
        table,
        rows,
        specs=[SMEM, VMEM, VMEM],
        scratch=[pltpu.VMEM((4096, 256), BF16)],
        flops=2 * 2048 * 4096 * 256,
        nbytes=5 << 20,
    )
    inverse_counts = call(
        counts_body,
        jax.ShapeDtypeStruct((2048, 128), F32),
        near,
        base,
        specs=[VMEM, SMEM],
        flops=2 * 2048 * 640 * 128,
        nbytes=1 << 20,
    )
    mine = exchange(sums, 1)
    factors = call(
        shrink_body,
        jax.ShapeDtypeStruct((128 * 18, 128), BF16),
        tau,
        mine,
        specs=[SMEM, VMEM],
        scratch=[pltpu.VMEM((16, 128, 128), F32), pltpu.VMEM((64 * 18, 128), F32)],
        flops=2 * 16 * 8 * 6 * 128**3,
        nbytes=2 << 20,
    )
    factor_rows = exchange(factors, 2)
    patch_rows = call(
        expand_body,
        jax.ShapeDtypeStruct((128 * 34, 128), BF16),
        table,
        factor_rows,
        scratch=[
            pltpu.VMEM((128, 32), jnp.int32),
            pltpu.VMEM((128 * 18, 128), F32),
            pltpu.VMEM((512, 512), BF16),
            pltpu.VMEM((128 * 34, 128), F32),
        ],
        flops=2 * 2048 * 4096 * 256,
        nbytes=3 << 20,
    )
    patch_factors = exchange(patch_rows, 2)
    edge = jax.ShapeDtypeStruct((2048, 128), BF16)
    half_result = pltpu.VMEM((1024, 128), F32)
    partial, low, high, patch_factors = call(
        edge_apply_body,
        (
            jax.ShapeDtypeStruct((4096, 128), F32),
            edge,
            edge,
            jax.ShapeDtypeStruct((64, 128, 128), BF16),
        ),
        first_edge,
        cells,
        patch_factors,
        specs=[SMEM, VMEM, VMEM],
        scratch=[
            pltpu.VMEM((128 * 34, 128), F32),
            pltpu.VMEM((8192, 128), F32),
            half_result,
            half_result,
            pltpu.VMEM((128, 128), F32),
        ],
        flops=2 * 64 * 256 * 128 * 128,
        nbytes=10 << 20,
    )
    from_low, from_high = neighbors(
        partial, "gx", low.reshape(4, 16, 32, 128), high.reshape(4, 16, 32, 128)
    )
    inner = call(
        inner_apply_body,
        jax.ShapeDtypeStruct((4096, 128), F32),
        first_inner,
        inner_cells,
        patch_factors,
        partial,
        specs=[SMEM, VMEM, VMEM, VMEM],
        scratch=[half_result, half_result],
        flops=2 * 64 * 256 * 128 * 128,
        nbytes=8 << 20,
    )
    inner = inner.reshape(8, 16, 32, 128)
    inner = jnp.concatenate(
        [inner[:margin] + from_low.astype(F32), inner[margin:] + from_high.astype(F32)], 0
    )
    from_low, from_high = neighbors(
        inner, "gy", inner[:, :margin].astype(BF16), inner[:, 16 - margin :].astype(BF16)
    )
    sums = inner[:, margin : 16 - margin]
    sums = jnp.concatenate(
        [sums[:, :margin] + from_low.astype(F32), sums[:, margin:] + from_high.astype(F32)], 1
    )
    lowrank = (sums + DATA_WEIGHT * mixture.astype(F32)) * inverse_counts.reshape(8, 8, 32, 128)
    dual_next = dual.astype(F32) + estimate.astype(F32) - lowrank
    return lowrank, dual_next


def solution(mesh):
    in_specs = (
        P("gx", "gy", None, None),
        P("gx", "gy", None, None),
        P(None, ("gx", "gy")),
        P(),
        P(),
    )
    out_specs = (P("gx", "gy", None, None), P("gx", "gy", None, None))
    return jax.shard_map(shards, mesh=mesh, in_specs=in_specs, out_specs=out_specs, check_vma=False)
```

```python
import functools

import jax
import jax.numpy as jnp
from jax import lax
from jax.experimental import pallas as pl
from jax.experimental.pallas import tpu as pltpu
from jax.sharding import PartitionSpec as P

PATCH = 8
DATA_WEIGHT = 2.0
F32 = jnp.float32
BF16 = jnp.bfloat16
BOTH = ("gx", "gy")
NB = 16

VMEM = pl.BlockSpec(memory_space=pltpu.VMEM)
SMEM = pl.BlockSpec(memory_space=pltpu.SMEM)
PARAMS = pltpu.CompilerParams(vmem_limit_bytes=20 * 1024 * 1024)


def call(body, out_shape, *args, specs=None, scratch=(), flops=0, nbytes=0):
    outs = jax.tree.map(lambda _: VMEM, out_shape)
    return pl.pallas_call(
        body,
        out_shape=out_shape,
        in_specs=specs or [VMEM] * len(args),
        out_specs=outs,
        scratch_shapes=list(scratch),
        compiler_params=PARAMS,
        cost_estimate=pl.CostEstimate(flops=flops, bytes_accessed=nbytes, transcendentals=0),
    )(*args)


def neighbors(value, axis, first, last):
    size = lax.axis_size(axis)
    up = [(i, i + 1) for i in range(size - 1)]
    down = [(j, i) for i, j in up]
    before = lax.ppermute(last, axis, up)
    after = lax.ppermute(first, axis, down)
    return before, after


def packed_masks():
    row = lax.broadcasted_iota(jnp.int32, (64, 128), 0)
    lane = lax.broadcasted_iota(jnp.int32, (64, 128), 1)
    return (lane < 64) & (row > lane), row == lane, lane == row + 64


def pack_symmetric(matrix, masks):
    moved, _, low_diagonal = masks
    top, bottom = matrix[:64], matrix[64:]
    packed = jnp.where(moved, pltpu.roll(bottom, 64, axis=1), top)
    return packed, jnp.where(low_diagonal, bottom, 0.0)


def unpack_symmetric(packed, diagonal, masks, dtype):
    moved, top_diagonal, low_diagonal = masks
    top = jnp.where(moved, 0.0, jnp.where(top_diagonal, 0.5 * packed, packed))
    bottom = pltpu.roll(jnp.where(moved, packed, 0.0), 64, axis=1)
    bottom = bottom + jnp.where(low_diagonal, 0.5 * diagonal, 0.0)
    half = jnp.concatenate([top, bottom], 0).astype(dtype)
    return half + half.T


def group_table_body(side_ref, members_ref, out_ref):
    groups = members_ref.shape[1]
    high = lax.broadcasted_iota(jnp.int32, (32, 128), 0)
    low = lax.broadcasted_iota(jnp.int32, (128, 128), 0)
    lane = lax.broadcasted_iota(jnp.int32, (1, 128), 1)
    side = side_ref[0]

    def step(i, acc):
        block = members_ref[:, pl.ds(pl.multiple_of(i * 128, 128), 128)]
        group = i * 128 + lane
        group_high = jnp.broadcast_to((group >> 4).astype(F32), (32, 128))
        group_low = jnp.broadcast_to((group & 15).astype(F32), (32, 128))
        coarse, fine, lows = [], [], []
        for j in range(16):
            entry = block[j : j + 1, :]
            at_high = jnp.where(((entry >> 5) & 1) == side, entry >> 8, -1)
            at_low = ((entry >> 6) & 3) * 32 + (entry & 31)
            on = high == at_high
            coarse.append(jnp.where(on, group_high, 0.0))
            fine.append(jnp.where(on, group_low, 0.0))
            lows.append(jnp.where(low == at_low, 1.0, 0.0))
        left = jnp.concatenate(
            [jnp.concatenate(coarse, 1), jnp.concatenate(fine, 1)], 0
        ).astype(BF16)
        right = jnp.concatenate(lows, 1).astype(BF16)
        return acc + lax.dot_general(
            left, right, (((1,), (1,)), ((), ())), preferred_element_type=F32
        )

    acc = lax.fori_loop(0, groups // 128, step, jnp.zeros((64, 128), F32))
    out_ref[...] = (acc[:32] * 16.0 + acc[32:]).astype(jnp.int32)


def counts_body(near_ref, base_ref, out_ref):
    code = jnp.concatenate([near_ref[m : m + 1, :] for m in range(5)], 1).astype(jnp.int32)
    lanes = code.shape[1]
    px = jnp.where(code < 0, -1000, code >> 12) - base_ref[0]
    py = ((code >> 5) & 127) - base_ref[1]
    pz = code & 31
    z = lax.broadcasted_iota(jnp.int32, (32, lanes), 0)
    in_z = jnp.where((z >= pz) & (z < pz + PATCH), 1.0, 0.0).astype(BF16)
    ones = jnp.ones((lanes, 128), BF16)

    def column(x, _):
        in_x = (px <= x) & (px > x - PATCH)
        parts = []
        for y in range(8):
            hit = jnp.where(in_x & (py <= y) & (py > y - PATCH), 1.0, 0.0).astype(BF16)
            parts.append(jnp.broadcast_to(hit, in_z.shape) * in_z)
        cover = jnp.dot(jnp.concatenate(parts, 0), ones, preferred_element_type=F32)
        out_ref[pl.ds(pl.multiple_of(x * 256, 256), 256), :] = 1.0 / (cover + DATA_WEIGHT)
        return 0

    lax.fori_loop(0, 8, column, 0, unroll=4)


def load_half(cells_ref, first):
    rows = []
    for a in range(PATCH // 2):
        for b in range(PATCH):
            rows.append(cells_ref[pl.ds(first + (a * 16 + b) * 32, PATCH), :])
    return jnp.concatenate(rows, 0).astype(BF16)


def half_gram(cells_ref, first):
    values = load_half(cells_ref, first)
    return lax.dot_general(values, values, (((0,), (0,)), ((), ())), preferred_element_type=F32)


def inner_gram_body(first_ref, own_ref, yb_ref, ya_ref, cells_ref, gram_ref):
    def fill(x, _):
        row = pl.multiple_of(x * 512, 512)
        cells_ref[pl.ds(row, 128), :] = yb_ref[x].reshape(128, 128).astype(F32)
        cells_ref[pl.ds(row + 128, 256), :] = own_ref[x].reshape(256, 128).astype(F32)
        cells_ref[pl.ds(row + 384, 128), :] = ya_ref[x].reshape(128, 128).astype(F32)
        return 0

    lax.fori_loop(0, 8, fill, 0)

    def patch(p, _):
        gram_ref[p] = half_gram(cells_ref, first_ref[p])
        return 0

    lax.fori_loop(0, 64, patch, 0, unroll=16)


def gram_body(
    first_ref, code_ref, inner_ref, xb_ref, xa_ref, half_ref, cells_ref, out_ref, diag_ref
):
    cells_ref[0:2048, :] = xb_ref[...].reshape(2048, 128).astype(F32)
    cells_ref[2048:6144, :] = inner_ref[...]
    cells_ref[6144:8192, :] = xa_ref[...].reshape(2048, 128).astype(F32)
    diag_ref[...] = jnp.zeros_like(diag_ref)
    masks = packed_masks()

    def patch(p, _):
        gram = half_ref[p] + half_gram(cells_ref, first_ref[p])
        packed, rest = pack_symmetric(gram, masks)
        out_ref[pl.ds((p // 32) * (64 * 33 - 32) + p, 64, stride=33), :] = packed
        diag_ref[pl.ds(p, 1), :] = jnp.sum(rest, axis=0, keepdims=True)
        return 0

    lax.fori_loop(0, 64, patch, 0, unroll=16)
    left = lax.broadcasted_iota(jnp.int32, (64, 128), 1) < 64
    turned = diag_ref[...].T[64:]
    out_ref[pl.ds(32, 64, stride=33), :] = jnp.where(left, turned, code_ref[...])
    out_ref[pl.ds(64 * 33 + 32, 64, stride=33), :] = jnp.where(
        left, pltpu.roll(turned, 96, axis=1), code_ref[...]
    )


def group_sum_body(near_id_ref, group_ref, rows_ref, out_ref, near_ref, limbs_ref):
    right_half = lax.broadcasted_iota(jnp.int32, (1, 128), 1) >= 64
    codes = []
    for n in range(10):
        code = jnp.full((1, 128), -1.0, F32)
        if n < 9:
            source = near_id_ref[n]
            row = rows_ref[pl.ds(jnp.maximum(source, 0) * 33 + 32, 1), :]
            code = jnp.where(source >= 0, row, code)
        codes.append(code)
    near_ref[...] = jnp.concatenate(
        [
            jnp.where(right_half, codes[2 * m], pltpu.roll(codes[2 * m + 1], 64, axis=1))
            for m in range(5)
        ]
        + [jnp.full((3, 128), -1.0, F32)],
        0,
    )

    def split(i, _):
        value = rows_ref[pl.ds(i * 33, 32), :]
        high = value.astype(BF16)
        row = pl.multiple_of(i * 32, 32)
        limbs_ref[pl.ds(row, 32), 0:128] = high
        limbs_ref[pl.ds(row, 32), 128:256] = (value - high.astype(F32)).astype(BF16)
        return 0

    lax.fori_loop(0, 128, split, 0, unroll=8)
    one = jnp.ones((128, 128), BF16)
    zero = jnp.zeros((128, 128), BF16)
    sub16 = lax.broadcasted_iota(jnp.int32, (128, 128), 0).astype(F32).astype(BF16)

    used = lax.broadcasted_iota(jnp.int32, (32, 128), 1) < 32
    diagonal = jnp.zeros((32, 128), F32)
    for c in range(4):
        part = jnp.where(used, rows_ref[pl.ds(32 + 33 * c, 32, stride=132), :], 0.0)
        diagonal = diagonal + (pltpu.roll(part, 32 * c, axis=1) if c else part)
    diagonal_high = diagonal.astype(BF16)
    diagonal_low = (diagonal - diagonal_high.astype(F32)).astype(BF16)
    group = group_ref[...]
    owner, place = (group >> 4).astype(F32).astype(BF16), (group & 15).astype(F32).astype(BF16)
    left, right = [], []

    def rows_of(x, t):
        return jnp.broadcast_to(x[t : t + 1, :], (128, 128))

    for t in range(32):
        on = sub16 == rows_of(owner, t)
        left.append(
            jnp.concatenate(
                [
                    jnp.where(on, rows_of(diagonal_high, t), zero),
                    jnp.where(on, rows_of(diagonal_low, t), zero),
                ],
                0,
            )
        )
        right.append(jnp.where(sub16 == rows_of(place, t), one, zero))
    extra = lax.dot_general(
        jnp.concatenate(left, 1),
        jnp.concatenate(right, 1),
        (((1,), (1,)), ((), ())),
        preferred_element_type=F32,
    )
    out_ref[pl.ds(16, 128, stride=17), :] = extra[:128] + extra[128:]

    def chunk(i, _):
        locals_ = []
        for k in range(8):
            local = group_ref[...] - (i * 8 + k) * 128
            inside = (local >= 0) & (local < 128)
            locals_.append(jnp.where(inside, local, 128).astype(F32).astype(BF16))
        hot = []
        for t in range(32):
            hot.append(
                jnp.concatenate(
                    [jnp.where(sub16 == rows_of(local, t), one, zero) for local in locals_], 0
                )
            )
        total = jnp.dot(jnp.concatenate(hot, 1), limbs_ref[...], preferred_element_type=F32)
        total = total[:, :128] + total[:, 128:]
        for d in range(8 * 8):
            out_ref[pl.ds((i * 8 * 8 + d) * 17, 16), :] = total[d * 16 : d * 16 + 16]
        return 0

    lax.fori_loop(0, 16 // 8, chunk, 0)


def shrink_body(tau_ref, rows_ref, out_ref, sys_ref, stage_ref):
    per = 16
    row_id = lax.broadcasted_iota(jnp.int32, (128, 128), 0)
    lane_id = lax.broadcasted_iota(jnp.int32, (128, 128), 1)
    eye = jnp.where(row_id == lane_id, 1.0, 0.0)
    masks = packed_masks()
    half = 64 * 17
    diagonals = rows_ref[pl.ds(16, 64, stride=17), :] + rows_ref[pl.ds(half + 16, 64, stride=17), :]
    diagonals = jnp.concatenate([jnp.zeros((64, 128), F32), diagonals], 0).T
    for g in range(per):
        packed = rows_ref[pl.ds(g, 64, stride=17), :] + rows_ref[pl.ds(half + g, 64, stride=17), :]
        sys_ref[g] = unpack_symmetric(packed, diagonals[g : g + 1], masks, F32) + tau_ref[g] * eye
    lane16 = lax.broadcasted_iota(jnp.int32, (NB, 128), 1)
    sub16 = lax.broadcasted_iota(jnp.int32, (NB, 128), 0)
    same = (row_id >> 4) == (lane_id >> 4)
    segment = (lane_id >> 4).astype(F32).astype(BF16)
    first_lanes = segment < jnp.asarray(3, BF16)
    second_lanes = segment < jnp.asarray(5, BF16)

    def block(b, _):
        start = pl.multiple_of(b * NB, NB)
        panels = [sys_ref[g, pl.ds(start, NB), :] for g in range(per)]
        pivots = []
        for h in range(2):
            joined = jnp.zeros((NB, 128), F32)
            for k in range(8):
                moved = pltpu.roll(panels[h * 8 + k], lax.rem(128 + k * NB - start, 128), axis=1)
                joined = jnp.where((lane16 >> 4) == k, moved, joined)
            pivots.append(joined)
        originals = pivots
        pivots = invert_blocks(jnp.concatenate(pivots, 0))
        in_block = (lane16 >= start) & (lane16 < start + NB)
        identity = jnp.where(lane16 - start == sub16, 1.0, 0.0)
        in_lanes = (lane_id >= start) & (lane_id < start + NB)
        scaled = []
        for h in range(2):
            left = jnp.where(same, jnp.concatenate([pivots[h * NB : (h + 1) * NB]] * 8, 0), 0.0)
            right = jnp.concatenate(
                [jnp.where(in_block, identity, panels[h * 8 + k]) for k in range(8)], 0
            )
            product = wide_product(left, right)
            own = jnp.where(same, jnp.concatenate([originals[h]] * 8, 0), 0.0)
            product = product + wide_product(left, right - wide_product(own, product))
            scaled += [product[k * NB : (k + 1) * NB] for k in range(8)]
        pick = start + (lane_id & (NB - 1))
        for g in range(per):
            matrix = sys_ref[g]
            columns = jnp.take_along_axis(matrix, pick, axis=1, mode="promise_in_bounds")
            c0, c1, c2 = limbs(columns)
            w0, w1, w2 = limbs(scaled[g])
            none = jnp.zeros_like(w0)
            update = jnp.dot(
                jnp.where(first_lanes, c0, jnp.where(second_lanes, c1, c2)),
                jnp.concatenate([w2, w1, w0, w1, w0, w0, none, none], 0),
                preferred_element_type=F32,
            )
            sys_ref[g] = jnp.where(in_lanes, 0.0, matrix) - update
        for g in range(per):
            sys_ref[g, pl.ds(start, NB), :] = scaled[g]
        return 0

    lax.fori_loop(0, 128 // NB, block, 0)
    extra = []
    for g in range(per):
        packed, rest = pack_symmetric(eye - tau_ref[g] * sys_ref[g], masks)
        stage_ref[pl.ds(g, 64, stride=18), :] = packed
        extra.append(jnp.sum(rest, axis=0, keepdims=True))
    extra = jnp.concatenate(extra + [jnp.zeros((128 - per, 128), F32)], 0)
    stage_ref[pl.ds(16, 64, stride=18), :] = extra.T[64:]
    stage_ref[pl.ds(17, 64, stride=18), :] = jnp.zeros((64, 128), F32)
    result = stage_ref[...].astype(BF16)
    out_ref[0:1152, :] = result
    out_ref[1152:2304, :] = result


def limbs(value):
    first = value.astype(BF16)
    rest = value - first.astype(F32)
    second = rest.astype(BF16)
    return first, second, (rest - second.astype(F32)).astype(BF16)


def wide_product(left, right):
    a0, a1, a2 = limbs(left)
    w0, w1, w2 = limbs(right)
    main = jnp.dot(
        jnp.concatenate([a0, a1], 1),
        jnp.concatenate([jnp.concatenate([w0, w0], 0), jnp.concatenate([w1, w1], 0)], 1),
        preferred_element_type=F32,
    )
    small = jnp.dot(
        jnp.concatenate([a0, a2], 1), jnp.concatenate([w2, w0], 0), preferred_element_type=F32
    )
    return main[:, :128] + (main[:, 128:] + small)


def invert_blocks(value):
    shape = value.shape
    lane = lax.broadcasted_iota(jnp.int32, shape, 1)
    sub = lax.broadcasted_iota(jnp.int32, shape, 0) & (NB - 1)
    within = lane & (NB - 1)
    segment = lane - within

    def spread(x, row):
        parts = [jnp.broadcast_to(x[h * NB + row : h * NB + row + 1], (NB, 128)) for h in range(2)]
        return jnp.concatenate(parts, 0)

    for j in range(0, NB, 2):
        c0 = jnp.take_along_axis(value, segment + j, axis=1, mode="promise_in_bounds")
        c1 = jnp.take_along_axis(value, segment + (j + 1), axis=1, mode="promise_in_bounds")
        at0, at1 = within == j, within == j + 1
        r0, r1 = spread(value, j), spread(value, j + 1)
        inverse = 1.0 / spread(c0, j)
        ratio = spread(c1, j) * inverse
        below = spread(c0, j + 1)
        s0 = jnp.where(at0, inverse, r0 * inverse)
        pivot = 1.0 / (spread(c1, j + 1) - below * ratio)
        rest = jnp.where(at0, 0.0, r1) - below * s0
        s1 = jnp.where(at1, pivot, rest * pivot)
        s0 = jnp.where(at1, 0.0, s0) - ratio * s1
        kept = jnp.where(at0 | at1, 0.0, value)
        c1 = c1 - c0 * ratio
        first = jnp.where(at0, inverse, jnp.where(at1, 0.0, r0 * inverse))
        value = jnp.where(
            sub == j, s0, jnp.where(sub == j + 1, s1, (kept - c0 * first) - c1 * s1)
        )
    return value


def expand_body(group_ref, rows_ref, out_ref, turned_ref, wide_ref, table_ref, stage_ref):
    turned_ref[...] = group_ref[...].astype(F32).T.astype(jnp.int32)
    wide_ref[...] = rows_ref[...].astype(F32)
    for j in range(4):

        def gather(d, _):
            value = wide_ref[pl.ds((d + 32 * j) * 18, 16), :].astype(BF16)
            table_ref[pl.ds(pl.multiple_of(d * 16, 16), 16), j * 128 : (j + 1) * 128] = value
            return 0

        lax.fori_loop(0, 32, gather, 0, unroll=8)
    extras = wide_ref[pl.ds(16, 128, stride=18), :].astype(BF16)
    lane = lax.broadcasted_iota(jnp.int32, (128, 128), 1)
    lane16 = lane.astype(F32).astype(BF16)
    zero = jnp.zeros((128, 128), BF16)
    one = jnp.ones((128, 128), BF16)
    eye = lax.broadcasted_iota(jnp.int32, (32, 128), 0) == lax.broadcasted_iota(
        jnp.int32, (32, 128), 1
    )
    stage_ref[pl.ds(33, 128, stride=34), :] = jnp.zeros((128, 128), F32)
    for u in range(4):
        groups, hot, owners = [], [], []
        for v in range(8):
            group = jnp.broadcast_to(turned_ref[:, u * 8 + v : u * 8 + v + 1], (128, 128))
            groups.append(group)
            low = jnp.where((group & 127).astype(F32).astype(BF16) == lane16, one, zero)
            high = ((group >> 7) & 3).astype(F32).astype(BF16)
            hot.append(
                jnp.concatenate(
                    [jnp.where(high == jnp.full((128, 128), c, BF16), low, zero) for c in range(4)],
                    1,
                )
            )
            owners.append(jnp.where((group >> 4).astype(F32).astype(BF16) == lane16, one, zero))
        wide = jnp.dot(jnp.concatenate(hot, 0), table_ref[...], preferred_element_type=F32)
        spots = jnp.dot(jnp.concatenate(owners, 0), extras, preferred_element_type=F32)
        for v in range(8):
            group = groups[v]
            rows = slice(v * 128, (v + 1) * 128)
            quarter = group >> 9
            piece = wide[rows, 384:512]
            for j in (2, 1, 0):
                piece = jnp.where(quarter == j, wide[rows, j * 128 : (j + 1) * 128], piece)
            spot = jnp.where(lane == (group & 15), spots[rows], 0.0)
            value = jnp.sum(spot, axis=1, keepdims=True)
            for k in range(4):
                row = ((u * 8 + v) * 4 + k) * 34
                part = slice(k * 32, k * 32 + 32)
                stage_ref[row : row + 32, :] = piece[part]
                stage_ref[row + 32 : row + 33, :] = jnp.sum(
                    jnp.where(eye, value[part], 0.0), axis=0, keepdims=True
                )
    out_ref[...] = stage_ref[...].astype(BF16)


def add_halves(first_ref, cells_ref, factor_ref, sum_ref, even_ref, odd_ref):
    odd_ref[...] = jnp.zeros_like(odd_ref)
    count = 4

    def multiply(p, ref):
        for k in range(count):
            values = load_half(cells_ref, first_ref[p + k])
            ref[k * 256 : (k + 1) * 256, :] = jnp.dot(
                values, factor_ref[p + k], preferred_element_type=F32
            )

    def accumulate(p, ref):
        for k in range(count):
            first = first_ref[p + k]
            spots, sums = [], []
            for a in range(PATCH // 2):
                for b in range(PATCH):
                    at = pl.ds(first + (a * 16 + b) * 32, PATCH)
                    row = k * 256 + (a * PATCH + b) * PATCH
                    spots.append(at)
                    sums.append(sum_ref[at, :] + ref[row : row + PATCH, :])
            for at, value in zip(spots, sums):
                sum_ref[at, :] = value

    def several(i, _):
        p = i * (2 * count)
        multiply(p, even_ref)
        accumulate(jnp.maximum(p - count, 0), odd_ref)
        multiply(p + count, odd_ref)
        accumulate(p, even_ref)
        return 0

    lax.fori_loop(0, 64 // (2 * count), several, 0)
    accumulate(64 - count, odd_ref)


def edge_apply_body(
    first_ref,
    cells_ref,
    rows_ref,
    inner_ref,
    low_ref,
    high_ref,
    factor_ref,
    wide_ref,
    sum_ref,
    even_ref,
    odd_ref,
    diag_ref,
):
    wide_ref[...] = rows_ref[...].astype(F32)
    masks = packed_masks()
    used = lax.broadcasted_iota(jnp.int32, (64, 128), 1) < 32
    first_side = jnp.where(used, wide_ref[pl.ds(32, 64, stride=34), :], 0.0)
    last_side = jnp.where(used, wide_ref[pl.ds(64 * 34 + 32, 64, stride=34), :], 0.0)
    diagonals = first_side + pltpu.roll(last_side, 32, axis=1)
    diag_ref[...] = jnp.concatenate([jnp.zeros((64, 128), F32), diagonals], 0).T

    def unpack(p, _):
        side = p // 32
        packed = wide_ref[pl.ds(side * (64 * 34 - 32) + p, 64, stride=34), :]
        sum_ref[pl.ds(pl.multiple_of(p * 128, 128), 128), :] = jnp.zeros((128, 128), F32)
        factor_ref[p] = unpack_symmetric(packed, diag_ref[pl.ds(p, 1), :], masks, BF16)
        return 0

    lax.fori_loop(0, 64, unpack, 0, unroll=8)
    add_halves(first_ref, cells_ref, factor_ref, sum_ref, even_ref, odd_ref)
    low_ref[...] = sum_ref[0:2048, :].astype(BF16)
    inner_ref[...] = sum_ref[2048:6144, :]
    high_ref[...] = sum_ref[6144:8192, :].astype(BF16)


def inner_apply_body(
    first_ref, cells_ref, factor_ref, start_ref, sum_ref, even_ref, odd_ref
):
    sum_ref[...] = start_ref[...]
    add_halves(first_ref, cells_ref, factor_ref, sum_ref, even_ref, odd_ref)


def exchange(rows, sublanes):
    shape = rows.shape
    rows = rows.reshape(128, shape[0] // (128 * sublanes), sublanes, 128)
    rows = lax.all_to_all(rows, BOTH, split_axis=0, concat_axis=0, tiled=True)
    return rows.reshape(shape)


def shards(estimate, dual, corners, members, thresholds):
    margin = PATCH // 2
    index_x = lax.axis_index("gx")
    index_y = lax.axis_index("gy")
    myself = index_x * 16 + index_y
    mixture = (estimate.astype(F32) + dual.astype(F32)).astype(BF16)

    begin_x = corners[0] - (index_x * 8 - margin)
    begin_y = corners[1] - (index_y * 8 - margin)
    first = (begin_x * 16 + begin_y) * 32 + corners[2]
    low_half = begin_x <= margin
    first_edge = first + jnp.where(low_half, 0, 2048)
    first_inner = first + jnp.where(low_half, 0, -2048)
    code = ((corners[0] * 128 + corners[1]) * 32 + corners[2]).astype(F32)
    code = jnp.concatenate([jnp.zeros((64,), F32), code]).reshape(1, 128)

    side = (myself // 64).reshape(1)
    table = call(
        group_table_body,
        jax.ShapeDtypeStruct((32, 128), jnp.int32),
        side,
        members.T,
        specs=[SMEM, VMEM],
        flops=2 * 128 * 32768 * 64,
        nbytes=1 << 17,
    )
    base = jnp.stack([index_x * 8, index_y * 8])
    offset = jnp.arange(9, dtype=jnp.int32)
    near_x = index_x + offset // 3 - 1
    near_y = index_y + offset % 3 - 1
    exists = (near_x >= 0) & (near_x < 8) & (near_y >= 0) & (near_y < 16)
    near_id = jnp.where(exists, near_x * 16 + near_y, -1)
    tau = lax.dynamic_slice_in_dim(thresholds, myself * 16, 16)
    held, code, table, near_id, tau, base = lax.optimization_barrier(
        (mixture, code, table, near_id, tau, base)
    )
    yb, ya = neighbors(mixture, "gy", mixture[:, :margin], mixture[:, 8 - margin :])
    inner_cells, half_grams = call(
        inner_gram_body,
        (jax.ShapeDtypeStruct((4096, 128), F32), jax.ShapeDtypeStruct((64, 128, 128), F32)),
        first_inner,
        mixture,
        yb,
        ya,
        specs=[SMEM] + [VMEM] * 3,
        flops=2 * 64 * 256 * 128 * 128,
        nbytes=8 << 20,
    )
    wide = jnp.concatenate(
        [
            jnp.concatenate([yb[:margin], held[:margin], ya[:margin]], 1),
            jnp.concatenate([yb[margin:], held[margin:], ya[margin:]], 1),
        ],
        0,
    )
    xb, xa = neighbors(wide, "gx", wide[:margin], wide[8 - margin :])
    cells, grams = call(
        gram_body,
        (jax.ShapeDtypeStruct((8192, 128), F32), jax.ShapeDtypeStruct((128 * 33, 128), F32)),
        first_edge,
        code,
        inner_cells,
        xb,
        xa,
        half_grams,
        specs=[SMEM] + [VMEM] * 5,
        scratch=[pltpu.VMEM((128, 128), F32)],
        flops=2 * 64 * 256 * 128 * 128,
        nbytes=10 << 20,
    )
    rows = exchange(grams, 1)
    sums, near = call(
        group_sum_body,
        (jax.ShapeDtypeStruct((128 * 17, 128), F32), jax.ShapeDtypeStruct((8, 128), F32)),
        near_id,
        table,
        rows,
        specs=[SMEM, VMEM, VMEM],
        scratch=[pltpu.VMEM((4096, 256), BF16)],
        flops=2 * 2048 * 4096 * 256,
        nbytes=5 << 20,
    )
    inverse_counts = call(
        counts_body,
        jax.ShapeDtypeStruct((2048, 128), F32),
        near,
        base,
        specs=[VMEM, SMEM],
        flops=2 * 2048 * 640 * 128,
        nbytes=1 << 20,
    )
    mine = exchange(sums, 1)
    factors = call(
        shrink_body,
        jax.ShapeDtypeStruct((128 * 18, 128), BF16),
        tau,
        mine,
        specs=[SMEM, VMEM],
        scratch=[pltpu.VMEM((16, 128, 128), F32), pltpu.VMEM((64 * 18, 128), F32)],
        flops=2 * 16 * 8 * 6 * 128**3,
        nbytes=2 << 20,
    )
    factor_rows = exchange(factors, 2)
    patch_rows = call(
        expand_body,
        jax.ShapeDtypeStruct((128 * 34, 128), BF16),
        table,
        factor_rows,
        scratch=[
            pltpu.VMEM((128, 32), jnp.int32),
            pltpu.VMEM((128 * 18, 128), F32),
            pltpu.VMEM((512, 512), BF16),
            pltpu.VMEM((128 * 34, 128), F32),
        ],
        flops=2 * 2048 * 4096 * 256,
        nbytes=3 << 20,
    )
    patch_factors = exchange(patch_rows, 2)
    edge = jax.ShapeDtypeStruct((2048, 128), BF16)
    half_result = pltpu.VMEM((1024, 128), F32)
    partial, low, high, patch_factors = call(
        edge_apply_body,
        (
            jax.ShapeDtypeStruct((4096, 128), F32),
            edge,
            edge,
            jax.ShapeDtypeStruct((64, 128, 128), BF16),
        ),
        first_edge,
        cells,
        patch_factors,
        specs=[SMEM, VMEM, VMEM],
        scratch=[
            pltpu.VMEM((128 * 34, 128), F32),
            pltpu.VMEM((8192, 128), F32),
            half_result,
            half_result,
            pltpu.VMEM((128, 128), F32),
        ],
        flops=2 * 64 * 256 * 128 * 128,
        nbytes=10 << 20,
    )
    from_low, from_high = neighbors(
        partial, "gx", low.reshape(4, 16, 32, 128), high.reshape(4, 16, 32, 128)
    )
    inner = call(
        inner_apply_body,
        jax.ShapeDtypeStruct((4096, 128), F32),
        first_inner,
        inner_cells,
        patch_factors,
        partial,
        specs=[SMEM, VMEM, VMEM, VMEM],
        scratch=[half_result, half_result],
        flops=2 * 64 * 256 * 128 * 128,
        nbytes=8 << 20,
    )
    inner = inner.reshape(8, 16, 32, 128)
    inner = jnp.concatenate(
        [inner[:margin] + from_low.astype(F32), inner[margin:] + from_high.astype(F32)], 0
    )
    from_low, from_high = neighbors(
        inner, "gy", inner[:, :margin].astype(BF16), inner[:, 16 - margin :].astype(BF16)
    )
    sums = inner[:, margin : 16 - margin]
    sums = jnp.concatenate(
        [sums[:, :margin] + from_low.astype(F32), sums[:, margin:] + from_high.astype(F32)], 1
    )
    lowrank = (sums + DATA_WEIGHT * mixture.astype(F32)) * inverse_counts.reshape(8, 8, 32, 128)
    dual_next = dual.astype(F32) + estimate.astype(F32) - lowrank
    return lowrank, dual_next


def solution(mesh):
    in_specs = (
        P("gx", "gy", None, None),
        P("gx", "gy", None, None),
        P(None, ("gx", "gy")),
        P(),
        P(),
    )
    out_specs = (P("gx", "gy", None, None), P("gx", "gy", None, None))
    return jax.shard_map(shards, mesh=mesh, in_specs=in_specs, out_specs=out_specs, check_vma=False)
```

```python
import functools

import jax
import jax.numpy as jnp
from jax import lax
from jax.experimental import pallas as pl
from jax.experimental.pallas import tpu as pltpu
from jax.sharding import PartitionSpec as P

PATCH = 8
DATA_WEIGHT = 2.0
F32 = jnp.float32
BF16 = jnp.bfloat16
BOTH = ("gx", "gy")
NB = 16

VMEM = pl.BlockSpec(memory_space=pltpu.VMEM)
SMEM = pl.BlockSpec(memory_space=pltpu.SMEM)
PARAMS = pltpu.CompilerParams(vmem_limit_bytes=20 * 1024 * 1024)


def call(body, out_shape, *args, specs=None, scratch=(), flops=0, nbytes=0):
    outs = jax.tree.map(lambda _: VMEM, out_shape)
    return pl.pallas_call(
        body,
        out_shape=out_shape,
        in_specs=specs or [VMEM] * len(args),
        out_specs=outs,
        scratch_shapes=list(scratch),
        compiler_params=PARAMS,
        cost_estimate=pl.CostEstimate(flops=flops, bytes_accessed=nbytes, transcendentals=0),
    )(*args)


def neighbors(value, axis, first, last):
    size = lax.axis_size(axis)
    up = [(i, i + 1) for i in range(size - 1)]
    down = [(j, i) for i, j in up]
    before = lax.ppermute(last, axis, up)
    after = lax.ppermute(first, axis, down)
    return before, after


def packed_masks():
    row = lax.broadcasted_iota(jnp.int32, (64, 128), 0)
    lane = lax.broadcasted_iota(jnp.int32, (64, 128), 1)
    return (lane < 64) & (row > lane), row == lane, lane == row + 64


def pack_symmetric(matrix, masks):
    moved, _, low_diagonal = masks
    top, bottom = matrix[:64], matrix[64:]
    packed = jnp.where(moved, pltpu.roll(bottom, 64, axis=1), top)
    return packed, jnp.where(low_diagonal, bottom, 0.0)


def unpack_symmetric(packed, diagonal, masks, dtype):
    moved, top_diagonal, low_diagonal = masks
    top = jnp.where(moved, 0.0, jnp.where(top_diagonal, 0.5 * packed, packed))
    bottom = pltpu.roll(jnp.where(moved, packed, 0.0), 64, axis=1)
    bottom = bottom + jnp.where(low_diagonal, 0.5 * diagonal, 0.0)
    half = jnp.concatenate([top, bottom], 0).astype(dtype)
    return half + half.T


def group_table_body(side_ref, members_ref, out_ref):
    groups = members_ref.shape[1]
    high = lax.broadcasted_iota(jnp.int32, (32, 128), 0)
    low = lax.broadcasted_iota(jnp.int32, (128, 128), 0)
    lane = lax.broadcasted_iota(jnp.int32, (1, 128), 1)
    side = side_ref[0]

    def step(i, acc):
        block = members_ref[:, pl.ds(pl.multiple_of(i * 128, 128), 128)]
        group = i * 128 + lane
        group_high = jnp.broadcast_to((group >> 4).astype(F32), (32, 128))
        group_low = jnp.broadcast_to((group & 15).astype(F32), (32, 128))
        coarse, fine, lows = [], [], []
        for j in range(16):
            entry = block[j : j + 1, :]
            at_high = jnp.where(((entry >> 5) & 1) == side, entry >> 8, -1)
            at_low = ((entry >> 6) & 3) * 32 + (entry & 31)
            on = high == at_high
            coarse.append(jnp.where(on, group_high, 0.0))
            fine.append(jnp.where(on, group_low, 0.0))
            lows.append(jnp.where(low == at_low, 1.0, 0.0))
        left = jnp.concatenate(
            [jnp.concatenate(coarse, 1), jnp.concatenate(fine, 1)], 0
        ).astype(BF16)
        right = jnp.concatenate(lows, 1).astype(BF16)
        return acc + lax.dot_general(
            left, right, (((1,), (1,)), ((), ())), preferred_element_type=F32
        )

    acc = lax.fori_loop(0, groups // 128, step, jnp.zeros((64, 128), F32))
    out_ref[...] = (acc[:32] * 16.0 + acc[32:]).astype(jnp.int32)


def counts_body(near_ref, base_ref, out_ref):
    code = jnp.concatenate([near_ref[m : m + 1, :] for m in range(5)], 1).astype(jnp.int32)
    lanes = code.shape[1]
    px = jnp.where(code < 0, -1000, code >> 12) - base_ref[0]
    py = ((code >> 5) & 127) - base_ref[1]
    pz = code & 31
    z = lax.broadcasted_iota(jnp.int32, (32, lanes), 0)
    in_z = jnp.where((z >= pz) & (z < pz + PATCH), 1.0, 0.0).astype(BF16)
    ones = jnp.ones((lanes, 128), BF16)

    def column(x, _):
        in_x = (px <= x) & (px > x - PATCH)
        parts = []
        for y in range(8):
            hit = jnp.where(in_x & (py <= y) & (py > y - PATCH), 1.0, 0.0).astype(BF16)
            parts.append(jnp.broadcast_to(hit, in_z.shape) * in_z)
        cover = jnp.dot(jnp.concatenate(parts, 0), ones, preferred_element_type=F32)
        out_ref[pl.ds(pl.multiple_of(x * 256, 256), 256), :] = 1.0 / (cover + DATA_WEIGHT)
        return 0

    lax.fori_loop(0, 8, column, 0, unroll=4)


def load_half(cells_ref, first):
    rows = []
    for a in range(PATCH // 2):
        for b in range(PATCH):
            rows.append(cells_ref[pl.ds(first + (a * 16 + b) * 32, PATCH), :])
    return jnp.concatenate(rows, 0).astype(BF16)


def half_gram(cells_ref, first):
    values = load_half(cells_ref, first)
    return lax.dot_general(values, values, (((0,), (0,)), ((), ())), preferred_element_type=F32)


def inner_gram_body(first_ref, own_ref, yb_ref, ya_ref, cells_ref, gram_ref):
    def fill(x, _):
        row = pl.multiple_of(x * 512, 512)
        cells_ref[pl.ds(row, 128), :] = yb_ref[x].reshape(128, 128).astype(F32)
        cells_ref[pl.ds(row + 128, 256), :] = own_ref[x].reshape(256, 128).astype(F32)
        cells_ref[pl.ds(row + 384, 128), :] = ya_ref[x].reshape(128, 128).astype(F32)
        return 0

    lax.fori_loop(0, 8, fill, 0)

    def patch(p, _):
        gram_ref[p] = half_gram(cells_ref, first_ref[p])
        return 0

    lax.fori_loop(0, 64, patch, 0, unroll=16)


def gram_body(
    first_ref, code_ref, inner_ref, xb_ref, xa_ref, half_ref, cells_ref, out_ref, diag_ref
):
    cells_ref[0:2048, :] = xb_ref[...].reshape(2048, 128).astype(F32)
    cells_ref[2048:6144, :] = inner_ref[...]
    cells_ref[6144:8192, :] = xa_ref[...].reshape(2048, 128).astype(F32)
    diag_ref[...] = jnp.zeros_like(diag_ref)
    masks = packed_masks()

    def patch(p, _):
        gram = half_ref[p] + half_gram(cells_ref, first_ref[p])
        packed, rest = pack_symmetric(gram, masks)
        out_ref[pl.ds((p // 32) * (64 * 33 - 32) + p, 64, stride=33), :] = packed
        diag_ref[pl.ds(p, 1), :] = jnp.sum(rest, axis=0, keepdims=True)
        return 0

    lax.fori_loop(0, 64, patch, 0, unroll=16)
    left = lax.broadcasted_iota(jnp.int32, (64, 128), 1) < 64
    turned = diag_ref[...].T[64:]
    out_ref[pl.ds(32, 64, stride=33), :] = jnp.where(left, turned, code_ref[...])
    out_ref[pl.ds(64 * 33 + 32, 64, stride=33), :] = jnp.where(
        left, pltpu.roll(turned, 96, axis=1), code_ref[...]
    )


def group_sum_body(near_id_ref, group_ref, rows_ref, out_ref, near_ref, limbs_ref):
    right_half = lax.broadcasted_iota(jnp.int32, (1, 128), 1) >= 64
    codes = []
    for n in range(10):
        code = jnp.full((1, 128), -1.0, F32)
        if n < 9:
            source = near_id_ref[n]
            row = rows_ref[pl.ds(jnp.maximum(source, 0) * 33 + 32, 1), :]
            code = jnp.where(source >= 0, row, code)
        codes.append(code)
    near_ref[...] = jnp.concatenate(
        [
            jnp.where(right_half, codes[2 * m], pltpu.roll(codes[2 * m + 1], 64, axis=1))
            for m in range(5)
        ]
        + [jnp.full((3, 128), -1.0, F32)],
        0,
    )

    def split(i, _):
        value = rows_ref[pl.ds(i * 33, 32), :]
        high = value.astype(BF16)
        row = pl.multiple_of(i * 32, 32)
        limbs_ref[pl.ds(row, 32), 0:128] = high
        limbs_ref[pl.ds(row, 32), 128:256] = (value - high.astype(F32)).astype(BF16)
        return 0

    lax.fori_loop(0, 128, split, 0, unroll=8)
    one = jnp.ones((128, 128), BF16)
    zero = jnp.zeros((128, 128), BF16)
    sub16 = lax.broadcasted_iota(jnp.int32, (128, 128), 0).astype(F32).astype(BF16)

    used = lax.broadcasted_iota(jnp.int32, (32, 128), 1) < 32
    diagonal = jnp.zeros((32, 128), F32)
    for c in range(4):
        part = jnp.where(used, rows_ref[pl.ds(32 + 33 * c, 32, stride=132), :], 0.0)
        diagonal = diagonal + (pltpu.roll(part, 32 * c, axis=1) if c else part)
    diagonal_high = diagonal.astype(BF16)
    diagonal_low = (diagonal - diagonal_high.astype(F32)).astype(BF16)
    group = group_ref[...]
    owner, place = (group >> 4).astype(F32).astype(BF16), (group & 15).astype(F32).astype(BF16)
    left, right = [], []

    def rows_of(x, t):
        return jnp.broadcast_to(x[t : t + 1, :], (128, 128))

    for t in range(32):
        on = sub16 == rows_of(owner, t)
        left.append(
            jnp.concatenate(
                [
                    jnp.where(on, rows_of(diagonal_high, t), zero),
                    jnp.where(on, rows_of(diagonal_low, t), zero),
                ],
                0,
            )
        )
        right.append(jnp.where(sub16 == rows_of(place, t), one, zero))
    extra = lax.dot_general(
        jnp.concatenate(left, 1),
        jnp.concatenate(right, 1),
        (((1,), (1,)), ((), ())),
        preferred_element_type=F32,
    )
    out_ref[pl.ds(16, 128, stride=17), :] = extra[:128] + extra[128:]

    def chunk(i, _):
        locals_ = []
        for k in range(8):
            local = group_ref[...] - (i * 8 + k) * 128
            inside = (local >= 0) & (local < 128)
            locals_.append(jnp.where(inside, local, 128).astype(F32).astype(BF16))
        hot = []
        for t in range(32):
            hot.append(
                jnp.concatenate(
                    [jnp.where(sub16 == rows_of(local, t), one, zero) for local in locals_], 0
                )
            )
        total = jnp.dot(jnp.concatenate(hot, 1), limbs_ref[...], preferred_element_type=F32)
        total = total[:, :128] + total[:, 128:]
        for d in range(8 * 8):
            out_ref[pl.ds((i * 8 * 8 + d) * 17, 16), :] = total[d * 16 : d * 16 + 16]
        return 0

    lax.fori_loop(0, 16 // 8, chunk, 0)


def shrink_body(tau_ref, rows_ref, out_ref, sys_ref, stage_ref):
    per = 16
    row_id = lax.broadcasted_iota(jnp.int32, (128, 128), 0)
    lane_id = lax.broadcasted_iota(jnp.int32, (128, 128), 1)
    eye = jnp.where(row_id == lane_id, 1.0, 0.0)
    masks = packed_masks()
    half = 64 * 17
    diagonals = rows_ref[pl.ds(16, 64, stride=17), :] + rows_ref[pl.ds(half + 16, 64, stride=17), :]
    diagonals = jnp.concatenate([jnp.zeros((64, 128), F32), diagonals], 0).T
    for g in range(per):
        packed = rows_ref[pl.ds(g, 64, stride=17), :] + rows_ref[pl.ds(half + g, 64, stride=17), :]
        sys_ref[g] = unpack_symmetric(packed, diagonals[g : g + 1], masks, F32) + tau_ref[g] * eye
    lane16 = lax.broadcasted_iota(jnp.int32, (NB, 128), 1)
    sub16 = lax.broadcasted_iota(jnp.int32, (NB, 128), 0)
    same = (row_id >> 4) == (lane_id >> 4)
    segment = (lane_id >> 4).astype(F32).astype(BF16)
    first_lanes = segment < jnp.asarray(3, BF16)
    second_lanes = segment < jnp.asarray(5, BF16)

    def block(b, _):
        start = pl.multiple_of(b * NB, NB)
        panels = [sys_ref[g, pl.ds(start, NB), :] for g in range(per)]
        pivots = []
        for h in range(2):
            joined = jnp.zeros((NB, 128), F32)
            for k in range(8):
                moved = pltpu.roll(panels[h * 8 + k], lax.rem(128 + k * NB - start, 128), axis=1)
                joined = jnp.where((lane16 >> 4) == k, moved, joined)
            pivots.append(joined)
        originals = pivots
        pivots = invert_blocks(jnp.concatenate(pivots, 0))
        in_block = (lane16 >= start) & (lane16 < start + NB)
        identity = jnp.where(lane16 - start == sub16, 1.0, 0.0)
        in_lanes = (lane_id >= start) & (lane_id < start + NB)
        scaled = []
        lefts, owns, rights = [], [], []
        for h in range(2):
            pivot = pivots[h * NB : (h + 1) * NB]
            lefts.append(jnp.where(same, jnp.concatenate([pivot] * 8, 0), 0.0))
            owns.append(jnp.where(same, jnp.concatenate([originals[h]] * 8, 0), 0.0))
            rights.append(
                jnp.concatenate(
                    [jnp.where(in_block, identity, panels[h * 8 + k]) for k in range(8)], 0
                )
            )
        products = [wide_product(lefts[h], rights[h]) for h in range(2)]
        rests = [rights[h] - wide_product(owns[h], products[h]) for h in range(2)]
        products = [products[h] + wide_product(lefts[h], rests[h]) for h in range(2)]
        for product in products:
            scaled += [product[k * NB : (k + 1) * NB] for k in range(8)]
        pick = start + (lane_id & (NB - 1))
        for g in range(per):
            matrix = sys_ref[g]
            columns = jnp.take_along_axis(matrix, pick, axis=1, mode="promise_in_bounds")
            c0, c1, c2 = limbs(columns)
            w0, w1, w2 = limbs(scaled[g])
            none = jnp.zeros_like(w0)
            update = jnp.dot(
                jnp.where(first_lanes, c0, jnp.where(second_lanes, c1, c2)),
                jnp.concatenate([w2, w1, w0, w1, w0, w0, none, none], 0),
                preferred_element_type=F32,
            )
            sys_ref[g] = jnp.where(in_lanes, 0.0, matrix) - update
        for g in range(per):
            sys_ref[g, pl.ds(start, NB), :] = scaled[g]
        return 0

    lax.fori_loop(0, 128 // NB, block, 0)
    extra = []
    for g in range(per):
        packed, rest = pack_symmetric(eye - tau_ref[g] * sys_ref[g], masks)
        stage_ref[pl.ds(g, 64, stride=18), :] = packed
        extra.append(jnp.sum(rest, axis=0, keepdims=True))
    extra = jnp.concatenate(extra + [jnp.zeros((128 - per, 128), F32)], 0)
    stage_ref[pl.ds(16, 64, stride=18), :] = extra.T[64:]
    stage_ref[pl.ds(17, 64, stride=18), :] = jnp.zeros((64, 128), F32)
    result = stage_ref[...].astype(BF16)
    out_ref[0:1152, :] = result
    out_ref[1152:2304, :] = result


def limbs(value):
    first = value.astype(BF16)
    rest = value - first.astype(F32)
    second = rest.astype(BF16)
    return first, second, (rest - second.astype(F32)).astype(BF16)


def wide_product(left, right):
    a0, a1, a2 = limbs(left)
    w0, w1, w2 = limbs(right)
    main = jnp.dot(
        jnp.concatenate([a0, a1], 1),
        jnp.concatenate([jnp.concatenate([w0, w0], 0), jnp.concatenate([w1, w1], 0)], 1),
        preferred_element_type=F32,
    )
    small = jnp.dot(
        jnp.concatenate([a0, a2], 1), jnp.concatenate([w2, w0], 0), preferred_element_type=F32
    )
    return main[:, :128] + (main[:, 128:] + small)


def invert_blocks(value):
    shape = value.shape
    lane = lax.broadcasted_iota(jnp.int32, shape, 1)
    sub = lax.broadcasted_iota(jnp.int32, shape, 0) & (NB - 1)
    within = lane & (NB - 1)
    segment = lane - within

    def spread(x, row):
        parts = [jnp.broadcast_to(x[h * NB + row : h * NB + row + 1], (NB, 128)) for h in range(2)]
        return jnp.concatenate(parts, 0)

    for j in range(0, NB, 2):
        c0 = jnp.take_along_axis(value, segment + j, axis=1, mode="promise_in_bounds")
        c1 = jnp.take_along_axis(value, segment + (j + 1), axis=1, mode="promise_in_bounds")
        at0, at1 = within == j, within == j + 1
        r0, r1 = spread(value, j), spread(value, j + 1)
        inverse = 1.0 / spread(c0, j)
        ratio = spread(c1, j) * inverse
        below = spread(c0, j + 1)
        s0 = jnp.where(at0, inverse, r0 * inverse)
        pivot = 1.0 / (spread(c1, j + 1) - below * ratio)
        rest = jnp.where(at0, 0.0, r1) - below * s0
        s1 = jnp.where(at1, pivot, rest * pivot)
        s0 = jnp.where(at1, 0.0, s0) - ratio * s1
        kept = jnp.where(at0 | at1, 0.0, value)
        c1 = c1 - c0 * ratio
        first = jnp.where(at0, inverse, jnp.where(at1, 0.0, r0 * inverse))
        value = jnp.where(
            sub == j, s0, jnp.where(sub == j + 1, s1, (kept - c0 * first) - c1 * s1)
        )
    return value


def expand_body(group_ref, rows_ref, out_ref, turned_ref, wide_ref, table_ref, stage_ref):
    turned_ref[...] = group_ref[...].astype(F32).T.astype(jnp.int32)
    wide_ref[...] = rows_ref[...].astype(F32)
    for j in range(4):

        def gather(d, _):
            value = wide_ref[pl.ds((d + 32 * j) * 18, 16), :].astype(BF16)
            table_ref[pl.ds(pl.multiple_of(d * 16, 16), 16), j * 128 : (j + 1) * 128] = value
            return 0

        lax.fori_loop(0, 32, gather, 0, unroll=8)
    extras = wide_ref[pl.ds(16, 128, stride=18), :].astype(BF16)
    lane = lax.broadcasted_iota(jnp.int32, (128, 128), 1)
    lane16 = lane.astype(F32).astype(BF16)
    zero = jnp.zeros((128, 128), BF16)
    one = jnp.ones((128, 128), BF16)
    eye = lax.broadcasted_iota(jnp.int32, (32, 128), 0) == lax.broadcasted_iota(
        jnp.int32, (32, 128), 1
    )
    stage_ref[pl.ds(33, 128, stride=34), :] = jnp.zeros((128, 128), F32)
    for u in range(4):
        groups, hot, owners = [], [], []
        for v in range(8):
            group = jnp.broadcast_to(turned_ref[:, u * 8 + v : u * 8 + v + 1], (128, 128))
            groups.append(group)
            low = jnp.where((group & 127).astype(F32).astype(BF16) == lane16, one, zero)
            high = ((group >> 7) & 3).astype(F32).astype(BF16)
            hot.append(
                jnp.concatenate(
                    [jnp.where(high == jnp.full((128, 128), c, BF16), low, zero) for c in range(4)],
                    1,
                )
            )
            owners.append(jnp.where((group >> 4).astype(F32).astype(BF16) == lane16, one, zero))
        wide = jnp.dot(jnp.concatenate(hot, 0), table_ref[...], preferred_element_type=F32)
        spots = jnp.dot(jnp.concatenate(owners, 0), extras, preferred_element_type=F32)
        for v in range(8):
            group = groups[v]
            rows = slice(v * 128, (v + 1) * 128)
            quarter = group >> 9
            piece = wide[rows, 384:512]
            for j in (2, 1, 0):
                piece = jnp.where(quarter == j, wide[rows, j * 128 : (j + 1) * 128], piece)
            spot = jnp.where(lane == (group & 15), spots[rows], 0.0)
            value = jnp.sum(spot, axis=1, keepdims=True)
            for k in range(4):
                row = ((u * 8 + v) * 4 + k) * 34
                part = slice(k * 32, k * 32 + 32)
                stage_ref[row : row + 32, :] = piece[part]
                stage_ref[row + 32 : row + 33, :] = jnp.sum(
                    jnp.where(eye, value[part], 0.0), axis=0, keepdims=True
                )
    out_ref[...] = stage_ref[...].astype(BF16)


def add_halves(first_ref, cells_ref, factor_ref, sum_ref, even_ref, odd_ref):
    odd_ref[...] = jnp.zeros_like(odd_ref)
    count = 4

    def multiply(p, ref):
        for k in range(count):
            values = load_half(cells_ref, first_ref[p + k])
            ref[k * 256 : (k + 1) * 256, :] = jnp.dot(
                values, factor_ref[p + k], preferred_element_type=F32
            )

    def accumulate(p, ref):
        for k in range(count):
            first = first_ref[p + k]
            spots, sums = [], []
            for a in range(PATCH // 2):
                for b in range(PATCH):
                    at = pl.ds(first + (a * 16 + b) * 32, PATCH)
                    row = k * 256 + (a * PATCH + b) * PATCH
                    spots.append(at)
                    sums.append(sum_ref[at, :] + ref[row : row + PATCH, :])
            for at, value in zip(spots, sums):
                sum_ref[at, :] = value

    def several(i, _):
        p = i * (2 * count)
        multiply(p, even_ref)
        accumulate(jnp.maximum(p - count, 0), odd_ref)
        multiply(p + count, odd_ref)
        accumulate(p, even_ref)
        return 0

    lax.fori_loop(0, 64 // (2 * count), several, 0)
    accumulate(64 - count, odd_ref)


def edge_apply_body(
    first_ref,
    cells_ref,
    rows_ref,
    inner_ref,
    low_ref,
    high_ref,
    factor_ref,
    wide_ref,
    sum_ref,
    even_ref,
    odd_ref,
    diag_ref,
):
    wide_ref[...] = rows_ref[...].astype(F32)
    masks = packed_masks()
    used = lax.broadcasted_iota(jnp.int32, (64, 128), 1) < 32
    first_side = jnp.where(used, wide_ref[pl.ds(32, 64, stride=34), :], 0.0)
    last_side = jnp.where(used, wide_ref[pl.ds(64 * 34 + 32, 64, stride=34), :], 0.0)
    diagonals = first_side + pltpu.roll(last_side, 32, axis=1)
    diag_ref[...] = jnp.concatenate([jnp.zeros((64, 128), F32), diagonals], 0).T

    def unpack(p, _):
        side = p // 32
        packed = wide_ref[pl.ds(side * (64 * 34 - 32) + p, 64, stride=34), :]
        sum_ref[pl.ds(pl.multiple_of(p * 128, 128), 128), :] = jnp.zeros((128, 128), F32)
        factor_ref[p] = unpack_symmetric(packed, diag_ref[pl.ds(p, 1), :], masks, BF16)
        return 0

    lax.fori_loop(0, 64, unpack, 0, unroll=8)
    add_halves(first_ref, cells_ref, factor_ref, sum_ref, even_ref, odd_ref)
    low_ref[...] = sum_ref[0:2048, :].astype(BF16)
    inner_ref[...] = sum_ref[2048:6144, :]
    high_ref[...] = sum_ref[6144:8192, :].astype(BF16)


def inner_apply_body(
    first_ref, cells_ref, factor_ref, start_ref, sum_ref, even_ref, odd_ref
):
    sum_ref[...] = start_ref[...]
    add_halves(first_ref, cells_ref, factor_ref, sum_ref, even_ref, odd_ref)


def exchange(rows, sublanes):
    shape = rows.shape
    rows = rows.reshape(128, shape[0] // (128 * sublanes), sublanes, 128)
    rows = lax.all_to_all(rows, BOTH, split_axis=0, concat_axis=0, tiled=True)
    return rows.reshape(shape)


def shards(estimate, dual, corners, members, thresholds):
    margin = PATCH // 2
    index_x = lax.axis_index("gx")
    index_y = lax.axis_index("gy")
    myself = index_x * 16 + index_y
    mixture = (estimate.astype(F32) + dual.astype(F32)).astype(BF16)

    begin_x = corners[0] - (index_x * 8 - margin)
    begin_y = corners[1] - (index_y * 8 - margin)
    first = (begin_x * 16 + begin_y) * 32 + corners[2]
    low_half = begin_x <= margin
    first_edge = first + jnp.where(low_half, 0, 2048)
    first_inner = first + jnp.where(low_half, 0, -2048)
    code = ((corners[0] * 128 + corners[1]) * 32 + corners[2]).astype(F32)
    code = jnp.concatenate([jnp.zeros((64,), F32), code]).reshape(1, 128)

    side = (myself // 64).reshape(1)
    table = call(
        group_table_body,
        jax.ShapeDtypeStruct((32, 128), jnp.int32),
        side,
        members.T,
        specs=[SMEM, VMEM],
        flops=2 * 128 * 32768 * 64,
        nbytes=1 << 17,
    )
    base = jnp.stack([index_x * 8, index_y * 8])
    offset = jnp.arange(9, dtype=jnp.int32)
    near_x = index_x + offset // 3 - 1
    near_y = index_y + offset % 3 - 1
    exists = (near_x >= 0) & (near_x < 8) & (near_y >= 0) & (near_y < 16)
    near_id = jnp.where(exists, near_x * 16 + near_y, -1)
    tau = lax.dynamic_slice_in_dim(thresholds, myself * 16, 16)
    held, code, table, near_id, tau, base = lax.optimization_barrier(
        (mixture, code, table, near_id, tau, base)
    )
    yb, ya = neighbors(mixture, "gy", mixture[:, :margin], mixture[:, 8 - margin :])
    inner_cells, half_grams = call(
        inner_gram_body,
        (jax.ShapeDtypeStruct((4096, 128), F32), jax.ShapeDtypeStruct((64, 128, 128), F32)),
        first_inner,
        mixture,
        yb,
        ya,
        specs=[SMEM] + [VMEM] * 3,
        flops=2 * 64 * 256 * 128 * 128,
        nbytes=8 << 20,
    )
    wide = jnp.concatenate(
        [
            jnp.concatenate([yb[:margin], held[:margin], ya[:margin]], 1),
            jnp.concatenate([yb[margin:], held[margin:], ya[margin:]], 1),
        ],
        0,
    )
    xb, xa = neighbors(wide, "gx", wide[:margin], wide[8 - margin :])
    cells, grams = call(
        gram_body,
        (jax.ShapeDtypeStruct((8192, 128), F32), jax.ShapeDtypeStruct((128 * 33, 128), F32)),
        first_edge,
        code,
        inner_cells,
        xb,
        xa,
        half_grams,
        specs=[SMEM] + [VMEM] * 5,
        scratch=[pltpu.VMEM((128, 128), F32)],
        flops=2 * 64 * 256 * 128 * 128,
        nbytes=10 << 20,
    )
    rows = exchange(grams, 1)
    sums, near = call(
        group_sum_body,
        (jax.ShapeDtypeStruct((128 * 17, 128), F32), jax.ShapeDtypeStruct((8, 128), F32)),
        near_id,
        table,
        rows,
        specs=[SMEM, VMEM, VMEM],
        scratch=[pltpu.VMEM((4096, 256), BF16)],
        flops=2 * 2048 * 4096 * 256,
        nbytes=5 << 20,
    )
    inverse_counts = call(
        counts_body,
        jax.ShapeDtypeStruct((2048, 128), F32),
        near,
        base,
        specs=[VMEM, SMEM],
        flops=2 * 2048 * 640 * 128,
        nbytes=1 << 20,
    )
    mine = exchange(sums, 1)
    factors = call(
        shrink_body,
        jax.ShapeDtypeStruct((128 * 18, 128), BF16),
        tau,
        mine,
        specs=[SMEM, VMEM],
        scratch=[pltpu.VMEM((16, 128, 128), F32), pltpu.VMEM((64 * 18, 128), F32)],
        flops=2 * 16 * 8 * 6 * 128**3,
        nbytes=2 << 20,
    )
    factor_rows = exchange(factors, 2)
    patch_rows = call(
        expand_body,
        jax.ShapeDtypeStruct((128 * 34, 128), BF16),
        table,
        factor_rows,
        scratch=[
            pltpu.VMEM((128, 32), jnp.int32),
            pltpu.VMEM((128 * 18, 128), F32),
            pltpu.VMEM((512, 512), BF16),
            pltpu.VMEM((128 * 34, 128), F32),
        ],
        flops=2 * 2048 * 4096 * 256,
        nbytes=3 << 20,
    )
    patch_factors = exchange(patch_rows, 2)
    edge = jax.ShapeDtypeStruct((2048, 128), BF16)
    half_result = pltpu.VMEM((1024, 128), F32)
    partial, low, high, patch_factors = call(
        edge_apply_body,
        (
            jax.ShapeDtypeStruct((4096, 128), F32),
            edge,
            edge,
            jax.ShapeDtypeStruct((64, 128, 128), BF16),
        ),
        first_edge,
        cells,
        patch_factors,
        specs=[SMEM, VMEM, VMEM],
        scratch=[
            pltpu.VMEM((128 * 34, 128), F32),
            pltpu.VMEM((8192, 128), F32),
            half_result,
            half_result,
            pltpu.VMEM((128, 128), F32),
        ],
        flops=2 * 64 * 256 * 128 * 128,
        nbytes=10 << 20,
    )
    from_low, from_high = neighbors(
        partial, "gx", low.reshape(4, 16, 32, 128), high.reshape(4, 16, 32, 128)
    )
    inner = call(
        inner_apply_body,
        jax.ShapeDtypeStruct((4096, 128), F32),
        first_inner,
        inner_cells,
        patch_factors,
        partial,
        specs=[SMEM, VMEM, VMEM, VMEM],
        scratch=[half_result, half_result],
        flops=2 * 64 * 256 * 128 * 128,
        nbytes=8 << 20,
    )
    inner = inner.reshape(8, 16, 32, 128)
    inner = jnp.concatenate(
        [inner[:margin] + from_low.astype(F32), inner[margin:] + from_high.astype(F32)], 0
    )
    from_low, from_high = neighbors(
        inner, "gy", inner[:, :margin].astype(BF16), inner[:, 16 - margin :].astype(BF16)
    )
    sums = inner[:, margin : 16 - margin]
    sums = jnp.concatenate(
        [sums[:, :margin] + from_low.astype(F32), sums[:, margin:] + from_high.astype(F32)], 1
    )
    lowrank = (sums + DATA_WEIGHT * mixture.astype(F32)) * inverse_counts.reshape(8, 8, 32, 128)
    dual_next = dual.astype(F32) + estimate.astype(F32) - lowrank
    return lowrank, dual_next


def solution(mesh):
    in_specs = (
        P("gx", "gy", None, None),
        P("gx", "gy", None, None),
        P(None, ("gx", "gy")),
        P(),
        P(),
    )
    out_specs = (P("gx", "gy", None, None), P("gx", "gy", None, None))
    return jax.shard_map(shards, mesh=mesh, in_specs=in_specs, out_specs=out_specs, check_vma=False)
```
